32 devices in a mesh: row: 8 (over y, x, core), col: 4 (over z).
Axes of the slice: x: 2, y: 2, z: 4, core: 2. Of those that a mesh axis runs over, the one named last changes fastest.
Arguments:
- raw_rows: bfloat16 [32768, 64], P(('row', 'col')), may hold values from -6 to 6
- raw_wide: int32 [32768], P(('row', 'col')), may hold values from 0 to 1
- raw_dest: int32 [32768], P(('row', 'col')), may hold values from 0 to 31, as said below
- raw_slot: int32 [32768], P(('row', 'col')), may hold values from 0 to 511
- proj_narrow: bfloat16 [32, 128], replicated, may hold values from -1 to 1
- proj_wide: bfloat16 [64, 128], replicated, may hold values from -0.75 to 0.75
- adj_values: bfloat16 [8192, 8192], P('row', 'col'), may hold values from -1 to 1
- tile_mask: int32 [64, 64], P('row', 'col'), may hold values 0 or 1
- tile_scale: float32 [64, 64], P('row', 'col'), may hold values from 0.008286407 to 0.082864076
- weight_sum: bfloat16 [2, 128, 128], replicated, may hold values from -0.5 to 0.5
- weight_product: bfloat16 [2, 128, 128], replicated, may hold values from -0.5 to 0.5
Outputs:
- user_out: bfloat16 [8192, 128], P(('row', 'col'))
- item_out: bfloat16 [4, 2048, 128], P('col', 'row')
The draws below stay inside these ranges and needn't reach their ends.
Inputs may be any that keep to these rules, and one draw needn't show every extreme that they name: `raw_dest`: among the feature rows stored on one device at most 96 have any one destination; one device, drawn from the seed, is the destination of exactly 96 rows of every device.
All inputs are finite; a program needn't handle non-finite values. No bound on the sum of `tile_mask` on one device may be relied on, other than what follows from the above.
Results may differ from the reference program's by a relative error of at most 0.025.
Values may be sent and summed in bfloat16 or wider, within the bound.
No kernel may reach another device: no remote copies, remote signals or barrier semaphores. Data moves between devices by JAX's collectives and lax.ppermute only.
A program may use at most 128 MiB of HBM per device.

```python
import math
import jax
import jax.numpy as jnp
from jax import lax

D = 128
RAW_COLS = 64
NARROW = 32
TILE = 128
LAYERS = 2
UPD = 256
IPD = 256
RAW_DEV = 1024
CAP = 96
NU = 8192
NI = 8192
N_ROW = 8
N_COL = 4
DEVICES = 32


def draw_raw_dest(key, part):
    busiest = jax.random.randint(jax.random.fold_in(key, 11), (), 0, DEVICES)
    source_keys = jax.random.split(jax.random.fold_in(key, 12), DEVICES)

    def one_source(source_key):
        key_one, key_two = jax.random.split(source_key)
        shuffled = jax.random.permutation(key_one, (DEVICES - 1) * CAP)[:RAW_DEV - CAP]
        others = (shuffled // CAP).astype(jnp.int32)
        others = others + (others >= busiest).astype(jnp.int32)
        chosen = jnp.concatenate([jnp.full((CAP,), busiest, jnp.int32), others])
        return jax.random.permutation(key_two, chosen)
    return jax.vmap(one_source)(source_keys).reshape(DEVICES * RAW_DEV).astype(jnp.int32)


def touch_ends(entries, rng, least, high):
    place = [jax.random.randint(jax.random.fold_in(rng, axis), (), 0, length) for axis, length in enumerate(entries.shape)]
    main_axis = entries.shape.index(max(entries.shape))
    beside = place[:main_axis] + [(place[main_axis] + 1) % entries.shape[main_axis]] + place[main_axis + 1:]
    return entries.at[tuple(place)].set(least).at[tuple(beside)].set(high)


def block_scale(stream_key, dims, shards, smallest, high):
    loudness, own = 1.0, jax.random.fold_in(stream_key, 6)
    for dim, shards_of in shards:
        heights = jnp.exp(jax.random.uniform(jax.random.fold_in(own, dim), (shards_of,), jnp.float32, smallest / len(shards), high / len(shards)))
        loudness = loudness * jnp.repeat(heights, dims[dim] // shards_of).reshape([-1 if axis == dim else 1 for axis in range(len(dims))])
    return loudness


def normal_values(own_key, shape, scale, bound, cuts=(), dtype=jnp.bfloat16):
    drawn = jax.random.normal(own_key, shape, jnp.float32) * scale
    if len(cuts) > 0:
        drawn = block_scale(own_key, shape, cuts, -0.22, 0.18) * drawn
    return jnp.clip(drawn, min=-bound, max=bound).astype(dtype)


def setup_inputs(seed: int = 0) -> dict:
    streams_of = jax.random.split(jax.random.key(seed), 12)
    raw_rows = normal_values(streams_of[0], (DEVICES * RAW_DEV, RAW_COLS), 1.0, 6.0, ((0, 32),))
    raw_wide = touch_ends(jax.random.randint(streams_of[1], (DEVICES * RAW_DEV,), 0, 2), jax.random.fold_in(streams_of[1], 1), 0, 1).astype(jnp.int32)
    raw_dest = draw_raw_dest(jax.random.fold_in(streams_of[11], 71), 0)
    raw_slot = touch_ends(jax.random.randint(streams_of[3], (DEVICES * RAW_DEV,), 0, UPD + IPD), jax.random.fold_in(streams_of[3], 1), 0, (UPD + IPD) - 1).astype(jnp.int32)
    proj_narrow = normal_values(streams_of[4], (NARROW, D), NARROW ** -0.5, 1.0)
    proj_wide = normal_values(streams_of[5], (RAW_COLS, D), RAW_COLS ** -0.5, 0.75)
    adj_values = jnp.clip(jax.random.uniform(streams_of[6], (NU, NI), jnp.float32, -1.0, 1.0) * block_scale(streams_of[6], (NU, NI), ((0, 8), (1, 4)), -0.4, 0.0), -1.0, 1.0).astype(jnp.bfloat16)
    tile_mask = touch_ends((jax.random.randint(streams_of[7], (NU // TILE, NI // TILE), 0, 2) < 1).astype(jnp.int32), jax.random.fold_in(streams_of[7], 1), 0, 1)
    tile_scale = jnp.clip(jnp.exp(math.log(0.082864076) - 2.3025851 * jax.random.uniform(streams_of[8], (NU // TILE, NI // TILE), jnp.float32) ** block_scale(streams_of[8], (NU // TILE, NI // TILE), ((0, 8), (1, 4)), -0.2, 0.2)), 0.008286407, 0.082864076)
    weight_sum = normal_values(streams_of[9], (LAYERS, D, D), D ** -0.5, 0.5)
    weight_product = normal_values(streams_of[10], (LAYERS, D, D), D ** -0.5, 0.5)
    return dict(raw_rows=raw_rows, raw_wide=raw_wide, raw_dest=raw_dest, raw_slot=raw_slot, proj_narrow=proj_narrow, proj_wide=proj_wide, adj_values=adj_values, tile_mask=tile_mask, tile_scale=tile_scale, weight_sum=weight_sum, weight_product=weight_product)


def dequantize(values_bf, mask_tiles, scale_tiles):
    row_count = values_bf.shape[0]
    columns = values_bf.shape[1]
    values = values_bf.astype(jnp.float32)
    factor = mask_tiles.astype(jnp.float32) * scale_tiles
    tiled = values.reshape(row_count // TILE, TILE, columns // TILE, TILE) * factor[:, None, :, None]
    return tiled.reshape(row_count, columns).astype(jnp.bfloat16)


def update(side_sum, own_rows, weight_sum, weight_product):
    own_float = own_rows.astype(jnp.float32)
    summed = (side_sum + own_float).astype(jnp.bfloat16)
    product = (side_sum * own_float).astype(jnp.bfloat16)
    linear = jnp.dot(summed, weight_sum, preferred_element_type=jnp.float32)
    linear = linear + jnp.dot(product, weight_product, preferred_element_type=jnp.float32)
    return jnp.where(linear > 0, linear, 0.2 * linear).astype(jnp.bfloat16)


def reference(raw_rows, raw_wide, raw_dest, raw_slot, proj_narrow, proj_wide, adj_values, tile_mask, tile_scale, weight_sum, weight_product):
    wide_part = jnp.dot(raw_rows, proj_wide, preferred_element_type=jnp.float32)
    narrow_part = jnp.dot(raw_rows[:, :NARROW], proj_narrow, preferred_element_type=jnp.float32)
    projected = jnp.where((raw_wide == 1)[:, None], wide_part, narrow_part)
    is_user = raw_slot < UPD
    user_index = raw_dest * UPD + raw_slot
    grid_row = raw_dest // N_COL
    grid_col = raw_dest % N_COL
    item_index = grid_col * (IPD * N_ROW) + grid_row * IPD + (raw_slot - UPD)
    target = jnp.where(is_user, user_index, NU + item_index).astype(jnp.int32)
    totals = jax.ops.segment_sum(projected, target, num_segments=NU + NI)
    user_rows = totals[:NU].astype(jnp.bfloat16)
    item_rows = totals[NU:].astype(jnp.bfloat16)
    block_rows = math.gcd(NU, 2048)
    block_count = NU // block_rows
    value_blocks = adj_values.reshape(block_count, block_rows, NI)
    mask_blocks = tile_mask.reshape(block_count, block_rows // TILE, NI // TILE)
    scale_blocks = tile_scale.reshape(block_count, block_rows // TILE, NI // TILE)
    for layer_index in range(LAYERS):
        current_items = item_rows

        def visit_block(item_total, inputs):
            value_block, mask_block, scale_block, user_block = inputs
            adjacency = dequantize(value_block, mask_block, scale_block)
            user_part = jnp.dot(adjacency, current_items, preferred_element_type=jnp.float32)
            item_total = item_total + lax.dot_general(adjacency, user_block, (((0,), (0,)), ((), ())), preferred_element_type=jnp.float32)
            return item_total, user_part

        item_side, user_side = lax.scan(visit_block, jnp.zeros((NI, D), jnp.float32), (value_blocks, mask_blocks, scale_blocks, user_rows.reshape(block_count, block_rows, D)))
        new_users = update(user_side.reshape(NU, D), user_rows, weight_sum[layer_index], weight_product[layer_index])
        new_items = update(item_side, item_rows, weight_sum[layer_index], weight_product[layer_index])
        user_rows = new_users
        item_rows = new_items
    return user_rows, item_rows.reshape(N_COL, IPD * N_ROW, D)
```

```python
import functools

import jax
import jax.numpy as jnp
from jax import lax
from jax.experimental import pallas as pl
from jax.experimental.pallas import tpu as pltpu
from jax.sharding import PartitionSpec as P

TILE = 128
LANES = 128
CODE_ROWS = 8
F32 = jnp.float32
BF16 = jnp.bfloat16
NT = (((1,), (1,)), ((), ()))


def power_of_two(n):
    return n & (n - 1) == 0


def peer_to(i, k, n):
    return i ^ k if power_of_two(n) else (i + k) % n


def peer_from(i, k, n):
    return i ^ k if power_of_two(n) else (i + n - k) % n


def vmem_spec():
    return pl.BlockSpec(memory_space=pltpu.VMEM)


def params(mib=24):
    return pltpu.CompilerParams(vmem_limit_bytes=mib * 2**20)


def dispatch_kernel(devices, slots, raw_ref, dest_ref, slot_ref, wide_ref, out_ref):
    features, rows = raw_ref.shape
    chunks = rows // LANES
    dest = dest_ref[...]
    hot = (lax.broadcasted_iota(jnp.int32, (devices, rows), 0) == dest).astype(F32)
    hot_bf = hot.astype(BF16)
    before = lax.broadcasted_iota(jnp.int32, (LANES, 2 * LANES), 0)
    column = lax.broadcasted_iota(jnp.int32, (LANES, 2 * LANES), 1)
    prefix = ((before < column) | (column >= LANES)).astype(F32).astype(BF16)
    base = jnp.zeros((devices, LANES), F32)
    ranks = []
    for chunk in range(chunks):
        lanes = slice(chunk * LANES, (chunk + 1) * LANES)
        counted = jnp.dot(hot_bf[:, lanes], prefix, preferred_element_type=F32)
        ranks.append(
            jnp.sum((counted[:, :LANES] + base) * hot[:, lanes], axis=0, keepdims=True)
        )
        base = base + counted[:, LANES:]
    rank = jnp.concatenate(ranks, axis=1)
    place = (
        lax.broadcasted_iota(jnp.int32, (slots, rows), 0).astype(F32) == rank
    ).astype(F32).astype(BF16)
    slot = slot_ref[...]
    code = lax.broadcasted_iota(jnp.int32, (2 * CODE_ROWS, rows), 0)
    codes = jnp.where(
        code == 0,
        slot // 256,
        jnp.where(code == 1, slot % 256, jnp.where(code == 2, wide_ref[...], 0)),
    )
    ext = jnp.concatenate([raw_ref[...], codes.astype(F32).astype(BF16)], axis=0)
    group = 8
    for first in range(0, devices, group):
        masked = jnp.concatenate(
            [ext * hot_bf[d : d + 1, :] for d in range(first, first + group)], axis=0
        )
        placed = lax.dot_general(masked, place, NT, preferred_element_type=F32).astype(BF16)
        for d in range(group):
            start = d * (features + 2 * CODE_ROWS)
            out_ref[first + d] = placed[start : start + features + CODE_ROWS]


def dispatch(raw, dest, slot, wide, devices, slots):
    features, rows = raw.shape
    return pl.pallas_call(
        functools.partial(dispatch_kernel, devices, slots),
        out_shape=jax.ShapeDtypeStruct((devices, features + CODE_ROWS, slots), BF16),
        in_specs=[vmem_spec()] * 4,
        out_specs=vmem_spec(),
        compiler_params=params(),
        name="dispatch",
    )(raw, dest, slot, wide)


def segment_kernel(narrow, upd, recv_ref, proj_narrow_ref, proj_wide_ref, *out_refs):
    user_ref, user_t_ref, item_ref, items_ref = out_refs
    devices, height, slots = recv_ref.shape
    features = height - CODE_ROWS
    nodes = user_ref.shape[0] + item_ref.shape[0]
    group = 8
    total = jnp.zeros((nodes, features + narrow), F32)
    for first in range(0, devices, group):
        block = jnp.concatenate([recv_ref[first + p] for p in range(group)], axis=1)
        codes = block[features:].astype(F32)
        node = (codes[0:1] * 256 + codes[1:2]).astype(jnp.int32)
        wide = codes[2:3].astype(BF16)
        rows = block[:features]
        values = jnp.concatenate([rows * wide, rows[:narrow] * (1 - wide)], axis=0)
        hot = (
            lax.broadcasted_iota(jnp.int32, (nodes, group * slots), 0) == node
        ).astype(F32).astype(BF16)
        total = total + lax.dot_general(hot, values, NT, preferred_element_type=F32)
    weights = jnp.concatenate([proj_wide_ref[...], proj_narrow_ref[...]], axis=0)
    initial = jnp.zeros((nodes, weights.shape[1]), F32)
    rest = total
    for _ in range(3):
        part = rest.astype(BF16)
        initial = initial + jnp.dot(part, weights, preferred_element_type=F32)
        rest = rest - part.astype(F32)
    users = initial[:upd]
    items = initial[upd:].astype(BF16)
    user_ref[...] = users.astype(BF16)
    user_t_ref[...] = users.T.astype(BF16)
    item_ref[...] = items
    for r in range(items_ref.shape[0]):
        items_ref[r] = items


def segment(recv, proj_narrow, proj_wide, upd, ipd, rows):
    d = proj_wide.shape[1]
    return pl.pallas_call(
        functools.partial(segment_kernel, proj_narrow.shape[0], upd),
        out_shape=(
            jax.ShapeDtypeStruct((upd, d), BF16),
            jax.ShapeDtypeStruct((d, upd), BF16),
            jax.ShapeDtypeStruct((ipd, d), BF16),
            jax.ShapeDtypeStruct((rows, ipd, d), BF16),
        ),
        in_specs=[vmem_spec()] * 3,
        out_specs=(vmem_spec(),) * 4,
        compiler_params=params(),
        name="segment",
    )(recv, proj_narrow, proj_wide)


def dequantize_kernel(mask_ref, scale_ref, values_ref, out_ref):
    i = pl.program_id(0)
    for j in range(values_ref.shape[1] // TILE):
        lanes = slice(j * TILE, (j + 1) * TILE)
        factor = mask_ref[i, j].astype(F32) * scale_ref[i, j]
        out_ref[:, lanes] = (values_ref[:, lanes].astype(F32) * factor).astype(BF16)


def dequantize(values, mask, scale):
    m, n = values.shape
    smem = pl.BlockSpec(memory_space=pltpu.SMEM)
    spec = pl.BlockSpec((TILE, n), lambda i: (i, 0))
    return pl.pallas_call(
        dequantize_kernel,
        out_shape=jax.ShapeDtypeStruct((m, n), BF16),
        grid=(m // TILE,),
        in_specs=[smem, smem, spec],
        out_specs=spec,
        compiler_params=params(),
        cost_estimate=pl.CostEstimate(flops=m * n, bytes_accessed=4 * m * n, transcendentals=0),
        name="dequantize",
    )(mask, scale, values)


def user_sum_kernel(place_ref, adj_ref, items_ref, *out_refs):
    k = pl.program_id(0)
    part = jnp.dot(adj_ref[...], items_ref[...], preferred_element_type=F32).astype(BF16)
    for which, out_ref in enumerate(out_refs):

        @pl.when(k == which)
        def _():
            out_ref[...] = part


def user_sums(place, adjacency, items, cols):
    m, n = adjacency.shape
    d = items.shape[1]
    upd = m // cols
    return pl.pallas_call(
        user_sum_kernel,
        out_shape=(jax.ShapeDtypeStruct((upd, d), BF16),) * cols,
        grid_spec=pltpu.PrefetchScalarGridSpec(
            num_scalar_prefetch=1,
            grid=(cols,),
            in_specs=[
                pl.BlockSpec((upd, n), lambda k, place: (peer_to(place[1], k, cols), 0)),
                pl.BlockSpec((n, d), lambda k, place: (0, 0)),
            ],
            out_specs=(pl.BlockSpec((upd, d), lambda k, place: (0, 0)),) * cols,
        ),
        compiler_params=params(),
        cost_estimate=pl.CostEstimate(
            flops=2 * m * n * d, bytes_accessed=2 * m * n, transcendentals=0
        ),
        name="user_sums",
    )(place, adjacency, items)


def item_sum_kernel(cols, place_ref, adj_ref, *refs):
    users_refs, out_ref = refs[:-1], refs[-1]
    upd = users_refs[0].shape[1]
    total = None
    for k, users_ref in enumerate(users_refs):
        start = pl.multiple_of(peer_from(place_ref[1], k, cols) * upd, upd)
        part = jnp.dot(
            users_ref[...], adj_ref[pl.ds(start, upd), :], preferred_element_type=F32
        )
        total = part if total is None else total + part
    out_ref[0] = total.astype(BF16)


def item_sums(place, adjacency, users_t, rows):
    m, n = adjacency.shape
    cols = len(users_t)
    d, upd = users_t[0].shape
    ipd = n // rows
    return pl.pallas_call(
        functools.partial(item_sum_kernel, cols),
        out_shape=jax.ShapeDtypeStruct((rows, d, ipd), BF16),
        grid_spec=pltpu.PrefetchScalarGridSpec(
            num_scalar_prefetch=1,
            grid=(rows,),
            in_specs=[pl.BlockSpec((m, ipd), lambda r, place: (0, r))]
            + [pl.BlockSpec((d, upd), lambda r, place: (0, 0))] * cols,
            out_specs=pl.BlockSpec((1, d, ipd), lambda r, place: (r, 0, 0)),
        ),
        compiler_params=params(),
        cost_estimate=pl.CostEstimate(
            flops=2 * m * n * d, bytes_accessed=2 * m * n, transcendentals=0
        ),
        name="item_sums",
    )(place, adjacency, *users_t)


def updated(side, own, weight_sum, weight_product):
    own = own.astype(F32)
    linear = jnp.dot((side + own).astype(BF16), weight_sum, preferred_element_type=F32)
    linear = linear + jnp.dot(
        (side * own).astype(BF16), weight_product, preferred_element_type=F32
    )
    return jnp.where(linear > 0, linear, 0.2 * linear)


def user_update_kernel(own_ref, sum_ref, product_ref, *refs):
    parts, outs = refs[:-2], refs[-2:]
    side = parts[0][...].astype(F32)
    for part in parts[1:]:
        side = side + part[...].astype(F32)
    new = updated(side, own_ref[...], sum_ref[...], product_ref[...])
    outs[0][...] = new.astype(BF16)
    outs[1][...] = new.T.astype(BF16)


def user_update(parts, own, weight_sum, weight_product):
    upd, d = own.shape
    return pl.pallas_call(
        user_update_kernel,
        out_shape=(jax.ShapeDtypeStruct((upd, d), BF16), jax.ShapeDtypeStruct((d, upd), BF16)),
        in_specs=[vmem_spec()] * (3 + len(parts)),
        out_specs=(vmem_spec(),) * 2,
        compiler_params=params(),
        name="user_update",
    )(own, weight_sum, weight_product, *parts)


def item_update_kernel(own_ref, sum_ref, product_ref, parts_ref, new_ref, *wide_refs):
    side = parts_ref[0].astype(F32)
    for r in range(1, parts_ref.shape[0]):
        side = side + parts_ref[r].astype(F32)
    new = updated(side.T, own_ref[...], sum_ref[...], product_ref[...]).astype(BF16)
    new_ref[...] = new
    for wide_ref in wide_refs:
        for r in range(wide_ref.shape[0]):
            wide_ref[r] = new


def item_update(parts, own, weight_sum, weight_product, last):
    ipd, d = own.shape
    rows = parts.shape[0]
    outs = [jax.ShapeDtypeStruct((ipd, d), BF16)]
    if not last:
        outs.append(jax.ShapeDtypeStruct((rows, ipd, d), BF16))
    return pl.pallas_call(
        item_update_kernel,
        out_shape=outs,
        in_specs=[vmem_spec()] * 4,
        out_specs=[vmem_spec()] * len(outs),
        compiler_params=params(),
        name="item_update",
    )(own, weight_sum, weight_product, parts)


def exchange(blocks, axis, n):
    received = [blocks[0]]
    for k in range(1, n):
        pairs = [(i, peer_to(i, k, n)) for i in range(n)]
        received.append(lax.ppermute(blocks[k], axis, pairs))
    return received


def per_device(
    raw_rows,
    raw_wide,
    raw_dest,
    raw_slot,
    proj_narrow,
    proj_wide,
    adj_values,
    tile_mask,
    tile_scale,
    weight_sum,
    weight_product,
):
    rows = lax.axis_size("row")
    cols = lax.axis_size("col")
    devices = rows * cols
    count = raw_rows.shape[0]
    capacity = 3 * count // devices
    slots = -(-capacity // LANES) * LANES
    upd = adj_values.shape[0] // cols
    ipd = adj_values.shape[1] // rows
    layers = weight_sum.shape[0]
    place = jnp.stack([lax.axis_index("row"), lax.axis_index("col")]).astype(jnp.int32)

    send = dispatch(
        raw_rows.T,
        raw_dest.reshape(1, count),
        raw_slot.reshape(1, count),
        raw_wide.reshape(1, count),
        devices,
        slots,
    )
    recv = lax.all_to_all(send, ("row", "col"), split_axis=0, concat_axis=0, tiled=True)
    adjacency = dequantize(adj_values, tile_mask, tile_scale)
    users, users_t, items, items_wide = segment(recv, proj_narrow, proj_wide, upd, ipd, rows)
    for layer in range(layers):
        last = layer == layers - 1
        all_users_t = exchange([users_t] * cols, "col", cols)
        all_items = lax.all_to_all(items_wide, "row", split_axis=0, concat_axis=0, tiled=True)
        user_parts = user_sums(place, adjacency, all_items.reshape(rows * ipd, -1), cols)
        item_parts = item_sums(place, adjacency, all_users_t, rows)
        user_parts = exchange(user_parts, "col", cols)
        item_parts = lax.all_to_all(item_parts, "row", split_axis=0, concat_axis=0, tiled=True)
        users, users_t = user_update(user_parts, users, weight_sum[layer], weight_product[layer])
        items, *wide = item_update(
            item_parts, items, weight_sum[layer], weight_product[layer], last
        )
        items_wide = None if last else wide[0]
    return (users, items[None])


def solution(mesh):
    placed = (
        P(("row", "col"), None),
        P(("row", "col")),
        P(("row", "col")),
        P(("row", "col")),
        P(),
        P(),
        P("row", "col"),
        P("row", "col"),
        P("row", "col"),
        P(),
        P(),
    )
    return jax.shard_map(
        per_device,
        mesh=mesh,
        in_specs=placed,
        out_specs=(P(("row", "col"), None), P("col", "row", None)),
        check_vma=False,
    )
```

```python
import functools

import jax
import jax.numpy as jnp
from jax import lax
from jax.experimental import pallas as pl
from jax.experimental.pallas import tpu as pltpu
from jax.sharding import PartitionSpec as P


TILE = 128
LANES = 128
CODE_ROWS = 8
F32 = jnp.float32
BF16 = jnp.bfloat16
NT = (((1,), (1,)), ((), ()))


def power_of_two(n):
    return n & (n - 1) == 0


def peer_to(i, k, n):
    return i ^ k if power_of_two(n) else (i + k) % n


def peer_from(i, k, n):
    return i ^ k if power_of_two(n) else (i + n - k) % n


def vmem_spec():
    return pl.BlockSpec(memory_space=pltpu.VMEM)


def params():
    return pltpu.CompilerParams(vmem_limit_bytes=24 * 2**20)


def whole_vmem():
    return pltpu.CompilerParams(vmem_limit_bytes=67_043_328)


def no_room():
    return pltpu.CompilerParams(vmem_limit_bytes=52 * 2**20)


def dispatch_kernel(devices, slots, *refs):
    sources, out_ref, (raw_ref, dest_ref, slot_ref, wide_ref), sems = (
        refs[:4],
        refs[4],
        refs[5:9],
        refs[9],
    )
    copies = [
        pltpu.make_async_copy(source, ref, sems.at[n])
        for n, (source, ref) in enumerate(
            zip(sources, (raw_ref, dest_ref, slot_ref, wide_ref), strict=True)
        )
    ]
    for copy in copies:
        copy.start()
    copies[1].wait()
    features, rows = raw_ref.shape
    chunks = rows // LANES
    dest = dest_ref[...]
    hot = (lax.broadcasted_iota(jnp.int32, (devices, rows), 0) == dest).astype(F32)
    hot_bf = hot.astype(BF16)
    before = lax.broadcasted_iota(jnp.int32, (LANES, 2 * LANES), 0)
    column = lax.broadcasted_iota(jnp.int32, (LANES, 2 * LANES), 1)
    prefix = ((before < column) | (column >= LANES)).astype(F32).astype(BF16)
    base = jnp.zeros((devices, LANES), F32)
    ranks = []
    for chunk in range(chunks):
        lanes = slice(chunk * LANES, (chunk + 1) * LANES)
        counted = jnp.dot(hot_bf[:, lanes], prefix, preferred_element_type=F32)
        ranks.append(
            jnp.sum((counted[:, :LANES] + base) * hot[:, lanes], axis=0, keepdims=True)
        )
        base = base + counted[:, LANES:]
    rank = jnp.concatenate(ranks, axis=1)
    place = (
        lax.broadcasted_iota(jnp.int32, (slots, rows), 0).astype(F32) == rank
    ).astype(F32).astype(BF16)
    for copy in (copies[0], copies[2], copies[3]):
        copy.wait()
    slot = slot_ref[...]
    code = lax.broadcasted_iota(jnp.int32, (2 * CODE_ROWS, rows), 0)
    codes = jnp.where(
        code == 0,
        slot // 256,
        jnp.where(code == 1, slot % 256, jnp.where(code == 2, wide_ref[...], 0)),
    )
    ext = jnp.concatenate([raw_ref[...], codes.astype(F32).astype(BF16)], axis=0)
    group = 8
    for first in range(0, devices, group):
        masked = jnp.concatenate(
            [ext * hot_bf[d : d + 1, :] for d in range(first, first + group)], axis=0
        )
        placed = lax.dot_general(masked, place, NT, preferred_element_type=F32).astype(BF16)
        for d in range(group):
            start = d * (features + 2 * CODE_ROWS)
            out_ref[first + d] = placed[start : start + features + CODE_ROWS]


def dispatch(raw, dest, slot, wide, devices, slots):
    features, rows = raw.shape
    return pl.pallas_call(
        functools.partial(dispatch_kernel, devices, slots),
        out_shape=jax.ShapeDtypeStruct((devices, features + CODE_ROWS, slots), BF16),
        in_specs=[pl.BlockSpec(memory_space=pltpu.HBM)] * 4,
        out_specs=vmem_spec(),
        scratch_shapes=[
            pltpu.VMEM(raw.shape, raw.dtype),
            *[pltpu.VMEM((1, rows), jnp.int32) for _ in range(3)],
            pltpu.SemaphoreType.DMA((4,)),
        ],
        compiler_params=whole_vmem(),
        name="dispatch",
    )(raw, dest, slot, wide)


def segment_kernel(narrow, upd, recv_ref, proj_narrow_ref, proj_wide_ref, *out_refs):
    user_ref, user_t_ref, item_ref, items_ref = out_refs
    devices, height, slots = recv_ref.shape
    features = height - CODE_ROWS
    nodes = user_ref.shape[0] + item_ref.shape[0]
    group = 8
    total = jnp.zeros((nodes, features + narrow), F32)
    for first in range(0, devices, group):
        block = jnp.concatenate([recv_ref[first + p] for p in range(group)], axis=1)
        codes = block[features:].astype(F32)
        node = (codes[0:1] * 256 + codes[1:2]).astype(jnp.int32)
        wide = codes[2:3].astype(BF16)
        rows = block[:features]
        values = jnp.concatenate([rows * wide, rows[:narrow] * (1 - wide)], axis=0)
        hot = (
            lax.broadcasted_iota(jnp.int32, (nodes, group * slots), 0) == node
        ).astype(F32).astype(BF16)
        total = total + lax.dot_general(hot, values, NT, preferred_element_type=F32)
    weights = jnp.concatenate([proj_wide_ref[...], proj_narrow_ref[...]], axis=0)
    initial = jnp.zeros((nodes, weights.shape[1]), F32)
    rest = total
    for _ in range(3):
        part = rest.astype(BF16)
        initial = initial + jnp.dot(part, weights, preferred_element_type=F32)
        rest = rest - part.astype(F32)
    users = initial[:upd]
    items = initial[upd:].astype(BF16)
    user_ref[...] = users.astype(BF16)
    user_t_ref[...] = users.T.astype(BF16)
    item_ref[...] = items
    for r in range(items_ref.shape[0]):
        items_ref[r] = items


def segment(recv, proj_narrow, proj_wide, upd, ipd, rows):
    d = proj_wide.shape[1]
    return pl.pallas_call(
        functools.partial(segment_kernel, proj_narrow.shape[0], upd),
        out_shape=(
            jax.ShapeDtypeStruct((upd, d), BF16),
            jax.ShapeDtypeStruct((d, upd), BF16),
            jax.ShapeDtypeStruct((ipd, d), BF16),
            jax.ShapeDtypeStruct((rows, ipd, d), BF16),
        ),
        in_specs=[vmem_spec()] * 3,
        out_specs=(vmem_spec(),) * 4,
        compiler_params=params(),
        name="segment",
    )(recv, proj_narrow, proj_wide)


def dequantize_kernel(mask_ref, scale_ref, values_ref, out_ref):
    i = pl.program_id(0)
    for j in range(values_ref.shape[1] // TILE):
        lanes = slice(j * TILE, (j + 1) * TILE)
        factor = mask_ref[i, j].astype(F32) * scale_ref[i, j]
        out_ref[:, lanes] = (values_ref[:, lanes].astype(F32) * factor).astype(BF16)


def dequantize(values, mask, scale):
    m, n = values.shape
    smem = pl.BlockSpec(memory_space=pltpu.SMEM)
    spec = pl.BlockSpec((TILE, n), lambda i: (i, 0))
    return pl.pallas_call(
        dequantize_kernel,
        out_shape=jax.ShapeDtypeStruct((m, n), BF16),
        grid=(m // TILE,),
        in_specs=[smem, smem, spec],
        out_specs=spec,
        compiler_params=no_room(),
        cost_estimate=pl.CostEstimate(flops=m * n, bytes_accessed=4 * m * n, transcendentals=0),
        name="dequantize",
    )(mask, scale, values)


def fetch_blocks(source, held, sems, order):
    upd = held.shape[1]
    copies = []
    for k, block in enumerate(order):
        start = pl.multiple_of(block * upd, upd)
        copies.append(
            pltpu.make_async_copy(source.at[pl.ds(start, upd), :], held.at[k], sems.at[k])
        )
        copies[-1].start()
    return copies


def user_sum_kernel(place_ref, adj_ref, items_ref, *refs):
    out_refs, (held, sems) = refs[:-2], refs[-2:]
    cols = len(out_refs)
    copies = fetch_blocks(
        adj_ref, held, sems, [peer_to(place_ref[0], k, cols) for k in range(cols)]
    )
    items = items_ref[...]
    for k, out_ref in enumerate(out_refs):
        copies[k].wait()
        out_ref[...] = jnp.dot(held[k], items, preferred_element_type=F32).astype(BF16)


def user_sums(place, adjacency, items, cols):
    m, n = adjacency.shape
    d = items.shape[1]
    return pl.pallas_call(
        user_sum_kernel,
        out_shape=(jax.ShapeDtypeStruct((m // cols, d), BF16),) * cols,
        in_specs=[
            pl.BlockSpec(memory_space=pltpu.SMEM),
            pl.BlockSpec(memory_space=pltpu.HBM),
            vmem_spec(),
        ],
        out_specs=(vmem_spec(),) * cols,
        scratch_shapes=[
            pltpu.VMEM((cols, m // cols, n), BF16),
            pltpu.SemaphoreType.DMA((cols,)),
        ],
        compiler_params=no_room(),
        cost_estimate=pl.CostEstimate(
            flops=2 * m * n * d, bytes_accessed=2 * m * n, transcendentals=0
        ),
        name="user_sums",
    )(place, adjacency, items)


def item_sum_kernel(place_ref, adj_ref, *refs):
    users_refs, (out_ref, held, total, sems) = refs[:-4], refs[-4:]
    cols = len(users_refs)
    rows, _, ipd = out_ref.shape
    copies = fetch_blocks(
        adj_ref, held, sems, [peer_from(place_ref[0], k, cols) for k in range(cols)]
    )
    for k in range(cols):
        copies[k].wait()
        users = users_refs[k][...]
        for r in range(rows):
            lanes = slice(r * ipd, (r + 1) * ipd)
            part = jnp.dot(users, held[k, :, lanes], preferred_element_type=F32)
            if k > 0:
                part = part + total[r]
            if k < cols - 1:
                total[r] = part
            else:
                out_ref[r] = part.astype(BF16)


def item_sums(place, adjacency, users_t, rows):
    m, n = adjacency.shape
    cols = len(users_t)
    d, _ = users_t[0].shape
    return pl.pallas_call(
        item_sum_kernel,
        out_shape=jax.ShapeDtypeStruct((rows, d, n // rows), BF16),
        in_specs=[
            pl.BlockSpec(memory_space=pltpu.SMEM),
            pl.BlockSpec(memory_space=pltpu.HBM),
        ]
        + [vmem_spec()] * cols,
        out_specs=vmem_spec(),
        scratch_shapes=[
            pltpu.VMEM((cols, m // cols, n), BF16),
            pltpu.VMEM((rows, d, n // rows), F32),
            pltpu.SemaphoreType.DMA((cols,)),
        ],
        compiler_params=no_room(),
        cost_estimate=pl.CostEstimate(
            flops=2 * m * n * d, bytes_accessed=2 * m * n, transcendentals=0
        ),
        name="item_sums",
    )(place, adjacency, *users_t)


def updated(side, own, weight_sum, weight_product):
    own = own.astype(F32)
    linear = jnp.dot((side + own).astype(BF16), weight_sum, preferred_element_type=F32)
    linear = linear + jnp.dot(
        (side * own).astype(BF16), weight_product, preferred_element_type=F32
    )
    return jnp.where(linear > 0, linear, 0.2 * linear)


def user_update_kernel(layer, own_ref, sum_ref, product_ref, *refs):
    parts, outs = refs[:-2], refs[-2:]
    side = parts[0][...].astype(F32)
    for part in parts[1:]:
        side = side + part[...].astype(F32)
    new = updated(side, own_ref[...], sum_ref[layer], product_ref[layer])
    outs[0][...] = new.astype(BF16)
    outs[1][...] = new.T.astype(BF16)


def user_update(layer, parts, own, weight_sum, weight_product):
    upd, d = own.shape
    return pl.pallas_call(
        functools.partial(user_update_kernel, layer),
        out_shape=(jax.ShapeDtypeStruct((upd, d), BF16), jax.ShapeDtypeStruct((d, upd), BF16)),
        in_specs=[vmem_spec()] * (3 + len(parts)),
        out_specs=(vmem_spec(),) * 2,
        compiler_params=params(),
        name="user_update",
    )(own, weight_sum, weight_product, *parts)


def item_update_kernel(layer, own_ref, sum_ref, product_ref, parts_ref, new_ref, *wide_refs):
    side = parts_ref[0].astype(F32)
    for r in range(1, parts_ref.shape[0]):
        side = side + parts_ref[r].astype(F32)
    new = updated(side.T, own_ref[...], sum_ref[layer], product_ref[layer]).astype(BF16)
    new_ref[...] = new
    for wide_ref in wide_refs:
        for r in range(wide_ref.shape[0]):
            wide_ref[r] = new


def item_update(layer, parts, own, weight_sum, weight_product, last):
    ipd, d = own.shape
    rows = parts.shape[0]
    outs = [jax.ShapeDtypeStruct((ipd, d), BF16)]
    if not last:
        outs.append(jax.ShapeDtypeStruct((rows, ipd, d), BF16))
    return pl.pallas_call(
        functools.partial(item_update_kernel, layer),
        out_shape=outs,
        in_specs=[vmem_spec()] * 4,
        out_specs=[vmem_spec()] * len(outs),
        compiler_params=params(),
        name="item_update",
    )(own, weight_sum, weight_product, parts)


def exchange(blocks, axis, n):
    received = [blocks[0]]
    for k in range(1, n):
        pairs = [(i, peer_to(i, k, n)) for i in range(n)]
        received.append(lax.ppermute(blocks[k], axis, pairs))
    return received


def per_device(
    raw_rows,
    raw_wide,
    raw_dest,
    raw_slot,
    proj_narrow,
    proj_wide,
    adj_values,
    tile_mask,
    tile_scale,
    weight_sum,
    weight_product,
):
    rows = lax.axis_size("row")
    cols = lax.axis_size("col")
    devices = rows * cols
    count = raw_rows.shape[0]
    capacity = 3 * count // devices
    slots = -(-capacity // LANES) * LANES
    upd = adj_values.shape[0] // cols
    ipd = adj_values.shape[1] // rows
    layers = weight_sum.shape[0]
    place = lax.axis_index("col").astype(jnp.int32).reshape(1)
    send = dispatch(
        raw_rows.T,
        raw_dest.reshape(1, count),
        raw_slot.reshape(1, count),
        raw_wide.reshape(1, count),
        devices,
        slots,
    )
    recv = lax.all_to_all(send, ("row", "col"), split_axis=0, concat_axis=0, tiled=True)
    adjacency = dequantize(adj_values, tile_mask, tile_scale)
    users, users_t, items, items_wide = segment(
        recv, proj_narrow, proj_wide, upd, ipd, rows
    )
    for layer in range(layers):
        last = layer == layers - 1
        all_items = lax.all_to_all(
            items_wide, "row", split_axis=0, concat_axis=0, tiled=True
        )
        all_users_t = exchange([users_t] * cols, "col", cols)
        item_parts = item_sums(place, adjacency, all_users_t, rows)
        item_parts = lax.all_to_all(
            item_parts, "row", split_axis=0, concat_axis=0, tiled=True
        )
        user_parts = user_sums(
            place, adjacency, all_items.reshape(rows * ipd, -1), cols
        )
        user_parts = exchange(user_parts, "col", cols)
        items, *wide = item_update(
            layer, item_parts, items, weight_sum, weight_product, last
        )
        items_wide = None if last else wide[0]
        users, users_t = user_update(
            layer, user_parts, users, weight_sum, weight_product
        )
    return (users, items[None])


def solution(mesh):
    placed = (
        P(("row", "col"), None),
        P(("row", "col")),
        P(("row", "col")),
        P(("row", "col")),
        P(),
        P(),
        P("row", "col"),
        P("row", "col"),
        P("row", "col"),
        P(),
        P(),
    )
    return jax.shard_map(
        per_device,
        mesh=mesh,
        in_specs=placed,
        out_specs=(P(("row", "col"), None), P("col", "row", None)),
        check_vma=False,
    )
```

```python
import functools

import jax
import jax.numpy as jnp
from jax import lax
from jax.experimental import pallas as pl
from jax.experimental.pallas import tpu as pltpu
from jax.sharding import PartitionSpec as P


TILE = 128
LANES = 128
CODE_ROWS = 8
F32 = jnp.float32
BF16 = jnp.bfloat16
NT = (((1,), (1,)), ((), ()))


def power_of_two(n):
    return n & (n - 1) == 0


def peer_to(i, k, n):
    return i ^ k if power_of_two(n) else (i + k) % n


def vmem_spec():
    return pl.BlockSpec(memory_space=pltpu.VMEM)


def params():
    return pltpu.CompilerParams(vmem_limit_bytes=24 * 2**20)


def whole_vmem():
    return pltpu.CompilerParams(vmem_limit_bytes=67_043_328)


def no_room():
    return pltpu.CompilerParams(vmem_limit_bytes=52 * 2**20)


def dispatch_kernel(devices, slots, *refs):
    sources, out_ref, (raw_ref, dest_ref, slot_ref, wide_ref), sems = (
        refs[:4],
        refs[4],
        refs[5:9],
        refs[9],
    )
    copies = [
        pltpu.make_async_copy(source, ref, sems.at[n])
        for n, (source, ref) in enumerate(
            zip(sources, (raw_ref, dest_ref, slot_ref, wide_ref), strict=True)
        )
    ]
    for copy in copies:
        copy.start()
    copies[1].wait()
    features, rows = raw_ref.shape
    chunks = rows // LANES
    dest = dest_ref[...]
    hot = (lax.broadcasted_iota(jnp.int32, (devices, rows), 0) == dest).astype(F32)
    hot_bf = hot.astype(BF16)
    before = lax.broadcasted_iota(jnp.int32, (LANES, 2 * LANES), 0)
    column = lax.broadcasted_iota(jnp.int32, (LANES, 2 * LANES), 1)
    prefix = ((before < column) | (column >= LANES)).astype(F32).astype(BF16)
    base = jnp.zeros((devices, LANES), F32)
    ranks = []
    for chunk in range(chunks):
        lanes = slice(chunk * LANES, (chunk + 1) * LANES)
        counted = jnp.dot(hot_bf[:, lanes], prefix, preferred_element_type=F32)
        ranks.append(
            jnp.sum((counted[:, :LANES] + base) * hot[:, lanes], axis=0, keepdims=True)
        )
        base = base + counted[:, LANES:]
    rank = jnp.concatenate(ranks, axis=1)
    place = (
        lax.broadcasted_iota(jnp.int32, (slots, rows), 0).astype(F32) == rank
    ).astype(F32).astype(BF16)
    for copy in (copies[0], copies[2], copies[3]):
        copy.wait()
    slot = slot_ref[...]
    code = lax.broadcasted_iota(jnp.int32, (2 * CODE_ROWS, rows), 0)
    codes = jnp.where(
        code == 0,
        slot // 256,
        jnp.where(code == 1, slot % 256, jnp.where(code == 2, wide_ref[...], 0)),
    )
    ext = jnp.concatenate([raw_ref[...], codes.astype(F32).astype(BF16)], axis=0)
    group = 8
    for first in range(0, devices, group):
        masked = jnp.concatenate(
            [ext * hot_bf[d : d + 1, :] for d in range(first, first + group)], axis=0
        )
        placed = lax.dot_general(masked, place, NT, preferred_element_type=F32).astype(BF16)
        for d in range(group):
            start = d * (features + 2 * CODE_ROWS)
            out_ref[first + d] = placed[start : start + features + CODE_ROWS]


def dispatch(raw, dest, slot, wide, devices, slots):
    features, rows = raw.shape
    return pl.pallas_call(
        functools.partial(dispatch_kernel, devices, slots),
        out_shape=jax.ShapeDtypeStruct((devices, features + CODE_ROWS, slots), BF16),
        in_specs=[pl.BlockSpec(memory_space=pltpu.HBM)] * 4,
        out_specs=vmem_spec(),
        scratch_shapes=[
            pltpu.VMEM(raw.shape, raw.dtype),
            *[pltpu.VMEM((1, rows), jnp.int32) for _ in range(3)],
            pltpu.SemaphoreType.DMA((4,)),
        ],
        compiler_params=whole_vmem(),
        name="dispatch",
    )(raw, dest, slot, wide)


def segment_kernel(narrow, upd, recv_ref, proj_narrow_ref, proj_wide_ref, *out_refs):
    user_ref, user_t_ref, item_ref, items_ref = out_refs
    devices, height, slots = recv_ref.shape
    features = height - CODE_ROWS
    nodes = user_ref.shape[0] + item_ref.shape[0]
    group = 8
    total = jnp.zeros((nodes, features + narrow), F32)
    for first in range(0, devices, group):
        block = jnp.concatenate([recv_ref[first + p] for p in range(group)], axis=1)
        codes = block[features:].astype(F32)
        node = (codes[0:1] * 256 + codes[1:2]).astype(jnp.int32)
        wide = codes[2:3].astype(BF16)
        rows = block[:features]
        values = jnp.concatenate([rows * wide, rows[:narrow] * (1 - wide)], axis=0)
        hot = (
            lax.broadcasted_iota(jnp.int32, (nodes, group * slots), 0) == node
        ).astype(F32).astype(BF16)
        total = total + lax.dot_general(hot, values, NT, preferred_element_type=F32)
    weights = jnp.concatenate([proj_wide_ref[...], proj_narrow_ref[...]], axis=0)
    initial = jnp.zeros((nodes, weights.shape[1]), F32)
    rest = total
    for _ in range(3):
        part = rest.astype(BF16)
        initial = initial + jnp.dot(part, weights, preferred_element_type=F32)
        rest = rest - part.astype(F32)
    users = initial[:upd]
    items = initial[upd:].astype(BF16)
    user_ref[...] = users.astype(BF16)
    user_t_ref[...] = users.T.astype(BF16)
    item_ref[...] = items
    for r in range(items_ref.shape[0]):
        items_ref[r] = items


def segment(recv, proj_narrow, proj_wide, upd, ipd, rows):
    d = proj_wide.shape[1]
    return pl.pallas_call(
        functools.partial(segment_kernel, proj_narrow.shape[0], upd),
        out_shape=(
            jax.ShapeDtypeStruct((upd, d), BF16),
            jax.ShapeDtypeStruct((d, upd), BF16),
            jax.ShapeDtypeStruct((ipd, d), BF16),
            jax.ShapeDtypeStruct((rows, ipd, d), BF16),
        ),
        in_specs=[vmem_spec()] * 3,
        out_specs=(vmem_spec(),) * 4,
        compiler_params=params(),
        name="segment",
    )(recv, proj_narrow, proj_wide)


def dequantize_kernel(place_ref, mask_ref, scale_ref, values_ref, *refs):
    out_refs, (held, sems) = refs[:-2], refs[-2:]
    cols = len(out_refs)
    upd, n = out_refs[0].shape
    blocks = [peer_to(place_ref[0], k, cols) for k in range(cols)]
    copies = []
    for k, block in enumerate(blocks):
        start = pl.multiple_of(block * upd, upd)
        copies.append(
            pltpu.make_async_copy(values_ref.at[pl.ds(start, upd), :], held.at[k], sems.at[k])
        )
        copies[-1].start()
    for k, (block, out_ref) in enumerate(zip(blocks, out_refs, strict=True)):
        copies[k].wait()
        for i in range(upd // TILE):
            row = block * (upd // TILE) + i
            here = slice(i * TILE, (i + 1) * TILE)
            for j in range(n // TILE):
                lanes = slice(j * TILE, (j + 1) * TILE)
                factor = mask_ref[row, j].astype(F32) * scale_ref[row, j]
                out_ref[here, lanes] = (held[k, here, lanes].astype(F32) * factor).astype(BF16)


def dequantize(place, values, mask, scale, cols):
    m, n = values.shape
    smem = pl.BlockSpec(memory_space=pltpu.SMEM)
    return pl.pallas_call(
        dequantize_kernel,
        out_shape=(jax.ShapeDtypeStruct((m // cols, n), BF16),) * cols,
        in_specs=[smem, smem, smem, pl.BlockSpec(memory_space=pltpu.HBM)],
        out_specs=(vmem_spec(),) * cols,
        scratch_shapes=[
            pltpu.VMEM((cols, m // cols, n), BF16),
            pltpu.SemaphoreType.DMA((cols,)),
        ],
        compiler_params=no_room(),
        cost_estimate=pl.CostEstimate(flops=m * n, bytes_accessed=4 * m * n, transcendentals=0),
        name="dequantize",
    )(place, mask, scale, values)


def user_sum_kernel(cols, *refs):
    adj_refs, items_ref, out_refs = refs[:cols], refs[cols], refs[cols + 1 :]
    items = items_ref[...]
    for adj_ref, out_ref in zip(adj_refs, out_refs, strict=True):
        out_ref[...] = jnp.dot(adj_ref[...], items, preferred_element_type=F32).astype(BF16)


def user_sums(adjacency, items):
    cols = len(adjacency)
    upd, n = adjacency[0].shape
    d = items.shape[1]
    return pl.pallas_call(
        functools.partial(user_sum_kernel, cols),
        out_shape=(jax.ShapeDtypeStruct((upd, d), BF16),) * cols,
        in_specs=[vmem_spec()] * (cols + 1),
        out_specs=(vmem_spec(),) * cols,
        compiler_params=params(),
        cost_estimate=pl.CostEstimate(
            flops=2 * cols * upd * n * d, bytes_accessed=2 * cols * upd * n, transcendentals=0
        ),
        name="user_sums",
    )(*adjacency, items)


def item_sum_kernel(cols, *refs):
    adj_refs, users_refs, out_ref = refs[:cols], refs[cols : 2 * cols], refs[-1]
    rows, _, ipd = out_ref.shape
    order = [0] + [k if power_of_two(cols) else cols - k for k in range(1, cols)]
    users = [ref[...] for ref in users_refs]
    for r in range(rows):
        lanes = slice(r * ipd, (r + 1) * ipd)
        total = None
        for k in range(cols):
            part = jnp.dot(
                users[k], adj_refs[order[k]][:, lanes], preferred_element_type=F32
            )
            total = part if total is None else total + part
        out_ref[r] = total.astype(BF16)


def item_sums(adjacency, users_t, rows):
    cols = len(adjacency)
    upd, n = adjacency[0].shape
    d = users_t[0].shape[0]
    return pl.pallas_call(
        functools.partial(item_sum_kernel, cols),
        out_shape=jax.ShapeDtypeStruct((rows, d, n // rows), BF16),
        in_specs=[vmem_spec()] * (2 * cols),
        out_specs=vmem_spec(),
        compiler_params=params(),
        cost_estimate=pl.CostEstimate(
            flops=2 * cols * upd * n * d, bytes_accessed=2 * cols * upd * n, transcendentals=0
        ),
        name="item_sums",
    )(*adjacency, *users_t)


def updated(side, own, weight_sum, weight_product):
    own = own.astype(F32)
    linear = jnp.dot((side + own).astype(BF16), weight_sum, preferred_element_type=F32)
    linear = linear + jnp.dot(
        (side * own).astype(BF16), weight_product, preferred_element_type=F32
    )
    return jnp.where(linear > 0, linear, 0.2 * linear)


def user_update_kernel(layer, own_ref, sum_ref, product_ref, *refs):
    parts, outs = refs[:-2], refs[-2:]
    side = parts[0][...].astype(F32)
    for part in parts[1:]:
        side = side + part[...].astype(F32)
    new = updated(side, own_ref[...], sum_ref[layer], product_ref[layer])
    outs[0][...] = new.astype(BF16)
    outs[1][...] = new.T.astype(BF16)


def user_update(layer, parts, own, weight_sum, weight_product):
    upd, d = own.shape
    return pl.pallas_call(
        functools.partial(user_update_kernel, layer),
        out_shape=(jax.ShapeDtypeStruct((upd, d), BF16), jax.ShapeDtypeStruct((d, upd), BF16)),
        in_specs=[vmem_spec()] * (3 + len(parts)),
        out_specs=(vmem_spec(),) * 2,
        compiler_params=params(),
        name="user_update",
    )(own, weight_sum, weight_product, *parts)


def item_update_kernel(layer, own_ref, sum_ref, product_ref, parts_ref, new_ref, *wide_refs):
    side = parts_ref[0].astype(F32)
    for r in range(1, parts_ref.shape[0]):
        side = side + parts_ref[r].astype(F32)
    new = updated(side.T, own_ref[...], sum_ref[layer], product_ref[layer]).astype(BF16)
    new_ref[...] = new
    for wide_ref in wide_refs:
        for r in range(wide_ref.shape[0]):
            wide_ref[r] = new


def item_update(layer, parts, own, weight_sum, weight_product, last):
    ipd, d = own.shape
    rows = parts.shape[0]
    outs = [jax.ShapeDtypeStruct((ipd, d), BF16)]
    if not last:
        outs.append(jax.ShapeDtypeStruct((rows, ipd, d), BF16))
    return pl.pallas_call(
        functools.partial(item_update_kernel, layer),
        out_shape=outs,
        in_specs=[vmem_spec()] * 4,
        out_specs=[vmem_spec()] * len(outs),
        compiler_params=params(),
        name="item_update",
    )(own, weight_sum, weight_product, parts)


def exchange(blocks, axis, n):
    received = [blocks[0]]
    for k in range(1, n):
        pairs = [(i, peer_to(i, k, n)) for i in range(n)]
        received.append(lax.ppermute(blocks[k], axis, pairs))
    return received


def per_device(
    raw_rows,
    raw_wide,
    raw_dest,
    raw_slot,
    proj_narrow,
    proj_wide,
    adj_values,
    tile_mask,
    tile_scale,
    weight_sum,
    weight_product,
):
    rows = lax.axis_size("row")
    cols = lax.axis_size("col")
    devices = rows * cols
    count = raw_rows.shape[0]
    capacity = 3 * count // devices
    slots = -(-capacity // LANES) * LANES
    upd = adj_values.shape[0] // cols
    ipd = adj_values.shape[1] // rows
    layers = weight_sum.shape[0]
    place = lax.axis_index("col").astype(jnp.int32).reshape(1)
    send = dispatch(
        raw_rows.T,
        raw_dest.reshape(1, count),
        raw_slot.reshape(1, count),
        raw_wide.reshape(1, count),
        devices,
        slots,
    )
    recv = lax.all_to_all(send, ("row", "col"), split_axis=0, concat_axis=0, tiled=True)
    adjacency = dequantize(place, adj_values, tile_mask, tile_scale, cols)
    users, users_t, items, items_wide = segment(
        recv, proj_narrow, proj_wide, upd, ipd, rows
    )
    for layer in range(layers):
        last = layer == layers - 1
        all_items = lax.all_to_all(items_wide, "row", split_axis=0, concat_axis=0, tiled=True)
        all_users_t = exchange([users_t] * cols, "col", cols)
        item_parts = item_sums(adjacency, all_users_t, rows)
        item_parts = lax.all_to_all(item_parts, "row", split_axis=0, concat_axis=0, tiled=True)
        user_parts = user_sums(adjacency, all_items.reshape(rows * ipd, -1))
        user_parts = exchange(user_parts, "col", cols)
        items, *wide = item_update(layer, item_parts, items, weight_sum, weight_product, last)
        items_wide = None if last else wide[0]
        users, users_t = user_update(
            layer, user_parts, users, weight_sum, weight_product
        )
    return (users, items[None])


def solution(mesh):
    placed = (
        P(("row", "col"), None),
        P(("row", "col")),
        P(("row", "col")),
        P(("row", "col")),
        P(),
        P(),
        P("row", "col"),
        P("row", "col"),
        P("row", "col"),
        P(),
        P(),
    )
    return jax.shard_map(
        per_device,
        mesh=mesh,
        in_specs=placed,
        out_specs=(P(("row", "col"), None), P("col", "row", None)),
        check_vma=False,
    )
```

```python
import functools

import jax
import jax.numpy as jnp
from jax import lax
from jax.experimental import pallas as pl
from jax.experimental.pallas import tpu as pltpu
from jax.sharding import PartitionSpec as P


TILE = 128
LANES = 128
CODE_ROWS = 8
F32 = jnp.float32
BF16 = jnp.bfloat16
NT = (((1,), (1,)), ((), ()))


def power_of_two(n):
    return n & (n - 1) == 0


def peer_to(i, k, n):
    return i ^ k if power_of_two(n) else (i + k) % n


def vmem_spec():
    return pl.BlockSpec(memory_space=pltpu.VMEM)


def params():
    return pltpu.CompilerParams(vmem_limit_bytes=24 * 2**20)


def whole_vmem():
    return pltpu.CompilerParams(vmem_limit_bytes=67_043_328)


def no_room():
    return pltpu.CompilerParams(vmem_limit_bytes=52 * 2**20)


def dispatch_kernel(devices, slots, *refs):
    sources, out_ref, (raw_ref, dest_ref, slot_ref, wide_ref), sems = (
        refs[:4],
        refs[4],
        refs[5:9],
        refs[9],
    )
    copies = [
        pltpu.make_async_copy(source, ref, sems.at[n])
        for n, (source, ref) in enumerate(
            zip(sources, (raw_ref, dest_ref, slot_ref, wide_ref), strict=True)
        )
    ]
    for copy in copies:
        copy.start()
    copies[1].wait()
    features, rows = raw_ref.shape
    chunks = rows // LANES
    dest = dest_ref[...]
    hot = (lax.broadcasted_iota(jnp.int32, (devices, rows), 0) == dest).astype(F32)
    hot_bf = hot.astype(BF16)
    before = lax.broadcasted_iota(jnp.int32, (LANES, 2 * LANES), 0)
    column = lax.broadcasted_iota(jnp.int32, (LANES, 2 * LANES), 1)
    prefix = ((before < column) | (column >= LANES)).astype(F32).astype(BF16)
    base = jnp.zeros((devices, LANES), F32)
    ranks = []
    for chunk in range(chunks):
        lanes = slice(chunk * LANES, (chunk + 1) * LANES)
        counted = jnp.dot(hot_bf[:, lanes], prefix, preferred_element_type=F32)
        ranks.append(
            jnp.sum((counted[:, :LANES] + base) * hot[:, lanes], axis=0, keepdims=True)
        )
        base = base + counted[:, LANES:]
    rank = jnp.concatenate(ranks, axis=1)
    place = (
        lax.broadcasted_iota(jnp.int32, (slots, rows), 0).astype(F32) == rank
    ).astype(F32).astype(BF16)
    for copy in (copies[0], copies[2], copies[3]):
        copy.wait()
    slot = slot_ref[...]
    code = lax.broadcasted_iota(jnp.int32, (2 * CODE_ROWS, rows), 0)
    codes = jnp.where(
        code == 0,
        slot // 256,
        jnp.where(code == 1, slot % 256, jnp.where(code == 2, wide_ref[...], 0)),
    )
    ext = jnp.concatenate([raw_ref[...], codes.astype(F32).astype(BF16)], axis=0)
    group = 8
    for first in range(0, devices, group):
        masked = jnp.concatenate(
            [ext * hot_bf[d : d + 1, :] for d in range(first, first + group)], axis=0
        )
        placed = lax.dot_general(masked, place, NT, preferred_element_type=F32).astype(BF16)
        for d in range(group):
            start = d * (features + 2 * CODE_ROWS)
            out_ref[first + d] = placed[start : start + features + CODE_ROWS]


def dispatch(raw, dest, slot, wide, devices, slots):
    features, rows = raw.shape
    return pl.pallas_call(
        functools.partial(dispatch_kernel, devices, slots),
        out_shape=jax.ShapeDtypeStruct((devices, features + CODE_ROWS, slots), BF16),
        in_specs=[pl.BlockSpec(memory_space=pltpu.HBM)] * 4,
        out_specs=vmem_spec(),
        scratch_shapes=[
            pltpu.VMEM(raw.shape, raw.dtype),
            *[pltpu.VMEM((1, rows), jnp.int32) for _ in range(3)],
            pltpu.SemaphoreType.DMA((4,)),
        ],
        compiler_params=whole_vmem(),
        name="dispatch",
    )(raw, dest, slot, wide)


def segment_kernel(narrow, upd, cols, recv_ref, proj_narrow_ref, proj_wide_ref, *refs):
    adj_refs, (user_ref, user_t_ref, item_ref) = refs[:cols], refs[cols : cols + 3]
    held_refs, sems = refs[cols + 3 : -1], refs[-1]
    copies = [
        pltpu.make_async_copy(adj_ref, held_ref, sems.at[k])
        for k, (adj_ref, held_ref) in enumerate(zip(adj_refs, held_refs, strict=True))
    ]
    for copy in copies:
        copy.start()
    devices, height, slots = recv_ref.shape
    features = height - CODE_ROWS
    nodes = user_ref.shape[0] + item_ref.shape[0]
    group = 8
    total = jnp.zeros((nodes, features + narrow), F32)
    for first in range(0, devices, group):
        block = jnp.concatenate([recv_ref[first + p] for p in range(group)], axis=1)
        codes = block[features:].astype(F32)
        node = (codes[0:1] * 256 + codes[1:2]).astype(jnp.int32)
        wide = codes[2:3].astype(BF16)
        rows = block[:features]
        values = jnp.concatenate([rows * wide, rows[:narrow] * (1 - wide)], axis=0)
        hot = (
            lax.broadcasted_iota(jnp.int32, (nodes, group * slots), 0) == node
        ).astype(F32).astype(BF16)
        total = total + lax.dot_general(hot, values, NT, preferred_element_type=F32)
    weights = jnp.concatenate([proj_wide_ref[...], proj_narrow_ref[...]], axis=0)
    initial = jnp.zeros((nodes, weights.shape[1]), F32)
    rest = total
    for _ in range(3):
        part = rest.astype(BF16)
        initial = initial + jnp.dot(part, weights, preferred_element_type=F32)
        rest = rest - part.astype(F32)
    users = initial[:upd]
    items = initial[upd:].astype(BF16)
    user_ref[...] = users.astype(BF16)
    user_t_ref[...] = users.T.astype(BF16)
    item_ref[...] = items
    for copy in copies:
        copy.wait()


def segment(recv, proj_narrow, proj_wide, adjacency, upd, ipd):
    cols = len(adjacency)
    d = proj_wide.shape[1]
    return pl.pallas_call(
        functools.partial(segment_kernel, proj_narrow.shape[0], upd, cols),
        out_shape=(
            jax.ShapeDtypeStruct((upd, d), BF16),
            jax.ShapeDtypeStruct((d, upd), BF16),
            jax.ShapeDtypeStruct((ipd, d), BF16),
            *[jax.ShapeDtypeStruct(block.shape, BF16) for block in adjacency],
        ),
        in_specs=[vmem_spec()] * 3 + [pl.BlockSpec(memory_space=pltpu.HBM)] * cols,
        out_specs=(vmem_spec(),) * (3 + cols),
        scratch_shapes=[pltpu.SemaphoreType.DMA((cols,))],
        compiler_params=params(),
        name="segment",
    )(
        recv,
        proj_narrow,
        proj_wide,
        *[pltpu.with_memory_space_constraint(block, pltpu.HBM) for block in adjacency],
    )


def dequantize_kernel(shape, place_ref, mask_ref, scale_ref, values_ref, *refs):
    out_refs, (held, sems) = refs[:-2], refs[-2:]
    sides, chips, cols = shape
    upd, n = out_refs[0].shape
    ipd = n // (sides * chips)
    chip, side_here = place_ref[0] // sides, place_ref[0] % sides
    blocks = [peer_to(place_ref[1], k, cols) for k in range(cols)]
    lines = [
        peer_to(chip, k, chips) * sides + (side_here + side) % sides
        for side in range(sides)
        for k in range(chips)
    ]
    copies = []
    for k, block in enumerate(blocks):
        start = pl.multiple_of(block * upd, upd)
        for at, line in enumerate(lines):
            first = pl.multiple_of(line * ipd, ipd)
            copies.append(
                pltpu.make_async_copy(
                    values_ref.at[pl.ds(start, upd), pl.ds(first, ipd)],
                    held.at[k, :, pl.ds(at * ipd, ipd)],
                    sems.at[k, at],
                )
            )
            copies[-1].start()
    for k, (block, out_ref) in enumerate(zip(blocks, out_refs, strict=True)):
        for at, line in enumerate(lines):
            copies[k * len(lines) + at].wait()
            for i in range(upd // TILE):
                row = block * (upd // TILE) + i
                here = slice(i * TILE, (i + 1) * TILE)
                for j in range(ipd // TILE):
                    column = line * (ipd // TILE) + j
                    lanes = slice(at * ipd + j * TILE, at * ipd + (j + 1) * TILE)
                    factor = mask_ref[row, column].astype(F32) * scale_ref[row, column]
                    out_ref[here, lanes] = (
                        held[k, here, lanes].astype(F32) * factor
                    ).astype(BF16)


def dequantize(place, values, mask, scale, shape):
    m, n = values.shape
    sides, chips, cols = shape
    smem = pl.BlockSpec(memory_space=pltpu.SMEM)
    return pl.pallas_call(
        functools.partial(dequantize_kernel, shape),
        out_shape=(jax.ShapeDtypeStruct((m // cols, n), BF16),) * cols,
        in_specs=[smem, smem, smem, pl.BlockSpec(memory_space=pltpu.HBM)],
        out_specs=(vmem_spec(),) * cols,
        scratch_shapes=[
            pltpu.VMEM((cols, m // cols, n), BF16),
            pltpu.SemaphoreType.DMA((cols, sides * chips)),
        ],
        compiler_params=no_room(),
        cost_estimate=pl.CostEstimate(flops=m * n, bytes_accessed=4 * m * n, transcendentals=0),
        name="dequantize",
    )(place, mask, scale, values)


def from_order(n):
    return [k if power_of_two(n) else (n - k) % n for k in range(n)]


def user_sum_kernel(cols, *refs):
    adj_refs, items_refs, out_refs = refs[:cols], refs[cols:-cols], refs[-cols:]
    items = jnp.concatenate([ref[...] for ref in items_refs], axis=0)
    for adj_ref, out_ref in zip(adj_refs, out_refs, strict=True):
        out_ref[...] = jnp.dot(adj_ref[...], items, preferred_element_type=F32).astype(BF16)


def user_sums(adjacency, items):
    cols = len(adjacency)
    upd, n = adjacency[0].shape
    d = items[0].shape[1]
    return pl.pallas_call(
        functools.partial(user_sum_kernel, cols),
        out_shape=(jax.ShapeDtypeStruct((upd, d), BF16),) * cols,
        in_specs=[vmem_spec()] * (cols + len(items)),
        out_specs=(vmem_spec(),) * cols,
        compiler_params=params(),
        cost_estimate=pl.CostEstimate(
            flops=2 * cols * upd * n * d, bytes_accessed=2 * cols * upd * n, transcendentals=0
        ),
        name="user_sums",
    )(*adjacency, *items)


def item_sum_kernel(cols, *refs):
    adj_refs, users_refs, out_refs = refs[:cols], refs[cols : 2 * cols], refs[2 * cols :]
    order = from_order(cols)
    users = [ref[...] for ref in users_refs]
    at = 0
    for out_ref in reversed(out_refs):
        for r in range(out_ref.shape[0]):
            ipd = out_ref.shape[2]
            lanes = slice(at * ipd, (at + 1) * ipd)
            total = None
            for k in range(cols):
                part = jnp.dot(
                    users[k], adj_refs[order[k]][:, lanes], preferred_element_type=F32
                )
                total = part if total is None else total + part
            out_ref[r] = total.astype(out_ref.dtype)
            at += 1


def item_sums(adjacency, users_t, sides, chips):
    cols = len(adjacency)
    upd, n = adjacency[0].shape
    d = users_t[0].shape[0]
    block = (chips, d, n // (sides * chips))
    outs = [jax.ShapeDtypeStruct(block, BF16)] * (sides - 1)
    return pl.pallas_call(
        functools.partial(item_sum_kernel, cols),
        out_shape=[*outs, jax.ShapeDtypeStruct(block, F32)],
        in_specs=[vmem_spec()] * (2 * cols),
        out_specs=[vmem_spec()] * sides,
        compiler_params=params(),
        cost_estimate=pl.CostEstimate(
            flops=2 * cols * upd * n * d, bytes_accessed=2 * cols * upd * n, transcendentals=0
        ),
        name="item_sums",
    )(*adjacency, *users_t)


def item_add_kernel(chips, *refs):
    parts, outs = refs[:-chips], refs[-chips:]
    for k, out_ref in enumerate(outs):
        total = parts[0][k]
        for part in parts[1:]:
            total = total + part[k].astype(F32)
        out_ref[...] = total.astype(BF16)


def item_add(parts):
    chips, d, ipd = parts[0].shape
    return pl.pallas_call(
        functools.partial(item_add_kernel, chips),
        out_shape=(jax.ShapeDtypeStruct((d, ipd), BF16),) * chips,
        in_specs=[vmem_spec()] * len(parts),
        out_specs=(vmem_spec(),) * chips,
        compiler_params=params(),
        name="item_add",
    )(*parts)


def updated(side, own, weight_sum, weight_product):
    own = own.astype(F32)
    linear = jnp.dot((side + own).astype(BF16), weight_sum, preferred_element_type=F32)
    linear = linear + jnp.dot(
        (side * own).astype(BF16), weight_product, preferred_element_type=F32
    )
    return jnp.where(linear > 0, linear, 0.2 * linear)


def user_update_kernel(layer, own_ref, sum_ref, product_ref, *refs):
    parts, outs = refs[:-2], refs[-2:]
    side = parts[0][...].astype(F32)
    for part in parts[1:]:
        side = side + part[...].astype(F32)
    new = updated(side, own_ref[...], sum_ref[layer], product_ref[layer])
    outs[0][...] = new.astype(BF16)
    outs[1][...] = new.T.astype(BF16)


def user_update(layer, parts, own, weight_sum, weight_product):
    upd, d = own.shape
    return pl.pallas_call(
        functools.partial(user_update_kernel, layer),
        out_shape=(jax.ShapeDtypeStruct((upd, d), BF16), jax.ShapeDtypeStruct((d, upd), BF16)),
        in_specs=[vmem_spec()] * (3 + len(parts)),
        out_specs=(vmem_spec(),) * 2,
        compiler_params=params(),
        name="user_update",
    )(own, weight_sum, weight_product, *parts)


def item_update_kernel(layer, own_ref, sum_ref, product_ref, *refs):
    parts, new_ref = refs[:-1], refs[-1]
    side = parts[0][...].astype(F32)
    for part in parts[1:]:
        side = side + part[...].astype(F32)
    new = updated(side.T, own_ref[...], sum_ref[layer], product_ref[layer])
    new_ref[...] = new.astype(BF16)


def item_update(layer, parts, own, weight_sum, weight_product):
    return pl.pallas_call(
        functools.partial(item_update_kernel, layer),
        out_shape=jax.ShapeDtypeStruct(own.shape, BF16),
        in_specs=[vmem_spec()] * (3 + len(parts)),
        out_specs=vmem_spec(),
        compiler_params=params(),
        name="item_update",
    )(own, weight_sum, weight_product, *parts)


def exchange(blocks, axis, n, inner=1):
    received = [blocks[0]]
    for k in range(1, n):
        pairs = [
            (i * inner + j, peer_to(i, k, n) * inner + j) for i in range(n) for j in range(inner)
        ]
        received.append(lax.ppermute(blocks[k], axis, pairs))
    return received


def swap(block, axis, n):
    return lax.ppermute(block, axis, [(i, i ^ 1) for i in range(n)])


def ordered(received):
    order = from_order(len(received))
    return [received[order.index(k)] for k in range(len(received))]


def per_device(
    raw_rows,
    raw_wide,
    raw_dest,
    raw_slot,
    proj_narrow,
    proj_wide,
    adj_values,
    tile_mask,
    tile_scale,
    weight_sum,
    weight_product,
):
    rows = lax.axis_size("row")
    cols = lax.axis_size("col")
    devices = rows * cols
    count = raw_rows.shape[0]
    capacity = 3 * count // devices
    slots = -(-capacity // LANES) * LANES
    upd = adj_values.shape[0] // cols
    ipd = adj_values.shape[1] // rows
    layers = weight_sum.shape[0]
    sides = 2 if rows % 2 == 0 else 1
    chips = rows // sides
    place = jnp.stack([lax.axis_index("row"), lax.axis_index("col")]).astype(jnp.int32)
    send = dispatch(
        raw_rows.T,
        raw_dest.reshape(1, count),
        raw_slot.reshape(1, count),
        raw_wide.reshape(1, count),
        devices,
        slots,
    )
    recv = lax.all_to_all(send, ("row", "col"), split_axis=0, concat_axis=0, tiled=True)
    adjacency = dequantize(
        place, adj_values, tile_mask, tile_scale, (sides, chips, cols)
    )
    users, users_t, items, *adjacency = segment(recv, proj_narrow, proj_wide, adjacency, upd, ipd)
    for n in range(layers):
        all_users_t = exchange([users_t] * cols, "col", cols)
        own_swapped = [swap(items, "row", rows)]
        all_items = ordered(exchange([items] * chips, "row", chips, sides))
        swapped = [swap(block, "row", rows) for block in all_items[1:]]
        if sides > 1:
            all_items = [*all_items, *own_swapped, *swapped]
        *away, kept = item_sums(adjacency, all_users_t, sides, chips)
        came = [swap(part, "row", rows) for part in away]
        user_parts = user_sums(adjacency, all_items)
        item_parts = item_add([kept, *came])
        item_parts = exchange(item_parts, "row", chips, sides)
        user_parts = exchange(user_parts, "col", cols)
        items = item_update(n, item_parts, items, weight_sum, weight_product)
        users, users_t = user_update(n, user_parts, users, weight_sum, weight_product)
    return (users, items[None])


def solution(mesh):
    placed = (
        P(("row", "col"), None),
        P(("row", "col")),
        P(("row", "col")),
        P(("row", "col")),
        P(),
        P(),
        P("row", "col"),
        P("row", "col"),
        P("row", "col"),
        P(),
        P(),
    )
    return jax.shard_map(
        per_device,
        mesh=mesh,
        in_specs=placed,
        out_specs=(P(("row", "col"), None), P("col", "row", None)),
        check_vma=False,
    )
```

```python
import functools

import jax
import jax.numpy as jnp
from jax import lax
from jax.experimental import pallas as pl
from jax.experimental.pallas import tpu as pltpu
from jax.sharding import PartitionSpec as P


TILE = 128
LANES = 128
CODE_ROWS = 8
GROUP = 8
F32 = jnp.float32
BF16 = jnp.bfloat16
NT = (((1,), (1,)), ((), ()))


def power_of_two(n):
    return n & (n - 1) == 0


def peer_to(i, k, n):
    return i ^ k if power_of_two(n) else (i + k) % n


def vmem_spec():
    return pl.BlockSpec(memory_space=pltpu.VMEM)


def params():
    return pltpu.CompilerParams(vmem_limit_bytes=24 * 2**20)


def whole_vmem():
    return pltpu.CompilerParams(vmem_limit_bytes=67_043_328)


def no_room():
    return pltpu.CompilerParams(vmem_limit_bytes=52 * 2**20)


def chunks_of(capacity, features):
    chunks, base, row = [], 0, 0
    size = LANES // 2
    while base < capacity:
        while size > max(8, capacity - base):
            size //= 2
        height = features * size // LANES
        chunks.append((base, size, row, height))
        base += size
        row += height
    return chunks, -(-row // CODE_ROWS) * CODE_ROWS


def turned(block, shift):
    shift = shift % LANES
    return block if shift == 0 else pltpu.roll(block, shift, 1)


def packed(placed, codes, capacity):
    features = placed.shape[0]
    chunks, code_row = chunks_of(capacity, features)
    lane = lax.broadcasted_iota(jnp.int32, (1, LANES), 1)
    blocks, code_rows, height = [], jnp.zeros((CODE_ROWS, LANES), F32), 0
    code = lax.broadcasted_iota(jnp.int32, (CODE_ROWS, LANES), 0)
    for n, (base, size, row, rows) in enumerate(chunks):
        block = None
        for part in range(LANES // size):
            piece = turned(placed[part * rows : (part + 1) * rows], part * size - base)
            here = lane >= part * size
            block = piece if block is None else jnp.where(here, piece, block)
        blocks.append(block)
        height += rows
        low = turned(codes, -base)[0:1]
        high = turned(codes, size - base)[1:2]
        both = jnp.where(lane < size, low, jnp.where(lane < 2 * size, high, 0.0))
        code_rows = jnp.where(code == n, both, code_rows)
    if height < code_row:
        blocks.append(jnp.zeros((code_row - height, LANES), F32))
    return jnp.concatenate([*blocks, code_rows], axis=0)


def unpacked(block, features, capacity):
    chunks, code_row = chunks_of(capacity, features)
    lane = lax.broadcasted_iota(jnp.int32, (1, LANES), 1)
    placed = jnp.zeros((features, LANES), F32)
    low = jnp.zeros((1, LANES), F32)
    high = jnp.zeros((1, LANES), F32)
    codes = block[code_row:]
    for n, (base, size, row, rows) in enumerate(chunks):
        pieces = [
            turned(block[row : row + rows], base - part * size) for part in range(LANES // size)
        ]
        here = (lane >= base) & (lane < min(base + size, capacity))
        placed = jnp.where(here, jnp.concatenate(pieces, axis=0), placed)
        low = jnp.where(here, turned(codes, base)[n : n + 1], low)
        high = jnp.where(here, turned(codes, base - size)[n : n + 1], high)
    return placed, low, high


def dispatch_kernel(devices, capacity, *refs):
    sources, out_ref, (raw_ref, dest_ref, slot_ref, wide_ref, held), (sems, out_sems) = (
        refs[:4],
        refs[4],
        refs[5:10],
        refs[10:],
    )
    copies = [
        pltpu.make_async_copy(source, ref, sems.at[n])
        for n, (source, ref) in enumerate(
            zip(sources, (raw_ref, dest_ref, slot_ref, wide_ref), strict=True)
        )
    ]
    for copy in copies:
        copy.start()
    copies[1].wait()
    features, rows = raw_ref.shape
    chunks = rows // LANES
    dest = dest_ref[...]
    hot = (lax.broadcasted_iota(jnp.int32, (devices, rows), 0) == dest).astype(F32)
    hot_bf = hot.astype(BF16)
    before = lax.broadcasted_iota(jnp.int32, (LANES, 2 * LANES), 0)
    column = lax.broadcasted_iota(jnp.int32, (LANES, 2 * LANES), 1)
    prefix = ((before < column) | (column >= LANES)).astype(F32).astype(BF16)
    base = jnp.zeros((devices, LANES), F32)
    ranks = []
    for chunk in range(chunks):
        lanes = slice(chunk * LANES, (chunk + 1) * LANES)
        counted = jnp.dot(hot_bf[:, lanes], prefix, preferred_element_type=F32)
        ranks.append(
            jnp.sum((counted[:, :LANES] + base) * hot[:, lanes], axis=0, keepdims=True)
        )
        base = base + counted[:, LANES:]
    rank = jnp.concatenate(ranks, axis=1)
    place = (
        lax.broadcasted_iota(jnp.int32, (LANES, rows), 0).astype(F32) == rank
    ).astype(F32).astype(BF16)
    for copy in (copies[0], copies[2], copies[3]):
        copy.wait()
    slot = slot_ref[...]
    code = lax.broadcasted_iota(jnp.int32, (2 * CODE_ROWS, rows), 0)
    codes = jnp.where(
        code == 0,
        slot % 256,
        jnp.where(code == 1, slot // 256 * 2 + wide_ref[...], 0),
    )
    ext = jnp.concatenate([raw_ref[...], codes.astype(F32).astype(BF16)], axis=0)
    height = ext.shape[0]
    writes = []
    for n, first in enumerate(range(0, devices, GROUP)):
        masked = jnp.concatenate(
            [ext * hot_bf[d : d + 1, :] for d in range(first, first + GROUP)], axis=0
        )
        placed = lax.dot_general(masked, place, NT, preferred_element_type=F32)
        for d in range(GROUP):
            mine = placed[d * height : (d + 1) * height]
            held[first + d] = packed(
                mine[:features], mine[features : features + CODE_ROWS], capacity
            ).astype(BF16)
        writes.append(
            pltpu.make_async_copy(
                held.at[pl.ds(first, GROUP)], out_ref.at[pl.ds(first, GROUP)], out_sems.at[n]
            )
        )
        writes[-1].start()
    for write in writes:
        write.wait()


def dispatch(raw, dest, slot, wide, devices, capacity):
    features, rows = raw.shape
    shape = (devices, chunks_of(capacity, features)[1] + CODE_ROWS, LANES)
    return pl.pallas_call(
        functools.partial(dispatch_kernel, devices, capacity),
        out_shape=jax.ShapeDtypeStruct(shape, BF16),
        in_specs=[pl.BlockSpec(memory_space=pltpu.HBM)] * 4,
        out_specs=pl.BlockSpec(memory_space=pltpu.HBM),
        scratch_shapes=[
            pltpu.VMEM(raw.shape, raw.dtype),
            *[pltpu.VMEM((1, rows), jnp.int32) for _ in range(3)],
            pltpu.VMEM(shape, BF16),
            pltpu.SemaphoreType.DMA((4,)),
            pltpu.SemaphoreType.DMA((devices // GROUP,)),
        ],
        compiler_params=whole_vmem(),
        name="dispatch",
    )(raw, dest, slot, wide)


def segment_kernel(capacity, upd, cols, recv_ref, proj_narrow_ref, proj_wide_ref, *refs):
    adj_refs, (user_ref, user_t_ref, item_ref) = refs[:cols], refs[cols : cols + 3]
    held_refs, sems = refs[cols + 3 : -1], refs[-1]
    copies = [
        pltpu.make_async_copy(adj_ref, held_ref, sems.at[k])
        for k, (adj_ref, held_ref) in enumerate(zip(adj_refs, held_refs, strict=True))
    ]
    for copy in copies:
        copy.start()
    devices = recv_ref.shape[0]
    narrow, features = proj_narrow_ref.shape[0], proj_wide_ref.shape[0]
    nodes = user_ref.shape[0] + item_ref.shape[0]
    total = jnp.zeros((nodes, features + narrow), F32)
    for first in range(0, devices, GROUP):
        parts = [
            unpacked(recv_ref[first + p].astype(F32), features, capacity) for p in range(GROUP)
        ]
        rows, low, high = (jnp.concatenate(part, axis=1) for part in zip(*parts, strict=True))
        rows = rows.astype(BF16)
        high = high.astype(jnp.int32)
        node = low.astype(jnp.int32) + (high >> 1) * 256
        wide = (high & 1).astype(F32).astype(BF16)
        values = jnp.concatenate([rows * wide, rows[:narrow] * (1 - wide)], axis=0)
        hot = (
            lax.broadcasted_iota(jnp.int32, (nodes, GROUP * LANES), 0) == node
        ).astype(F32).astype(BF16)
        total = total + lax.dot_general(hot, values, NT, preferred_element_type=F32)
    weights = jnp.concatenate([proj_wide_ref[...], proj_narrow_ref[...]], axis=0)
    initial = jnp.zeros((nodes, weights.shape[1]), F32)
    rest = total
    for _ in range(3):
        part = rest.astype(BF16)
        initial = initial + jnp.dot(part, weights, preferred_element_type=F32)
        rest = rest - part.astype(F32)
    users = initial[:upd]
    items = initial[upd:].astype(BF16)
    user_ref[...] = users.astype(BF16)
    user_t_ref[...] = users.T.astype(BF16)
    item_ref[...] = items
    for copy in copies:
        copy.wait()


def segment(recv, proj_narrow, proj_wide, adjacency, upd, ipd, capacity):
    cols = len(adjacency)
    d = proj_wide.shape[1]
    return pl.pallas_call(
        functools.partial(segment_kernel, capacity, upd, cols),
        out_shape=(
            jax.ShapeDtypeStruct((upd, d), BF16),
            jax.ShapeDtypeStruct((d, upd), BF16),
            jax.ShapeDtypeStruct((ipd, d), BF16),
            *[jax.ShapeDtypeStruct(block.shape, BF16) for block in adjacency],
        ),
        in_specs=[vmem_spec()] * 3 + [pl.BlockSpec(memory_space=pltpu.HBM)] * cols,
        out_specs=(vmem_spec(),) * (3 + cols),
        scratch_shapes=[pltpu.SemaphoreType.DMA((cols,))],
        compiler_params=params(),
        name="segment",
    )(
        recv,
        proj_narrow,
        proj_wide,
        *[pltpu.with_memory_space_constraint(block, pltpu.HBM) for block in adjacency],
    )


def dequantize_kernel(shape, place_ref, mask_ref, scale_ref, values_ref, *refs):
    out_refs, (held, sems) = refs[:-2], refs[-2:]
    sides, chips, cols = shape
    upd, n = out_refs[0].shape
    ipd = n // (sides * chips)
    chip, side_here = place_ref[0] // sides, place_ref[0] % sides
    blocks = [peer_to(place_ref[1], k, cols) for k in range(cols)]
    lines = [
        peer_to(chip, k, chips) * sides + (side_here + side) % sides
        for side in range(sides)
        for k in range(chips)
    ]
    copies = []
    for k, block in enumerate(blocks):
        start = pl.multiple_of(block * upd, upd)
        for at, line in enumerate(lines):
            first = pl.multiple_of(line * ipd, ipd)
            copies.append(
                pltpu.make_async_copy(
                    values_ref.at[pl.ds(start, upd), pl.ds(first, ipd)],
                    held.at[k, :, pl.ds(at * ipd, ipd)],
                    sems.at[k, at],
                )
            )
            copies[-1].start()
    for k, (block, out_ref) in enumerate(zip(blocks, out_refs, strict=True)):
        for at, line in enumerate(lines):
            copies[k * len(lines) + at].wait()
            for i in range(upd // TILE):
                row = block * (upd // TILE) + i
                here = slice(i * TILE, (i + 1) * TILE)
                for j in range(ipd // TILE):
                    column = line * (ipd // TILE) + j
                    lanes = slice(at * ipd + j * TILE, at * ipd + (j + 1) * TILE)
                    factor = mask_ref[row, column].astype(F32) * scale_ref[row, column]
                    out_ref[here, lanes] = (
                        held[k, here, lanes].astype(F32) * factor
                    ).astype(BF16)


def dequantize(place, values, mask, scale, shape):
    m, n = values.shape
    sides, chips, cols = shape
    smem = pl.BlockSpec(memory_space=pltpu.SMEM)
    return pl.pallas_call(
        functools.partial(dequantize_kernel, shape),
        out_shape=(jax.ShapeDtypeStruct((m // cols, n), BF16),) * cols,
        in_specs=[smem, smem, smem, pl.BlockSpec(memory_space=pltpu.HBM)],
        out_specs=(vmem_spec(),) * cols,
        scratch_shapes=[
            pltpu.VMEM((cols, m // cols, n), BF16),
            pltpu.SemaphoreType.DMA((cols, sides * chips)),
        ],
        compiler_params=no_room(),
        cost_estimate=pl.CostEstimate(flops=m * n, bytes_accessed=4 * m * n, transcendentals=0),
        name="dequantize",
    )(place, mask, scale, values)


def from_order(n):
    return [k if power_of_two(n) else (n - k) % n for k in range(n)]


def user_sum_kernel(cols, *refs):
    adj_refs, items_refs, out_refs = refs[:cols], refs[cols:-cols], refs[-cols:]
    items = jnp.concatenate([ref[...] for ref in items_refs], axis=0)
    for adj_ref, out_ref in zip(adj_refs, out_refs, strict=True):
        out_ref[...] = jnp.dot(adj_ref[...], items, preferred_element_type=F32).astype(BF16)


def user_sums(adjacency, items):
    cols = len(adjacency)
    upd, n = adjacency[0].shape
    d = items[0].shape[1]
    return pl.pallas_call(
        functools.partial(user_sum_kernel, cols),
        out_shape=(jax.ShapeDtypeStruct((upd, d), BF16),) * cols,
        in_specs=[vmem_spec()] * (cols + len(items)),
        out_specs=(vmem_spec(),) * cols,
        compiler_params=params(),
        cost_estimate=pl.CostEstimate(
            flops=2 * cols * upd * n * d, bytes_accessed=2 * cols * upd * n, transcendentals=0
        ),
        name="user_sums",
    )(*adjacency, *items)


def item_sum_kernel(cols, *refs):
    adj_refs, users_refs, out_refs = refs[:cols], refs[cols : 2 * cols], refs[2 * cols :]
    order = from_order(cols)
    users = [ref[...] for ref in users_refs]
    at = 0
    for out_ref in reversed(out_refs):
        for r in range(out_ref.shape[0]):
            ipd = out_ref.shape[2]
            lanes = slice(at * ipd, (at + 1) * ipd)
            total = None
            for k in range(cols):
                part = jnp.dot(
                    users[k], adj_refs[order[k]][:, lanes], preferred_element_type=F32
                )
                total = part if total is None else total + part
            out_ref[r] = total.astype(out_ref.dtype)
            at += 1


def item_sums(adjacency, users_t, sides, chips):
    cols = len(adjacency)
    upd, n = adjacency[0].shape
    d = users_t[0].shape[0]
    block = (chips, d, n // (sides * chips))
    outs = [jax.ShapeDtypeStruct(block, BF16)] * (sides - 1)
    return pl.pallas_call(
        functools.partial(item_sum_kernel, cols),
        out_shape=[*outs, jax.ShapeDtypeStruct(block, F32)],
        in_specs=[vmem_spec()] * (2 * cols),
        out_specs=[vmem_spec()] * sides,
        compiler_params=params(),
        cost_estimate=pl.CostEstimate(
            flops=2 * cols * upd * n * d, bytes_accessed=2 * cols * upd * n, transcendentals=0
        ),
        name="item_sums",
    )(*adjacency, *users_t)


def item_add_kernel(chips, *refs):
    parts, outs = refs[:-chips], refs[-chips:]
    for k, out_ref in enumerate(outs):
        total = parts[0][k]
        for part in parts[1:]:
            total = total + part[k].astype(F32)
        out_ref[...] = total.astype(BF16)


def item_add(parts):
    chips, d, ipd = parts[0].shape
    return pl.pallas_call(
        functools.partial(item_add_kernel, chips),
        out_shape=(jax.ShapeDtypeStruct((d, ipd), BF16),) * chips,
        in_specs=[vmem_spec()] * len(parts),
        out_specs=(vmem_spec(),) * chips,
        compiler_params=params(),
        name="item_add",
    )(*parts)


def updated(side, own, weight_sum, weight_product):
    own = own.astype(F32)
    linear = jnp.dot((side + own).astype(BF16), weight_sum, preferred_element_type=F32)
    linear = linear + jnp.dot(
        (side * own).astype(BF16), weight_product, preferred_element_type=F32
    )
    return jnp.where(linear > 0, linear, 0.2 * linear)


def user_update_kernel(layer, own_ref, sum_ref, product_ref, *refs):
    parts, outs = refs[:-2], refs[-2:]
    side = parts[0][...].astype(F32)
    for part in parts[1:]:
        side = side + part[...].astype(F32)
    new = updated(side, own_ref[...], sum_ref[layer], product_ref[layer])
    outs[0][...] = new.astype(BF16)
    outs[1][...] = new.T.astype(BF16)


def user_update(layer, parts, own, weight_sum, weight_product):
    upd, d = own.shape
    return pl.pallas_call(
        functools.partial(user_update_kernel, layer),
        out_shape=(jax.ShapeDtypeStruct((upd, d), BF16), jax.ShapeDtypeStruct((d, upd), BF16)),
        in_specs=[vmem_spec()] * (3 + len(parts)),
        out_specs=(vmem_spec(),) * 2,
        compiler_params=params(),
        name="user_update",
    )(own, weight_sum, weight_product, *parts)


def item_update_kernel(layer, own_ref, sum_ref, product_ref, *refs):
    parts, new_ref = refs[:-1], refs[-1]
    side = parts[0][...].astype(F32)
    for part in parts[1:]:
        side = side + part[...].astype(F32)
    new = updated(side.T, own_ref[...], sum_ref[layer], product_ref[layer])
    new_ref[...] = new.astype(BF16)


def item_update(layer, parts, own, weight_sum, weight_product):
    return pl.pallas_call(
        functools.partial(item_update_kernel, layer),
        out_shape=jax.ShapeDtypeStruct(own.shape, BF16),
        in_specs=[vmem_spec()] * (3 + len(parts)),
        out_specs=vmem_spec(),
        compiler_params=params(),
        name="item_update",
    )(own, weight_sum, weight_product, *parts)


def exchange(blocks, axis, n, inner=1):
    received = [blocks[0]]
    for k in range(1, n):
        pairs = [
            (i * inner + j, peer_to(i, k, n) * inner + j) for i in range(n) for j in range(inner)
        ]
        received.append(lax.ppermute(blocks[k], axis, pairs))
    return received


def swap(block, axis, n):
    return lax.ppermute(block, axis, [(i, i ^ 1) for i in range(n)])


def ordered(received):
    order = from_order(len(received))
    return [received[order.index(k)] for k in range(len(received))]


def per_device(
    raw_rows,
    raw_wide,
    raw_dest,
    raw_slot,
    proj_narrow,
    proj_wide,
    adj_values,
    tile_mask,
    tile_scale,
    weight_sum,
    weight_product,
):
    rows = lax.axis_size("row")
    cols = lax.axis_size("col")
    devices = rows * cols
    count = raw_rows.shape[0]
    capacity = 3 * count // devices
    upd = adj_values.shape[0] // cols
    ipd = adj_values.shape[1] // rows
    layers = weight_sum.shape[0]
    sides = 2 if rows % 2 == 0 else 1
    chips = rows // sides
    place = jnp.stack([lax.axis_index("row"), lax.axis_index("col")]).astype(jnp.int32)
    send = dispatch(
        raw_rows.T,
        raw_dest.reshape(1, count),
        raw_slot.reshape(1, count),
        raw_wide.reshape(1, count),
        devices,
        capacity,
    )
    recv = lax.all_to_all(send, ("row", "col"), split_axis=0, concat_axis=0, tiled=True)
    adjacency = dequantize(
        place, adj_values, tile_mask, tile_scale, (sides, chips, cols)
    )
    users, users_t, items, *adjacency = segment(
        recv, proj_narrow, proj_wide, adjacency, upd, ipd, capacity
    )
    for n in range(layers):
        all_users_t = exchange([users_t] * cols, "col", cols)
        own_swapped = [swap(items, "row", rows)]
        all_items = ordered(exchange([items] * chips, "row", chips, sides))
        swapped = [swap(block, "row", rows) for block in all_items[1:]]
        if sides > 1:
            all_items = [*all_items, *own_swapped, *swapped]
        *away, kept = item_sums(adjacency, all_users_t, sides, chips)
        came = [swap(part, "row", rows) for part in away]
        user_parts = user_sums(adjacency, all_items)
        item_parts = item_add([kept, *came])
        item_parts = exchange(item_parts, "row", chips, sides)
        user_parts = exchange(user_parts, "col", cols)
        items = item_update(n, item_parts, items, weight_sum, weight_product)
        users, users_t = user_update(n, user_parts, users, weight_sum, weight_product)
    return (users, items[None])


def solution(mesh):
    placed = (
        P(("row", "col"), None),
        P(("row", "col")),
        P(("row", "col")),
        P(("row", "col")),
        P(),
        P(),
        P("row", "col"),
        P("row", "col"),
        P("row", "col"),
        P(),
        P(),
    )
    return jax.shard_map(
        per_device,
        mesh=mesh,
        in_specs=placed,
        out_specs=(P(("row", "col"), None), P("col", "row", None)),
        check_vma=False,
    )
```

```python
import functools

import jax
import jax.numpy as jnp
from jax import lax
from jax.experimental import pallas as pl
from jax.experimental.pallas import tpu as pltpu
from jax.sharding import PartitionSpec as P


TILE = 128
LANES = 128
CODE_ROWS = 8
GROUP = 8
F32 = jnp.float32
BF16 = jnp.bfloat16
NT = (((1,), (1,)), ((), ()))


def power_of_two(n):
    return n & (n - 1) == 0


def peer_to(i, k, n):
    return i ^ k if power_of_two(n) else (i + k) % n


def vmem_spec():
    return pl.BlockSpec(memory_space=pltpu.VMEM)


def params():
    return pltpu.CompilerParams(vmem_limit_bytes=24 * 2**20)


def whole_vmem():
    return pltpu.CompilerParams(vmem_limit_bytes=67_043_328)


def no_room():
    return pltpu.CompilerParams(vmem_limit_bytes=52 * 2**20)


def chunks_of(capacity, features):
    chunks, base, row = [], 0, 0
    size = LANES // 2
    while base < capacity:
        while size > max(8, capacity - base):
            size //= 2
        height = features * size // LANES
        chunks.append((base, size, row, height))
        base += size
        row += height
    return chunks, -(-row // CODE_ROWS) * CODE_ROWS


def turned(block, shift):
    shift = shift % LANES
    return block if shift == 0 else pltpu.roll(block, shift, 1)


def packed(placed, codes, chunks, code_row, shares):
    blocks, code_rows, height = [], jnp.zeros((CODE_ROWS, LANES), F32), 0
    code = lax.broadcasted_iota(jnp.int32, (CODE_ROWS, LANES), 0)
    for n, (_, size, _, rows) in enumerate(chunks):
        lanes = slice(n * LANES, (n + 1) * LANES)
        block = None
        for q in range(LANES // size):
            piece = turned(placed[q * rows : (q + 1) * rows, lanes], q * size)
            block = piece if block is None else jnp.where(shares[n] == q, piece, block)
        blocks.append(block)
        height += rows
        low = codes[0:1, lanes]
        high = turned(codes[:, lanes], size)[1:2]
        both = jnp.where(shares[n] == 0, low, jnp.where(shares[n] == 1, high, 0.0))
        code_rows = jnp.where(code == n, both, code_rows)
    if height < code_row:
        blocks.append(jnp.zeros((code_row - height, LANES), F32))
    return jnp.concatenate([*blocks, code_rows], axis=0)


def unpacked(recv_ref, first, count, features, capacity):
    chunks, code_row = chunks_of(capacity, features)
    lane = lax.broadcasted_iota(jnp.int32, (1, LANES), 1)
    out = []
    for n, (_, size, row, rows) in enumerate(chunks):
        parts = LANES // size
        share = lane // size
        for start in range(first, first + count, parts):

            def merged(q, lo, hi):
                block = None
                for s in range(parts):
                    piece = recv_ref[start + s, lo:hi].astype(F32)
                    here = share == (q + s) % parts
                    block = piece if block is None else jnp.where(here, piece, block)
                return turned(block, -q * size)

            values = jnp.concatenate(
                [merged(q, row, row + rows) for q in range(parts)], axis=0
            )
            low, high = (
                merged(q, code_row, code_row + CODE_ROWS)[n : n + 1] for q in range(2)
            )
            out.append((values, low, high))
    return [jnp.concatenate(part, axis=1) for part in zip(*out, strict=True)]


def dispatch_kernel(devices, capacity, me_ref, *refs):
    sources, out_ref, (raw_ref, dest_ref, slot_ref, wide_ref, held), (sems, out_sems) = (
        refs[:4],
        refs[4],
        refs[5:10],
        refs[10:],
    )
    copies = [
        pltpu.make_async_copy(source, ref, sems.at[n])
        for n, (source, ref) in enumerate(
            zip(sources, (raw_ref, dest_ref, slot_ref, wide_ref), strict=True)
        )
    ]
    for copy in copies:
        copy.start()
    copies[1].wait()
    features, rows = raw_ref.shape
    chunks = rows // LANES
    dest = dest_ref[...]
    hot = (lax.broadcasted_iota(jnp.int32, (devices, rows), 0) == dest).astype(F32)
    hot_bf = hot.astype(BF16)
    before = lax.broadcasted_iota(jnp.int32, (LANES, 2 * LANES), 0)
    column = lax.broadcasted_iota(jnp.int32, (LANES, 2 * LANES), 1)
    prefix = ((before < column) | (column >= LANES)).astype(F32).astype(BF16)
    base = jnp.zeros((devices, LANES), F32)
    ranks = []
    for chunk in range(chunks):
        lanes = slice(chunk * LANES, (chunk + 1) * LANES)
        counted = jnp.dot(hot_bf[:, lanes], prefix, preferred_element_type=F32)
        ranks.append(
            jnp.sum((counted[:, :LANES] + base) * hot[:, lanes], axis=0, keepdims=True)
        )
        base = base + counted[:, LANES:]
    rank = jnp.concatenate(ranks, axis=1)
    plan, code_row = chunks_of(capacity, features)
    lane = lax.broadcasted_iota(jnp.int32, (1, LANES), 1)
    line = lax.broadcasted_iota(jnp.int32, (LANES, 1), 0)
    shares, places = [], []
    for first, size, _, _ in plan:
        parts = LANES // size
        turn = me_ref[0] % parts
        shares.append((lane // size + parts - turn) % parts)
        slot_of = line - turn * size
        inside = (slot_of >= 0) & (slot_of < size)
        wanted = jnp.where(inside, slot_of + first, -1).astype(F32)
        places.append((wanted == rank).astype(F32).astype(BF16))
    place = jnp.concatenate(places, axis=0)
    for copy in (copies[0], copies[2], copies[3]):
        copy.wait()
    slot = slot_ref[...]
    code = lax.broadcasted_iota(jnp.int32, (2 * CODE_ROWS, rows), 0)
    codes = jnp.where(
        code == 0,
        slot % 256,
        jnp.where(code == 1, slot // 256 * 2 + wide_ref[...], 0),
    )
    ext = jnp.concatenate([raw_ref[...], codes.astype(F32).astype(BF16)], axis=0)
    height = ext.shape[0]
    writes = []
    for n, first in enumerate(range(0, devices, GROUP)):
        masked = jnp.concatenate(
            [ext * hot_bf[d : d + 1, :] for d in range(first, first + GROUP)], axis=0
        )
        placed = lax.dot_general(masked, place, NT, preferred_element_type=F32)
        for d in range(GROUP):
            mine = placed[d * height : (d + 1) * height]
            held[first + d] = packed(
                mine[:features],
                mine[features : features + CODE_ROWS],
                plan,
                code_row,
                shares,
            ).astype(BF16)
        writes.append(
            pltpu.make_async_copy(
                held.at[pl.ds(first, GROUP)], out_ref.at[pl.ds(first, GROUP)], out_sems.at[n]
            )
        )
        writes[-1].start()
    for write in writes:
        write.wait()


def dispatch(me, raw, dest, slot, wide, devices, capacity):
    features, rows = raw.shape
    shape = (devices, chunks_of(capacity, features)[1] + CODE_ROWS, LANES)
    return pl.pallas_call(
        functools.partial(dispatch_kernel, devices, capacity),
        out_shape=jax.ShapeDtypeStruct(shape, BF16),
        in_specs=[pl.BlockSpec(memory_space=pltpu.SMEM)]
        + [pl.BlockSpec(memory_space=pltpu.HBM)] * 4,
        out_specs=pl.BlockSpec(memory_space=pltpu.HBM),
        scratch_shapes=[
            pltpu.VMEM(raw.shape, raw.dtype),
            *[pltpu.VMEM((1, rows), jnp.int32) for _ in range(3)],
            pltpu.VMEM(shape, BF16),
            pltpu.SemaphoreType.DMA((4,)),
            pltpu.SemaphoreType.DMA((devices // GROUP,)),
        ],
        compiler_params=whole_vmem(),
        name="dispatch",
    )(me, raw, dest, slot, wide)


def segment_kernel(capacity, upd, cols, recv_ref, proj_narrow_ref, proj_wide_ref, *refs):
    adj_refs, (user_ref, user_t_ref, item_ref) = refs[:cols], refs[cols : cols + 3]
    held_refs, sems = refs[cols + 3 : -1], refs[-1]
    copies = [
        pltpu.make_async_copy(adj_ref, held_ref, sems.at[k])
        for k, (adj_ref, held_ref) in enumerate(zip(adj_refs, held_refs, strict=True))
    ]
    for copy in copies:
        copy.start()
    devices = recv_ref.shape[0]
    narrow, features = proj_narrow_ref.shape[0], proj_wide_ref.shape[0]
    nodes = user_ref.shape[0] + item_ref.shape[0]
    total = jnp.zeros((nodes, features + narrow), F32)
    count = max(GROUP, *[LANES // chunk[1] for chunk in chunks_of(capacity, features)[0]])
    for first in range(0, devices, count):
        rows, low, high = unpacked(recv_ref, first, count, features, capacity)
        rows = rows.astype(BF16)
        high = high.astype(jnp.int32)
        node = low.astype(jnp.int32) + (high >> 1) * 256
        wide = (high & 1).astype(F32).astype(BF16)
        values = jnp.concatenate([rows * wide, rows[:narrow] * (1 - wide)], axis=0)
        hot = (
            lax.broadcasted_iota(jnp.int32, (nodes, node.shape[1]), 0) == node
        ).astype(F32).astype(BF16)
        total = total + lax.dot_general(hot, values, NT, preferred_element_type=F32)
    weights = jnp.concatenate([proj_wide_ref[...], proj_narrow_ref[...]], axis=0)
    initial = jnp.zeros((nodes, weights.shape[1]), F32)
    rest = total
    for _ in range(3):
        part = rest.astype(BF16)
        initial = initial + jnp.dot(part, weights, preferred_element_type=F32)
        rest = rest - part.astype(F32)
    users = initial[:upd]
    items = initial[upd:].astype(BF16)
    user_ref[...] = users.astype(BF16)
    user_t_ref[...] = users.T.astype(BF16)
    item_ref[...] = items
    for copy in copies:
        copy.wait()


def segment(recv, proj_narrow, proj_wide, adjacency, upd, ipd, capacity):
    cols = len(adjacency)
    d = proj_wide.shape[1]
    return pl.pallas_call(
        functools.partial(segment_kernel, capacity, upd, cols),
        out_shape=(
            jax.ShapeDtypeStruct((upd, d), BF16),
            jax.ShapeDtypeStruct((d, upd), BF16),
            jax.ShapeDtypeStruct((ipd, d), BF16),
            *[jax.ShapeDtypeStruct(block.shape, BF16) for block in adjacency],
        ),
        in_specs=[vmem_spec()] * 3 + [pl.BlockSpec(memory_space=pltpu.HBM)] * cols,
        out_specs=(vmem_spec(),) * (3 + cols),
        scratch_shapes=[pltpu.SemaphoreType.DMA((cols,))],
        compiler_params=params(),
        name="segment",
    )(
        recv,
        proj_narrow,
        proj_wide,
        *[pltpu.with_memory_space_constraint(block, pltpu.HBM) for block in adjacency],
    )


def dequantize_kernel(shape, me_ref, mask_ref, scale_ref, values_ref, *refs):
    out_refs, (held, sems) = refs[:-2], refs[-2:]
    sides, chips, cols = shape
    upd, n = out_refs[0].shape
    ipd = n // (sides * chips)
    row_here, col_here = me_ref[0] // cols, me_ref[0] % cols
    chip, side_here = row_here // sides, row_here % sides
    blocks = [peer_to(col_here, k, cols) for k in range(cols)]
    lines = [
        peer_to(chip, k, chips) * sides + (side_here + side) % sides
        for side in range(sides)
        for k in range(chips)
    ]
    copies = []
    for k, block in enumerate(blocks):
        start = pl.multiple_of(block * upd, upd)
        for at, line in enumerate(lines):
            first = pl.multiple_of(line * ipd, ipd)
            copies.append(
                pltpu.make_async_copy(
                    values_ref.at[pl.ds(start, upd), pl.ds(first, ipd)],
                    held.at[k, :, pl.ds(at * ipd, ipd)],
                    sems.at[k, at],
                )
            )
            copies[-1].start()
    for k, (block, out_ref) in enumerate(zip(blocks, out_refs, strict=True)):
        for at, line in enumerate(lines):
            copies[k * len(lines) + at].wait()
            for i in range(upd // TILE):
                row = block * (upd // TILE) + i
                here = slice(i * TILE, (i + 1) * TILE)
                for j in range(ipd // TILE):
                    column = line * (ipd // TILE) + j
                    lanes = slice(at * ipd + j * TILE, at * ipd + (j + 1) * TILE)
                    factor = mask_ref[row, column].astype(F32) * scale_ref[row, column]
                    out_ref[here, lanes] = (
                        held[k, here, lanes].astype(F32) * factor
                    ).astype(BF16)


def dequantize(me, values, mask, scale, shape):
    m, n = values.shape
    sides, chips, cols = shape
    smem = pl.BlockSpec(memory_space=pltpu.SMEM)
    return pl.pallas_call(
        functools.partial(dequantize_kernel, shape),
        out_shape=(jax.ShapeDtypeStruct((m // cols, n), BF16),) * cols,
        in_specs=[smem, smem, smem, pl.BlockSpec(memory_space=pltpu.HBM)],
        out_specs=(vmem_spec(),) * cols,
        scratch_shapes=[
            pltpu.VMEM((cols, m // cols, n), BF16),
            pltpu.SemaphoreType.DMA((cols, sides * chips)),
        ],
        compiler_params=no_room(),
        cost_estimate=pl.CostEstimate(flops=m * n, bytes_accessed=4 * m * n, transcendentals=0),
        name="dequantize",
    )(me, mask, scale, values)


def from_order(n):
    return [k if power_of_two(n) else (n - k) % n for k in range(n)]


def user_sum_kernel(cols, *refs):
    adj_refs, items_refs, out_refs = refs[:cols], refs[cols:-cols], refs[-cols:]
    items = jnp.concatenate([ref[...] for ref in items_refs], axis=0)
    for adj_ref, out_ref in zip(adj_refs, out_refs, strict=True):
        out_ref[...] = jnp.dot(adj_ref[...], items, preferred_element_type=F32).astype(BF16)


def user_sums(adjacency, items):
    cols = len(adjacency)
    upd, n = adjacency[0].shape
    d = items[0].shape[1]
    return pl.pallas_call(
        functools.partial(user_sum_kernel, cols),
        out_shape=(jax.ShapeDtypeStruct((upd, d), BF16),) * cols,
        in_specs=[vmem_spec()] * (cols + len(items)),
        out_specs=(vmem_spec(),) * cols,
        compiler_params=params(),
        cost_estimate=pl.CostEstimate(
            flops=2 * cols * upd * n * d, bytes_accessed=2 * cols * upd * n, transcendentals=0
        ),
        name="user_sums",
    )(*adjacency, *items)


def item_sum_kernel(cols, *refs):
    adj_refs, users_refs, out_refs = refs[:cols], refs[cols : 2 * cols], refs[2 * cols :]
    order = from_order(cols)
    users = [ref[...] for ref in users_refs]
    at = 0
    for out_ref in reversed(out_refs):
        for r in range(out_ref.shape[0]):
            ipd = out_ref.shape[2]
            lanes = slice(at * ipd, (at + 1) * ipd)
            total = None
            for k in range(cols):
                part = jnp.dot(
                    users[k], adj_refs[order[k]][:, lanes], preferred_element_type=F32
                )
                total = part if total is None else total + part
            out_ref[r] = total.astype(out_ref.dtype)
            at += 1


def item_sums(adjacency, users_t, sides, chips):
    cols = len(adjacency)
    upd, n = adjacency[0].shape
    d = users_t[0].shape[0]
    block = (chips, d, n // (sides * chips))
    outs = [jax.ShapeDtypeStruct(block, BF16)] * (sides - 1)
    return pl.pallas_call(
        functools.partial(item_sum_kernel, cols),
        out_shape=[*outs, jax.ShapeDtypeStruct(block, F32)],
        in_specs=[vmem_spec()] * (2 * cols),
        out_specs=[vmem_spec()] * sides,
        compiler_params=params(),
        cost_estimate=pl.CostEstimate(
            flops=2 * cols * upd * n * d, bytes_accessed=2 * cols * upd * n, transcendentals=0
        ),
        name="item_sums",
    )(*adjacency, *users_t)


def item_add_kernel(chips, *refs):
    parts, outs = refs[:-chips], refs[-chips:]
    for k, out_ref in enumerate(outs):
        total = parts[0][k]
        for part in parts[1:]:
            total = total + part[k].astype(F32)
        out_ref[...] = total.astype(BF16)


def item_add(parts):
    chips, d, ipd = parts[0].shape
    return pl.pallas_call(
        functools.partial(item_add_kernel, chips),
        out_shape=(jax.ShapeDtypeStruct((d, ipd), BF16),) * chips,
        in_specs=[vmem_spec()] * len(parts),
        out_specs=(vmem_spec(),) * chips,
        compiler_params=params(),
        name="item_add",
    )(*parts)


def updated(side, own, weight_sum, weight_product):
    own = own.astype(F32)
    linear = jnp.dot((side + own).astype(BF16), weight_sum, preferred_element_type=F32)
    linear = linear + jnp.dot(
        (side * own).astype(BF16), weight_product, preferred_element_type=F32
    )
    return jnp.where(linear > 0, linear, 0.2 * linear)


def user_update_kernel(layer, own_ref, sum_ref, product_ref, *refs):
    parts, outs = refs[:-2], refs[-2:]
    side = parts[0][...].astype(F32)
    for part in parts[1:]:
        side = side + part[...].astype(F32)
    new = updated(side, own_ref[...], sum_ref[layer], product_ref[layer])
    outs[0][...] = new.astype(BF16)
    outs[1][...] = new.T.astype(BF16)


def user_update(layer, parts, own, weight_sum, weight_product):
    upd, d = own.shape
    return pl.pallas_call(
        functools.partial(user_update_kernel, layer),
        out_shape=(jax.ShapeDtypeStruct((upd, d), BF16), jax.ShapeDtypeStruct((d, upd), BF16)),
        in_specs=[vmem_spec()] * (3 + len(parts)),
        out_specs=(vmem_spec(),) * 2,
        compiler_params=params(),
        name="user_update",
    )(own, weight_sum, weight_product, *parts)


def item_update_kernel(layer, own_ref, sum_ref, product_ref, *refs):
    parts, new_ref = refs[:-1], refs[-1]
    side = parts[0][...].astype(F32)
    for part in parts[1:]:
        side = side + part[...].astype(F32)
    new = updated(side.T, own_ref[...], sum_ref[layer], product_ref[layer])
    new_ref[...] = new.astype(BF16)


def item_update(layer, parts, own, weight_sum, weight_product):
    return pl.pallas_call(
        functools.partial(item_update_kernel, layer),
        out_shape=jax.ShapeDtypeStruct(own.shape, BF16),
        in_specs=[vmem_spec()] * (3 + len(parts)),
        out_specs=vmem_spec(),
        compiler_params=params(),
        name="item_update",
    )(own, weight_sum, weight_product, *parts)


def exchange(blocks, axis, n, inner=1):
    received = [blocks[0]]
    for k in range(1, n):
        pairs = [
            (i * inner + j, peer_to(i, k, n) * inner + j) for i in range(n) for j in range(inner)
        ]
        received.append(lax.ppermute(blocks[k], axis, pairs))
    return received


def swap(block, axis, n):
    return lax.ppermute(block, axis, [(i, i ^ 1) for i in range(n)])


def ordered(received):
    order = from_order(len(received))
    return [received[order.index(k)] for k in range(len(received))]


def per_device(
    raw_rows,
    raw_wide,
    raw_dest,
    raw_slot,
    proj_narrow,
    proj_wide,
    adj_values,
    tile_mask,
    tile_scale,
    weight_sum,
    weight_product,
):
    rows = lax.axis_size("row")
    cols = lax.axis_size("col")
    devices = rows * cols
    count = raw_rows.shape[0]
    capacity = 3 * count // devices
    upd = adj_values.shape[0] // cols
    ipd = adj_values.shape[1] // rows
    layers = weight_sum.shape[0]
    sides = 2 if rows % 2 == 0 else 1
    chips = rows // sides
    me = lax.axis_index(("row", "col")).astype(jnp.int32).reshape(1)
    send = dispatch(
        me,
        raw_rows.T,
        raw_dest.reshape(1, count),
        raw_slot.reshape(1, count),
        raw_wide.reshape(1, count),
        devices,
        capacity,
    )
    recv = lax.all_to_all(send, ("row", "col"), split_axis=0, concat_axis=0, tiled=True)
    adjacency = dequantize(
        me, adj_values, tile_mask, tile_scale, (sides, chips, cols)
    )
    users, users_t, items, *adjacency = segment(
        recv, proj_narrow, proj_wide, adjacency, upd, ipd, capacity
    )
    for n in range(layers):
        all_users_t = exchange([users_t] * cols, "col", cols)
        own_swapped = [swap(items, "row", rows)]
        all_items = ordered(exchange([items] * chips, "row", chips, sides))
        swapped = [swap(block, "row", rows) for block in all_items[1:]]
        if sides > 1:
            all_items = [*all_items, *own_swapped, *swapped]
        *away, kept = item_sums(adjacency, all_users_t, sides, chips)
        came = [swap(part, "row", rows) for part in away]
        user_parts = user_sums(adjacency, all_items)
        item_parts = item_add([kept, *came])
        item_parts = exchange(item_parts, "row", chips, sides)
        user_parts = exchange(user_parts, "col", cols)
        items = item_update(n, item_parts, items, weight_sum, weight_product)
        users, users_t = user_update(n, user_parts, users, weight_sum, weight_product)
    return (users, items[None])


def solution(mesh):
    placed = (
        P(("row", "col"), None),
        P(("row", "col")),
        P(("row", "col")),
        P(("row", "col")),
        P(),
        P(),
        P("row", "col"),
        P("row", "col"),
        P("row", "col"),
        P(),
        P(),
    )
    return jax.shard_map(
        per_device,
        mesh=mesh,
        in_specs=placed,
        out_specs=(P(("row", "col"), None), P("col", "row", None)),
        check_vma=False,
    )
```

```python
import functools

import jax
import jax.numpy as jnp
from jax import lax
from jax.experimental import pallas as pl
from jax.experimental.pallas import tpu as pltpu
from jax.sharding import PartitionSpec as P


TILE = 128
LANES = 128
CODE_ROWS = 8
GROUP = 8
KEPT = 1
F32 = jnp.float32
BF16 = jnp.bfloat16
NT = (((1,), (1,)), ((), ()))


def power_of_two(n):
    return n & (n - 1) == 0


def peer_to(i, k, n):
    return i ^ k if power_of_two(n) else (i + k) % n


def vmem_spec():
    return pl.BlockSpec(memory_space=pltpu.VMEM)


def params():
    return pltpu.CompilerParams(vmem_limit_bytes=24 * 2**20)


def whole_vmem():
    return pltpu.CompilerParams(vmem_limit_bytes=67_043_328)


def no_room():
    return pltpu.CompilerParams(vmem_limit_bytes=52 * 2**20)


def chunks_of(capacity, features):
    chunks, base, row = [], 0, 0
    size = LANES // 2
    while base < capacity:
        while size > max(8, capacity - base):
            size //= 2
        height = features * size // LANES
        chunks.append((base, size, row, height))
        base += size
        row += height
    return chunks, -(-row // CODE_ROWS) * CODE_ROWS


def turned(block, shift):
    shift = shift % LANES
    return block if shift == 0 else pltpu.roll(block, shift, 1)


def packed(placed, codes, chunks, code_row, shares):
    blocks, code_rows, height = [], jnp.zeros((CODE_ROWS, LANES), F32), 0
    code = lax.broadcasted_iota(jnp.int32, (CODE_ROWS, LANES), 0)
    for n, (_, size, _, rows) in enumerate(chunks):
        lanes = slice(n * LANES, (n + 1) * LANES)
        block = None
        for q in range(LANES // size):
            piece = turned(placed[q * rows : (q + 1) * rows, lanes], q * size)
            block = piece if block is None else jnp.where(shares[n] == q, piece, block)
        blocks.append(block)
        height += rows
        low = codes[0:1, lanes]
        high = turned(codes[:, lanes], size)[1:2]
        both = jnp.where(shares[n] == 0, low, jnp.where(shares[n] == 1, high, 0.0))
        code_rows = jnp.where(code == n, both, code_rows)
    if height < code_row:
        blocks.append(jnp.zeros((code_row - height, LANES), F32))
    return jnp.concatenate([*blocks, code_rows], axis=0)


def unpacked(recv_ref, first, count, features, capacity):
    chunks, code_row = chunks_of(capacity, features)
    lane = lax.broadcasted_iota(jnp.int32, (1, LANES), 1)
    out = []
    for n, (_, size, row, rows) in enumerate(chunks):
        parts = LANES // size
        share = lane // size
        for start in range(first, first + count, parts):

            def merged(q, lo, hi):
                block = None
                for s in range(parts):
                    piece = recv_ref[start + s, lo:hi].astype(F32)
                    here = share == (q + s) % parts
                    block = piece if block is None else jnp.where(here, piece, block)
                return turned(block, -q * size)

            values = jnp.concatenate(
                [merged(q, row, row + rows) for q in range(parts)], axis=0
            )
            low, high = (
                merged(q, code_row, code_row + CODE_ROWS)[n : n + 1] for q in range(2)
            )
            out.append((values, low, high))
    return [jnp.concatenate(part, axis=1) for part in zip(*out, strict=True)]


def dispatch_kernel(devices, capacity, me_ref, *refs):
    sources, out_ref, (raw_ref, dest_ref, slot_ref, wide_ref, held), (sems, out_sems) = (
        refs[:4],
        refs[4],
        refs[5:10],
        refs[10:],
    )
    copies = [
        pltpu.make_async_copy(source, ref, sems.at[n])
        for n, (source, ref) in enumerate(
            zip(sources, (raw_ref, dest_ref, slot_ref, wide_ref), strict=True)
        )
    ]
    for copy in copies:
        copy.start()
    copies[1].wait()
    features, rows = raw_ref.shape
    chunks = rows // LANES
    dest = dest_ref[...]
    hot = (lax.broadcasted_iota(jnp.int32, (devices, rows), 0) == dest).astype(F32)
    hot_bf = hot.astype(BF16)
    before = lax.broadcasted_iota(jnp.int32, (LANES, 2 * LANES), 0)
    column = lax.broadcasted_iota(jnp.int32, (LANES, 2 * LANES), 1)
    prefix = ((before < column) | (column >= LANES)).astype(F32).astype(BF16)
    base = jnp.zeros((devices, LANES), F32)
    ranks = []
    for chunk in range(chunks):
        lanes = slice(chunk * LANES, (chunk + 1) * LANES)
        counted = jnp.dot(hot_bf[:, lanes], prefix, preferred_element_type=F32)
        ranks.append(
            jnp.sum((counted[:, :LANES] + base) * hot[:, lanes], axis=0, keepdims=True)
        )
        base = base + counted[:, LANES:]
    rank = jnp.concatenate(ranks, axis=1)
    plan, code_row = chunks_of(capacity, features)
    lane = lax.broadcasted_iota(jnp.int32, (1, LANES), 1)
    line = lax.broadcasted_iota(jnp.int32, (LANES, 1), 0)
    shares, places = [], []
    for first, size, _, _ in plan:
        parts = LANES // size
        turn = me_ref[0] % parts
        shares.append((lane // size + parts - turn) % parts)
        slot_of = line - turn * size
        inside = (slot_of >= 0) & (slot_of < size)
        wanted = jnp.where(inside, slot_of + first, -1).astype(F32)
        places.append((wanted == rank).astype(F32).astype(BF16))
    place = jnp.concatenate(places, axis=0)
    for copy in (copies[0], copies[2], copies[3]):
        copy.wait()
    slot = slot_ref[...]
    code = lax.broadcasted_iota(jnp.int32, (2 * CODE_ROWS, rows), 0)
    codes = jnp.where(
        code == 0,
        slot % 256,
        jnp.where(code == 1, slot // 256 * 2 + wide_ref[...], 0),
    )
    ext = jnp.concatenate([raw_ref[...], codes.astype(F32).astype(BF16)], axis=0)
    height = ext.shape[0]
    writes = []
    for n, first in enumerate(range(0, devices, GROUP)):
        masked = jnp.concatenate(
            [ext * hot_bf[d : d + 1, :] for d in range(first, first + GROUP)], axis=0
        )
        placed = lax.dot_general(masked, place, NT, preferred_element_type=F32)
        for d in range(GROUP):
            mine = placed[d * height : (d + 1) * height]
            held[first + d] = packed(
                mine[:features],
                mine[features : features + CODE_ROWS],
                plan,
                code_row,
                shares,
            ).astype(BF16)
        writes.append(
            pltpu.make_async_copy(
                held.at[pl.ds(first, GROUP)], out_ref.at[pl.ds(first, GROUP)], out_sems.at[n]
            )
        )
        writes[-1].start()
    for write in writes:
        write.wait()


def dispatch(me, raw, dest, slot, wide, devices, capacity):
    features, rows = raw.shape
    shape = (devices, chunks_of(capacity, features)[1] + CODE_ROWS, LANES)
    return pl.pallas_call(
        functools.partial(dispatch_kernel, devices, capacity),
        out_shape=jax.ShapeDtypeStruct(shape, BF16),
        in_specs=[pl.BlockSpec(memory_space=pltpu.SMEM)]
        + [pl.BlockSpec(memory_space=pltpu.HBM)] * 4,
        out_specs=pl.BlockSpec(memory_space=pltpu.HBM),
        scratch_shapes=[
            pltpu.VMEM(raw.shape, raw.dtype),
            *[pltpu.VMEM((1, rows), jnp.int32) for _ in range(3)],
            pltpu.VMEM(shape, BF16),
            pltpu.SemaphoreType.DMA((4,)),
            pltpu.SemaphoreType.DMA((devices // GROUP,)),
        ],
        compiler_params=whole_vmem(),
        name="dispatch",
    )(me, raw, dest, slot, wide)


def segment_kernel(
    capacity, upd, moved, me_ref, recv_ref, proj_narrow_ref, proj_wide_ref, *refs
):
    adj_refs, outs = refs[:moved], refs[moved : moved + 3]
    held_refs, sems = refs[moved + 3 : -1], refs[-1]
    copies = [
        pltpu.make_async_copy(adj_ref, held_ref, sems.at[k])
        for k, (adj_ref, held_ref) in enumerate(zip(adj_refs, held_refs, strict=True))
    ]
    for copy in copies:
        copy.start()

    @pl.when(me_ref[0] >= 0)
    def _():
        initial_rows(capacity, upd, recv_ref, proj_narrow_ref, proj_wide_ref, *outs)

    for copy in copies:
        copy.wait()


def initial_rows(
    capacity, upd, recv_ref, proj_narrow_ref, proj_wide_ref, user_ref, user_t_ref, item_ref
):
    devices = recv_ref.shape[0]
    narrow, features = proj_narrow_ref.shape[0], proj_wide_ref.shape[0]
    nodes = user_ref.shape[0] + item_ref.shape[0]
    total = jnp.zeros((nodes, features + narrow), F32)
    count = max(GROUP, *[LANES // chunk[1] for chunk in chunks_of(capacity, features)[0]])
    for first in range(0, devices, count):
        rows, low, high = unpacked(recv_ref, first, count, features, capacity)
        rows = rows.astype(BF16)
        high = high.astype(jnp.int32)
        node = low.astype(jnp.int32) + (high >> 1) * 256
        wide = (high & 1).astype(F32).astype(BF16)
        values = jnp.concatenate([rows * wide, rows[:narrow] * (1 - wide)], axis=0)
        hot = (
            lax.broadcasted_iota(jnp.int32, (nodes, node.shape[1]), 0) == node
        ).astype(F32).astype(BF16)
        total = total + lax.dot_general(hot, values, NT, preferred_element_type=F32)
    weights = jnp.concatenate([proj_wide_ref[...], proj_narrow_ref[...]], axis=0)
    initial = jnp.zeros((nodes, weights.shape[1]), F32)
    rest = total
    for _ in range(3):
        part = rest.astype(BF16)
        initial = initial + jnp.dot(part, weights, preferred_element_type=F32)
        rest = rest - part.astype(F32)
    users = initial[:upd]
    items = initial[upd:].astype(BF16)
    user_ref[...] = users.astype(BF16)
    user_t_ref[...] = users.T.astype(BF16)
    item_ref[...] = items


def segment(me, recv, proj_narrow, proj_wide, adjacency, upd, ipd, capacity):
    cols = len(adjacency)
    d = proj_wide.shape[1]
    return pl.pallas_call(
        functools.partial(segment_kernel, capacity, upd, cols),
        out_shape=(
            jax.ShapeDtypeStruct((upd, d), BF16),
            jax.ShapeDtypeStruct((d, upd), BF16),
            jax.ShapeDtypeStruct((ipd, d), BF16),
            *[jax.ShapeDtypeStruct(block.shape, BF16) for block in adjacency],
        ),
        in_specs=[pl.BlockSpec(memory_space=pltpu.SMEM)]
        + [vmem_spec()] * 3
        + [pl.BlockSpec(memory_space=pltpu.HBM)] * cols,
        out_specs=(vmem_spec(),) * (3 + cols),
        scratch_shapes=[pltpu.SemaphoreType.DMA((cols,))],
        compiler_params=params(),
        name="segment",
    )(
        me,
        recv,
        proj_narrow,
        proj_wide,
        *[pltpu.with_memory_space_constraint(block, pltpu.HBM) for block in adjacency],
    )


def dequantize_kernel(shape, me_ref, mask_ref, scale_ref, values_ref, *refs):
    out_refs, (held, sems) = refs[:-2], refs[-2:]
    sides, chips, cols = shape
    upd, n = out_refs[0].shape
    ipd = n // (sides * chips)
    row_here, col_here = me_ref[0] // cols, me_ref[0] % cols
    chip, side_here = row_here // sides, row_here % sides
    blocks = [peer_to(col_here, k, cols) for k in range(cols)]
    lines = [
        peer_to(chip, k, chips) * sides + (side_here + side) % sides
        for side in range(sides)
        for k in range(chips)
    ]
    copies = []
    for k, block in enumerate(blocks):
        start = pl.multiple_of(block * upd, upd)
        for at, line in enumerate(lines):
            first = pl.multiple_of(line * ipd, ipd)
            copies.append(
                pltpu.make_async_copy(
                    values_ref.at[pl.ds(start, upd), pl.ds(first, ipd)],
                    held.at[k, :, pl.ds(at * ipd, ipd)],
                    sems.at[k, at],
                )
            )
            copies[-1].start()
    for k, (block, out_ref) in enumerate(zip(blocks, out_refs, strict=True)):
        for at, line in enumerate(lines):
            copies[k * len(lines) + at].wait()
            for i in range(upd // TILE):
                row = block * (upd // TILE) + i
                here = slice(i * TILE, (i + 1) * TILE)
                for j in range(ipd // TILE):
                    column = line * (ipd // TILE) + j
                    lanes = slice(at * ipd + j * TILE, at * ipd + (j + 1) * TILE)
                    factor = mask_ref[row, column].astype(F32) * scale_ref[row, column]
                    out_ref[here, lanes] = (
                        held[k, here, lanes].astype(F32) * factor
                    ).astype(BF16)


def dequantize(me, values, mask, scale, shape):
    m, n = values.shape
    sides, chips, cols = shape
    smem = pl.BlockSpec(memory_space=pltpu.SMEM)
    return pl.pallas_call(
        functools.partial(dequantize_kernel, shape),
        out_shape=(jax.ShapeDtypeStruct((m // cols, n), BF16),) * cols,
        in_specs=[smem, smem, smem, pl.BlockSpec(memory_space=pltpu.HBM)],
        out_specs=(vmem_spec(),) * cols,
        scratch_shapes=[
            pltpu.VMEM((cols, m // cols, n), BF16),
            pltpu.SemaphoreType.DMA((cols, sides * chips)),
        ],
        compiler_params=no_room(),
        cost_estimate=pl.CostEstimate(flops=m * n, bytes_accessed=4 * m * n, transcendentals=0),
        name="dequantize",
    )(me, mask, scale, values)


def from_order(n):
    return [k if power_of_two(n) else (n - k) % n for k in range(n)]


def user_sum_kernel(cols, *refs):
    adj_refs, items_refs, out_refs = refs[:cols], refs[cols:-cols], refs[-cols:]
    items = jnp.concatenate([ref[...] for ref in items_refs], axis=0)
    for adj_ref, out_ref in zip(adj_refs, out_refs, strict=True):
        out_ref[...] = jnp.dot(adj_ref[...], items, preferred_element_type=F32).astype(BF16)


def user_sums(adjacency, items):
    cols = len(adjacency)
    upd, n = adjacency[0].shape
    d = items[0].shape[1]
    return pl.pallas_call(
        functools.partial(user_sum_kernel, cols),
        out_shape=(jax.ShapeDtypeStruct((upd, d), BF16),) * cols,
        in_specs=[vmem_spec()] * (cols + len(items)),
        out_specs=(vmem_spec(),) * cols,
        compiler_params=params(),
        cost_estimate=pl.CostEstimate(
            flops=2 * cols * upd * n * d, bytes_accessed=2 * cols * upd * n, transcendentals=0
        ),
        name="user_sums",
    )(*adjacency, *items)


def item_sum_kernel(cols, *refs):
    adj_refs, users_refs, out_refs = refs[:cols], refs[cols : 2 * cols], refs[2 * cols :]
    order = from_order(cols)
    users = [ref[...] for ref in users_refs]
    at = 0
    for out_ref in reversed(out_refs):
        for r in range(out_ref.shape[0]):
            ipd = out_ref.shape[2]
            lanes = slice(at * ipd, (at + 1) * ipd)
            total = None
            for k in range(cols):
                part = jnp.dot(
                    users[k], adj_refs[order[k]][:, lanes], preferred_element_type=F32
                )
                total = part if total is None else total + part
            out_ref[r] = total.astype(out_ref.dtype)
            at += 1


def item_sums(adjacency, users_t, sides, chips):
    cols = len(adjacency)
    upd, n = adjacency[0].shape
    d = users_t[0].shape[0]
    block = (chips, d, n // (sides * chips))
    outs = [jax.ShapeDtypeStruct(block, BF16)] * (sides - 1)
    return pl.pallas_call(
        functools.partial(item_sum_kernel, cols),
        out_shape=[*outs, jax.ShapeDtypeStruct(block, F32)],
        in_specs=[vmem_spec()] * (2 * cols),
        out_specs=[vmem_spec()] * sides,
        compiler_params=params(),
        cost_estimate=pl.CostEstimate(
            flops=2 * cols * upd * n * d, bytes_accessed=2 * cols * upd * n, transcendentals=0
        ),
        name="item_sums",
    )(*adjacency, *users_t)


def item_add_kernel(chips, *refs):
    parts, outs = refs[:-chips], refs[-chips:]
    for k, out_ref in enumerate(outs):
        total = parts[0][k]
        for part in parts[1:]:
            total = total + part[k].astype(F32)
        out_ref[...] = total.astype(BF16)


def item_add(parts):
    chips, d, ipd = parts[0].shape
    return pl.pallas_call(
        functools.partial(item_add_kernel, chips),
        out_shape=(jax.ShapeDtypeStruct((d, ipd), BF16),) * chips,
        in_specs=[vmem_spec()] * len(parts),
        out_specs=(vmem_spec(),) * chips,
        compiler_params=params(),
        name="item_add",
    )(*parts)


def updated(side, own, weight_sum, weight_product):
    own = own.astype(F32)
    linear = jnp.dot((side + own).astype(BF16), weight_sum, preferred_element_type=F32)
    linear = linear + jnp.dot(
        (side * own).astype(BF16), weight_product, preferred_element_type=F32
    )
    return jnp.where(linear > 0, linear, 0.2 * linear)


def user_update_kernel(layer, own_ref, sum_ref, product_ref, *refs):
    parts, outs = refs[:-2], refs[-2:]
    side = parts[0][...].astype(F32)
    for part in parts[1:]:
        side = side + part[...].astype(F32)
    new = updated(side, own_ref[...], sum_ref[layer], product_ref[layer])
    outs[0][...] = new.astype(BF16)
    outs[1][...] = new.T.astype(BF16)


def user_update(layer, parts, own, weight_sum, weight_product):
    upd, d = own.shape
    return pl.pallas_call(
        functools.partial(user_update_kernel, layer),
        out_shape=(jax.ShapeDtypeStruct((upd, d), BF16), jax.ShapeDtypeStruct((d, upd), BF16)),
        in_specs=[vmem_spec()] * (3 + len(parts)),
        out_specs=(vmem_spec(),) * 2,
        compiler_params=params(),
        name="user_update",
    )(own, weight_sum, weight_product, *parts)


def item_update_kernel(layer, own_ref, sum_ref, product_ref, *refs):
    parts, new_ref = refs[:-1], refs[-1]
    side = parts[0][...].astype(F32)
    for part in parts[1:]:
        side = side + part[...].astype(F32)
    new = updated(side.T, own_ref[...], sum_ref[layer], product_ref[layer])
    new_ref[...] = new.astype(BF16)


def item_update(layer, parts, own, weight_sum, weight_product):
    return pl.pallas_call(
        functools.partial(item_update_kernel, layer),
        out_shape=jax.ShapeDtypeStruct(own.shape, BF16),
        in_specs=[vmem_spec()] * (3 + len(parts)),
        out_specs=vmem_spec(),
        compiler_params=params(),
        name="item_update",
    )(own, weight_sum, weight_product, *parts)


def exchange(blocks, axis, n, inner=1):
    received = [blocks[0]]
    for k in range(1, n):
        pairs = [
            (i * inner + j, peer_to(i, k, n) * inner + j) for i in range(n) for j in range(inner)
        ]
        received.append(lax.ppermute(blocks[k], axis, pairs))
    return received


def swap(block, axis, n):
    return lax.ppermute(block, axis, [(i, i ^ 1) for i in range(n)])


def ordered(received):
    order = from_order(len(received))
    return [received[order.index(k)] for k in range(len(received))]


def per_device(
    raw_rows,
    raw_wide,
    raw_dest,
    raw_slot,
    proj_narrow,
    proj_wide,
    adj_values,
    tile_mask,
    tile_scale,
    weight_sum,
    weight_product,
):
    rows = lax.axis_size("row")
    cols = lax.axis_size("col")
    devices = rows * cols
    count = raw_rows.shape[0]
    capacity = 3 * count // devices
    upd = adj_values.shape[0] // cols
    ipd = adj_values.shape[1] // rows
    layers = weight_sum.shape[0]
    sides = 2 if rows % 2 == 0 else 1
    chips = rows // sides
    me = lax.axis_index(("row", "col")).astype(jnp.int32).reshape(1)
    send = dispatch(
        me,
        raw_rows.T,
        raw_dest.reshape(1, count),
        raw_slot.reshape(1, count),
        raw_wide.reshape(1, count),
        devices,
        capacity,
    )
    recv = lax.all_to_all(send, ("row", "col"), split_axis=0, concat_axis=0, tiled=True)
    adjacency = dequantize(
        me, adj_values, tile_mask, tile_scale, (sides, chips, cols)
    )
    users, users_t, items, *moved = segment(
        me, recv, proj_narrow, proj_wide, adjacency[KEPT:], upd, ipd, capacity
    )
    adjacency = [*adjacency[:KEPT], *moved]
    for n in range(layers):
        all_users_t = exchange([users_t] * cols, "col", cols)
        own_swapped = [swap(items, "row", rows)]
        all_items = ordered(exchange([items] * chips, "row", chips, sides))
        swapped = [swap(block, "row", rows) for block in all_items[1:]]
        if sides > 1:
            all_items = [*all_items, *own_swapped, *swapped]
        *away, kept = item_sums(adjacency, all_users_t, sides, chips)
        came = [swap(part, "row", rows) for part in away]
        user_parts = user_sums(adjacency, all_items)
        item_parts = item_add([kept, *came])
        item_parts = exchange(item_parts, "row", chips, sides)
        user_parts = exchange(user_parts, "col", cols)
        items = item_update(n, item_parts, items, weight_sum, weight_product)
        users, users_t = user_update(n, user_parts, users, weight_sum, weight_product)
    return (users, items[None])


def solution(mesh):
    placed = (
        P(("row", "col"), None),
        P(("row", "col")),
        P(("row", "col")),
        P(("row", "col")),
        P(),
        P(),
        P("row", "col"),
        P("row", "col"),
        P("row", "col"),
        P(),
        P(),
    )
    return jax.shard_map(
        per_device,
        mesh=mesh,
        in_specs=placed,
        out_specs=(P(("row", "col"), None), P("col", "row", None)),
        check_vma=False,
    )
```

```python
import functools

import jax
import jax.numpy as jnp
from jax import lax
from jax.experimental import pallas as pl
from jax.experimental.pallas import tpu as pltpu
from jax.sharding import PartitionSpec as P


TILE = 128
LANES = 128
CODE_ROWS = 8
GROUP = 8
KEPT = 1
F32 = jnp.float32
BF16 = jnp.bfloat16
NT = (((1,), (1,)), ((), ()))


def power_of_two(n):
    return n & (n - 1) == 0


def peer_to(i, k, n):
    return i ^ k if power_of_two(n) else (i + k) % n


def vmem_spec():
    return pl.BlockSpec(memory_space=pltpu.VMEM)


def params():
    return pltpu.CompilerParams(vmem_limit_bytes=24 * 2**20)


def whole_vmem():
    return pltpu.CompilerParams(vmem_limit_bytes=67_043_328)


def no_room():
    return pltpu.CompilerParams(vmem_limit_bytes=52 * 2**20)


def chunks_of(capacity, features):
    chunks, base, row = [], 0, 0
    size = LANES // 2
    while base < capacity:
        while size > max(8, capacity - base):
            size //= 2
        height = features * size // LANES
        chunks.append((base, size, row, height))
        base += size
        row += height
    return chunks, -(-row // CODE_ROWS) * CODE_ROWS


def turned(block, shift):
    shift = shift % LANES
    return block if shift == 0 else pltpu.roll(block, shift, 1)


def packed(placed, codes, chunks, code_row, shares):
    blocks, code_rows, height = [], jnp.zeros((CODE_ROWS, LANES), F32), 0
    code = lax.broadcasted_iota(jnp.int32, (CODE_ROWS, LANES), 0)
    for n, (_, size, _, rows) in enumerate(chunks):
        lanes = slice(n * LANES, (n + 1) * LANES)
        block = None
        for q in range(LANES // size):
            piece = turned(placed[q * rows : (q + 1) * rows, lanes], q * size)
            block = piece if block is None else jnp.where(shares[n] == q, piece, block)
        blocks.append(block)
        height += rows
        low = codes[0:1, lanes]
        high = turned(codes[:, lanes], size)[1:2]
        both = jnp.where(shares[n] == 0, low, jnp.where(shares[n] == 1, high, 0.0))
        code_rows = jnp.where(code == n, both, code_rows)
    if height < code_row:
        blocks.append(jnp.zeros((code_row - height, LANES), F32))
    return jnp.concatenate([*blocks, code_rows], axis=0)


def unpacked(recv_ref, first, count, features, capacity):
    chunks, code_row = chunks_of(capacity, features)
    lane = lax.broadcasted_iota(jnp.int32, (1, LANES), 1)
    out = []
    for n, (_, size, row, rows) in enumerate(chunks):
        parts = LANES // size
        share = lane // size
        for start in range(first, first + count, parts):

            def merged(q, lo, hi):
                block = None
                for s in range(parts):
                    piece = recv_ref[start + s, lo:hi].astype(F32)
                    here = share == (q + s) % parts
                    block = piece if block is None else jnp.where(here, piece, block)
                return turned(block, -q * size)

            values = jnp.concatenate(
                [merged(q, row, row + rows) for q in range(parts)], axis=0
            )
            low, high = (
                merged(q, code_row, code_row + CODE_ROWS)[n : n + 1] for q in range(2)
            )
            out.append((values, low, high))
    return [jnp.concatenate(part, axis=1) for part in zip(*out, strict=True)]


def dispatch_kernel(devices, capacity, me_ref, *refs):
    sources, out_ref, (raw_ref, dest_ref, slot_ref, wide_ref, held), (sems, out_sems) = (
        refs[:4],
        refs[4],
        refs[5:10],
        refs[10:],
    )
    copies = [
        pltpu.make_async_copy(source, ref, sems.at[n])
        for n, (source, ref) in enumerate(
            zip(sources, (raw_ref, dest_ref, slot_ref, wide_ref), strict=True)
        )
    ]
    for copy in copies:
        copy.start()
    copies[1].wait()
    features, rows = raw_ref.shape
    chunks = rows // LANES
    dest = dest_ref[...]
    hot = (lax.broadcasted_iota(jnp.int32, (devices, rows), 0) == dest).astype(F32)
    hot_bf = hot.astype(BF16)
    before = lax.broadcasted_iota(jnp.int32, (LANES, 2 * LANES), 0)
    column = lax.broadcasted_iota(jnp.int32, (LANES, 2 * LANES), 1)
    prefix = ((before < column) | (column >= LANES)).astype(F32).astype(BF16)
    base = jnp.zeros((devices, LANES), F32)
    ranks = []
    for chunk in range(chunks):
        lanes = slice(chunk * LANES, (chunk + 1) * LANES)
        counted = jnp.dot(hot_bf[:, lanes], prefix, preferred_element_type=F32)
        ranks.append(
            jnp.sum((counted[:, :LANES] + base) * hot[:, lanes], axis=0, keepdims=True)
        )
        base = base + counted[:, LANES:]
    rank = jnp.concatenate(ranks, axis=1)
    plan, code_row = chunks_of(capacity, features)
    lane = lax.broadcasted_iota(jnp.int32, (1, LANES), 1)
    line = lax.broadcasted_iota(jnp.int32, (LANES, 1), 0)
    shares, places = [], []
    for first, size, _, _ in plan:
        parts = LANES // size
        turn = me_ref[0] % parts
        shares.append((lane // size + parts - turn) % parts)
        slot_of = line - turn * size
        inside = (slot_of >= 0) & (slot_of < size)
        wanted = jnp.where(inside, slot_of + first, -1).astype(F32)
        places.append((wanted == rank).astype(F32).astype(BF16))
    place = jnp.concatenate(places, axis=0)
    for copy in (copies[0], copies[2], copies[3]):
        copy.wait()
    slot = slot_ref[...]
    code = lax.broadcasted_iota(jnp.int32, (2 * CODE_ROWS, rows), 0)
    codes = jnp.where(
        code == 0,
        slot % 256,
        jnp.where(code == 1, slot // 256 * 2 + wide_ref[...], 0),
    )
    ext = jnp.concatenate([raw_ref[...], codes.astype(F32).astype(BF16)], axis=0)
    height = ext.shape[0]
    writes = []
    for n, first in enumerate(range(0, devices, GROUP)):
        masked = jnp.concatenate(
            [ext * hot_bf[d : d + 1, :] for d in range(first, first + GROUP)], axis=0
        )
        placed = lax.dot_general(masked, place, NT, preferred_element_type=F32)
        for d in range(GROUP):
            mine = placed[d * height : (d + 1) * height]
            held[first + d] = packed(
                mine[:features],
                mine[features : features + CODE_ROWS],
                plan,
                code_row,
                shares,
            ).astype(BF16)
        writes.append(
            pltpu.make_async_copy(
                held.at[pl.ds(first, GROUP)], out_ref.at[pl.ds(first, GROUP)], out_sems.at[n]
            )
        )
        writes[-1].start()
    for write in writes:
        write.wait()


def dispatch(me, raw, dest, slot, wide, devices, capacity):
    features, rows = raw.shape
    shape = (devices, chunks_of(capacity, features)[1] + CODE_ROWS, LANES)
    return pl.pallas_call(
        functools.partial(dispatch_kernel, devices, capacity),
        out_shape=jax.ShapeDtypeStruct(shape, BF16),
        in_specs=[pl.BlockSpec(memory_space=pltpu.SMEM)]
        + [pl.BlockSpec(memory_space=pltpu.HBM)] * 4,
        out_specs=pl.BlockSpec(memory_space=pltpu.HBM),
        scratch_shapes=[
            pltpu.VMEM(raw.shape, raw.dtype),
            *[pltpu.VMEM((1, rows), jnp.int32) for _ in range(3)],
            pltpu.VMEM(shape, BF16),
            pltpu.SemaphoreType.DMA((4,)),
            pltpu.SemaphoreType.DMA((devices // GROUP,)),
        ],
        compiler_params=whole_vmem(),
        name="dispatch",
    )(me, raw, dest, slot, wide)


def segment_kernel(
    capacity, upd, moved, me_ref, recv_ref, proj_narrow_ref, proj_wide_ref, *refs
):
    adj_refs, outs = refs[:moved], refs[moved : moved + 3]
    held_refs, sems = refs[moved + 3 : -1], refs[-1]
    copies = [
        pltpu.make_async_copy(adj_ref, held_ref, sems.at[k])
        for k, (adj_ref, held_ref) in enumerate(zip(adj_refs, held_refs, strict=True))
    ]
    for copy in copies:
        copy.start()

    @pl.when(me_ref[0] >= 0)
    def _():
        initial_rows(capacity, upd, recv_ref, proj_narrow_ref, proj_wide_ref, *outs)

    for copy in copies:
        copy.wait()


def initial_rows(
    capacity, upd, recv_ref, proj_narrow_ref, proj_wide_ref, user_ref, user_t_ref, item_ref
):
    devices = recv_ref.shape[0]
    narrow, features = proj_narrow_ref.shape[0], proj_wide_ref.shape[0]
    nodes = user_ref.shape[0] + item_ref.shape[0]
    total = jnp.zeros((nodes, features + narrow), F32)
    count = max(GROUP, *[LANES // chunk[1] for chunk in chunks_of(capacity, features)[0]])
    for first in range(0, devices, count):
        rows, low, high = unpacked(recv_ref, first, count, features, capacity)
        rows = rows.astype(BF16)
        high = high.astype(jnp.int32)
        node = low.astype(jnp.int32) + (high >> 1) * 256
        wide = (high & 1).astype(F32).astype(BF16)
        values = jnp.concatenate([rows * wide, rows[:narrow] * (1 - wide)], axis=0)
        hot = (
            lax.broadcasted_iota(jnp.int32, (nodes, node.shape[1]), 0) == node
        ).astype(F32).astype(BF16)
        total = total + lax.dot_general(hot, values, NT, preferred_element_type=F32)
    weights = jnp.concatenate([proj_wide_ref[...], proj_narrow_ref[...]], axis=0)
    initial = jnp.zeros((nodes, weights.shape[1]), F32)
    rest = total
    for _ in range(3):
        part = rest.astype(BF16)
        initial = initial + jnp.dot(part, weights, preferred_element_type=F32)
        rest = rest - part.astype(F32)
    users = initial[:upd]
    items = initial[upd:].astype(BF16)
    user_ref[...] = users.astype(BF16)
    user_t_ref[...] = users.T.astype(BF16)
    item_ref[...] = items


def segment(me, recv, proj_narrow, proj_wide, adjacency, upd, ipd, capacity):
    cols = len(adjacency)
    d = proj_wide.shape[1]
    return pl.pallas_call(
        functools.partial(segment_kernel, capacity, upd, cols),
        out_shape=(
            jax.ShapeDtypeStruct((upd, d), BF16),
            jax.ShapeDtypeStruct((d, upd), BF16),
            jax.ShapeDtypeStruct((ipd, d), BF16),
            *[jax.ShapeDtypeStruct(block.shape, BF16) for block in adjacency],
        ),
        in_specs=[pl.BlockSpec(memory_space=pltpu.SMEM)]
        + [vmem_spec()] * 3
        + [pl.BlockSpec(memory_space=pltpu.HBM)] * cols,
        out_specs=(vmem_spec(),) * (3 + cols),
        scratch_shapes=[pltpu.SemaphoreType.DMA((cols,))],
        compiler_params=params(),
        name="segment",
    )(
        me,
        recv,
        proj_narrow,
        proj_wide,
        *[pltpu.with_memory_space_constraint(block, pltpu.HBM) for block in adjacency],
    )


def dequantize_kernel(shape, me_ref, mask_ref, scale_ref, values_ref, *refs):
    out_refs, (held, sems) = refs[:-2], refs[-2:]
    sides, chips, cols = shape
    upd, n = out_refs[0].shape
    ipd = n // (sides * chips)
    row_here, col_here = me_ref[0] // cols, me_ref[0] % cols
    chip, side_here = row_here // sides, row_here % sides
    blocks = [peer_to(col_here, k, cols) for k in range(cols)]
    lines = [
        peer_to(chip, k, chips) * sides + (side_here + side) % sides
        for side in range(sides)
        for k in range(chips)
    ]
    copies = []
    for k, block in enumerate(blocks):
        start = pl.multiple_of(block * upd, upd)
        for at, line in enumerate(lines):
            first = pl.multiple_of(line * ipd, ipd)
            copies.append(
                pltpu.make_async_copy(
                    values_ref.at[pl.ds(start, upd), pl.ds(first, ipd)],
                    held.at[k, :, pl.ds(at * ipd, ipd)],
                    sems.at[k, at],
                )
            )
            copies[-1].start()
    for k, (block, out_ref) in enumerate(zip(blocks, out_refs, strict=True)):
        for at, line in enumerate(lines):
            copies[k * len(lines) + at].wait()
            for i in range(upd // TILE):
                row = block * (upd // TILE) + i
                here = slice(i * TILE, (i + 1) * TILE)
                for j in range(ipd // TILE):
                    column = line * (ipd // TILE) + j
                    lanes = slice(at * ipd + j * TILE, at * ipd + (j + 1) * TILE)
                    factor = mask_ref[row, column].astype(F32) * scale_ref[row, column]
                    out_ref[here, lanes] = (
                        held[k, here, lanes].astype(F32) * factor
                    ).astype(BF16)


def dequantize(me, values, mask, scale, shape):
    m, n = values.shape
    sides, chips, cols = shape
    smem = pl.BlockSpec(memory_space=pltpu.SMEM)
    return pl.pallas_call(
        functools.partial(dequantize_kernel, shape),
        out_shape=(jax.ShapeDtypeStruct((m // cols, n), BF16),) * cols,
        in_specs=[smem, smem, smem, pl.BlockSpec(memory_space=pltpu.HBM)],
        out_specs=(vmem_spec(),) * cols,
        scratch_shapes=[
            pltpu.VMEM((cols, m // cols, n), BF16),
            pltpu.SemaphoreType.DMA((cols, sides * chips)),
        ],
        compiler_params=no_room(),
        cost_estimate=pl.CostEstimate(flops=m * n, bytes_accessed=4 * m * n, transcendentals=0),
        name="dequantize",
    )(me, mask, scale, values)


def from_order(n):
    return [k if power_of_two(n) else (n - k) % n for k in range(n)]


def user_sum_kernel(cols, *refs):
    adj_refs, items_refs, out_refs = refs[:cols], refs[cols:-cols], refs[-cols:]
    items = jnp.concatenate([ref[...].reshape(-1, ref.shape[-1]) for ref in items_refs], axis=0)
    for adj_ref, out_ref in zip(adj_refs, out_refs, strict=True):
        out_ref[...] = jnp.dot(adj_ref[...], items, preferred_element_type=F32).astype(BF16)


def merge_kernel(*refs):
    for k, ref in enumerate(refs[:-1]):
        refs[-1][k] = ref[...]


def merge(blocks):
    return pl.pallas_call(
        merge_kernel,
        out_shape=jax.ShapeDtypeStruct((len(blocks), *blocks[0].shape), blocks[0].dtype),
        in_specs=[vmem_spec()] * len(blocks),
        out_specs=vmem_spec(),
        compiler_params=params(),
        name="merge",
    )(*blocks)


def user_sums(adjacency, items):
    cols = len(adjacency)
    upd, n = adjacency[0].shape
    d = items[0].shape[-1]
    return pl.pallas_call(
        functools.partial(user_sum_kernel, cols),
        out_shape=(jax.ShapeDtypeStruct((upd, d), BF16),) * cols,
        in_specs=[vmem_spec()] * (cols + len(items)),
        out_specs=(vmem_spec(),) * cols,
        compiler_params=params(),
        cost_estimate=pl.CostEstimate(
            flops=2 * cols * upd * n * d, bytes_accessed=2 * cols * upd * n, transcendentals=0
        ),
        name="user_sums",
    )(*adjacency, *items)


def item_sum_kernel(cols, *refs):
    adj_refs, users_refs, out_refs = refs[:cols], refs[cols : 2 * cols], refs[2 * cols :]
    order = from_order(cols)
    users = [ref[...] for ref in users_refs]
    at = 0
    for out_ref in reversed(out_refs):
        for r in range(out_ref.shape[0]):
            ipd = out_ref.shape[2]
            lanes = slice(at * ipd, (at + 1) * ipd)
            total = None
            for k in range(cols):
                part = jnp.dot(
                    users[k], adj_refs[order[k]][:, lanes], preferred_element_type=F32
                )
                total = part if total is None else total + part
            out_ref[r] = total.astype(out_ref.dtype)
            at += 1


def item_sums(adjacency, users_t, sides, chips):
    cols = len(adjacency)
    upd, n = adjacency[0].shape
    d = users_t[0].shape[0]
    block = (chips, d, n // (sides * chips))
    outs = [jax.ShapeDtypeStruct(block, BF16)] * (sides - 1)
    return pl.pallas_call(
        functools.partial(item_sum_kernel, cols),
        out_shape=[*outs, jax.ShapeDtypeStruct(block, F32)],
        in_specs=[vmem_spec()] * (2 * cols),
        out_specs=[vmem_spec()] * sides,
        compiler_params=params(),
        cost_estimate=pl.CostEstimate(
            flops=2 * cols * upd * n * d, bytes_accessed=2 * cols * upd * n, transcendentals=0
        ),
        name="item_sums",
    )(*adjacency, *users_t)


def item_add_kernel(chips, *refs):
    parts, outs = refs[:-chips], refs[-chips:]
    for k, out_ref in enumerate(outs):
        total = parts[0][k]
        for part in parts[1:]:
            total = total + part[k].astype(F32)
        out_ref[...] = total.astype(BF16)


def item_add(parts):
    chips, d, ipd = parts[0].shape
    return pl.pallas_call(
        functools.partial(item_add_kernel, chips),
        out_shape=(jax.ShapeDtypeStruct((d, ipd), BF16),) * chips,
        in_specs=[vmem_spec()] * len(parts),
        out_specs=(vmem_spec(),) * chips,
        compiler_params=params(),
        name="item_add",
    )(*parts)


def updated(side, own, weight_sum, weight_product):
    own = own.astype(F32)
    linear = jnp.dot((side + own).astype(BF16), weight_sum, preferred_element_type=F32)
    linear = linear + jnp.dot(
        (side * own).astype(BF16), weight_product, preferred_element_type=F32
    )
    return jnp.where(linear > 0, linear, 0.2 * linear)


def user_update_kernel(layer, own_ref, sum_ref, product_ref, *refs):
    parts, outs = refs[:-2], refs[-2:]
    side = parts[0][...].astype(F32)
    for part in parts[1:]:
        side = side + part[...].astype(F32)
    new = updated(side, own_ref[...], sum_ref[layer], product_ref[layer])
    outs[0][...] = new.astype(BF16)
    outs[1][...] = new.T.astype(BF16)


def user_update(layer, parts, own, weight_sum, weight_product):
    upd, d = own.shape
    return pl.pallas_call(
        functools.partial(user_update_kernel, layer),
        out_shape=(jax.ShapeDtypeStruct((upd, d), BF16), jax.ShapeDtypeStruct((d, upd), BF16)),
        in_specs=[vmem_spec()] * (3 + len(parts)),
        out_specs=(vmem_spec(),) * 2,
        compiler_params=params(),
        name="user_update",
    )(own, weight_sum, weight_product, *parts)


def item_update_kernel(layer, own_ref, sum_ref, product_ref, *refs):
    parts, new_ref = refs[:-1], refs[-1]
    side = parts[0][...].astype(F32)
    for part in parts[1:]:
        side = side + part[...].astype(F32)
    new = updated(side.T, own_ref[...], sum_ref[layer], product_ref[layer])
    new_ref[...] = new.astype(BF16)


def item_update(layer, parts, own, weight_sum, weight_product):
    return pl.pallas_call(
        functools.partial(item_update_kernel, layer),
        out_shape=jax.ShapeDtypeStruct(own.shape, BF16),
        in_specs=[vmem_spec()] * (3 + len(parts)),
        out_specs=vmem_spec(),
        compiler_params=params(),
        name="item_update",
    )(own, weight_sum, weight_product, *parts)


def exchange(blocks, axis, n, inner=1):
    received = [blocks[0]]
    for k in range(1, n):
        pairs = [
            (i * inner + j, peer_to(i, k, n) * inner + j) for i in range(n) for j in range(inner)
        ]
        received.append(lax.ppermute(blocks[k], axis, pairs))
    return received


def swap(block, axis, n):
    return lax.ppermute(block, axis, [(i, i ^ 1) for i in range(n)])


def ordered(received):
    order = from_order(len(received))
    return [received[order.index(k)] for k in range(len(received))]


def per_device(
    raw_rows,
    raw_wide,
    raw_dest,
    raw_slot,
    proj_narrow,
    proj_wide,
    adj_values,
    tile_mask,
    tile_scale,
    weight_sum,
    weight_product,
):
    rows = lax.axis_size("row")
    cols = lax.axis_size("col")
    devices = rows * cols
    count = raw_rows.shape[0]
    capacity = 3 * count // devices
    upd = adj_values.shape[0] // cols
    ipd = adj_values.shape[1] // rows
    layers = weight_sum.shape[0]
    sides = 2 if rows % 2 == 0 else 1
    chips = rows // sides
    me = lax.axis_index(("row", "col")).astype(jnp.int32).reshape(1)
    send = dispatch(
        me,
        raw_rows.T,
        raw_dest.reshape(1, count),
        raw_slot.reshape(1, count),
        raw_wide.reshape(1, count),
        devices,
        capacity,
    )
    recv = lax.all_to_all(send, ("row", "col"), split_axis=0, concat_axis=0, tiled=True)
    adjacency = dequantize(
        me, adj_values, tile_mask, tile_scale, (sides, chips, cols)
    )
    users, users_t, items, *moved = segment(
        me, recv, proj_narrow, proj_wide, adjacency[KEPT:], upd, ipd, capacity
    )
    adjacency = [*adjacency[:KEPT], *moved]
    for n in range(layers):
        all_users_t = exchange([users_t] * cols, "col", cols)
        all_items = ordered(exchange([items] * chips, "row", chips, sides))
        if sides > 1:
            merged = merge(all_items)
            all_items = [*all_items, swap(merged, "row", rows)]
        *away, kept = item_sums(adjacency, all_users_t, sides, chips)
        came = [swap(part, "row", rows) for part in away]
        user_parts = user_sums(adjacency, all_items)
        item_parts = item_add([kept, *came])
        item_parts = exchange(item_parts, "row", chips, sides)
        user_parts = exchange(user_parts, "col", cols)
        items = item_update(n, item_parts, items, weight_sum, weight_product)
        users, users_t = user_update(n, user_parts, users, weight_sum, weight_product)
    return (users, items[None])


def solution(mesh):
    placed = (
        P(("row", "col"), None),
        P(("row", "col")),
        P(("row", "col")),
        P(("row", "col")),
        P(),
        P(),
        P("row", "col"),
        P("row", "col"),
        P("row", "col"),
        P(),
        P(),
    )
    return jax.shard_map(
        per_device,
        mesh=mesh,
        in_specs=placed,
        out_specs=(P(("row", "col"), None), P("col", "row", None)),
        check_vma=False,
    )
```

```python
import functools

import jax
import jax.numpy as jnp
from jax import lax
from jax.experimental import pallas as pl
from jax.experimental.pallas import tpu as pltpu
from jax.sharding import PartitionSpec as P


TILE = 128
LANES = 128
CODE_ROWS = 8
GROUP = 8
KEPT = 1
F32 = jnp.float32
BF16 = jnp.bfloat16
NT = (((1,), (1,)), ((), ()))


def power_of_two(n):
    return n & (n - 1) == 0


def peer_to(i, k, n):
    return i ^ k if power_of_two(n) else (i + k) % n


def vmem_spec():
    return pl.BlockSpec(memory_space=pltpu.VMEM)


def params():
    return pltpu.CompilerParams(vmem_limit_bytes=24 * 2**20)


def whole_vmem():
    return pltpu.CompilerParams(vmem_limit_bytes=67_043_328)


def no_room():
    return pltpu.CompilerParams(vmem_limit_bytes=52 * 2**20)


def chunks_of(capacity, features):
    chunks, base, row = [], 0, 0
    size = LANES // 2
    while base < capacity:
        while size > max(8, capacity - base):
            size //= 2
        height = features * size // LANES
        chunks.append((base, size, row, height))
        base += size
        row += height
    return chunks, -(-row // CODE_ROWS) * CODE_ROWS


def turned(block, shift):
    shift = shift % LANES
    return block if shift == 0 else pltpu.roll(block, shift, 1)


def packed(placed, codes, chunks, code_row, shares):
    blocks, code_rows, height = [], jnp.zeros((CODE_ROWS, LANES), F32), 0
    code = lax.broadcasted_iota(jnp.int32, (CODE_ROWS, LANES), 0)
    for n, (_, size, _, rows) in enumerate(chunks):
        lanes = slice(n * LANES, (n + 1) * LANES)
        block = None
        for q in range(LANES // size):
            piece = turned(placed[q * rows : (q + 1) * rows, lanes], q * size)
            block = piece if block is None else jnp.where(shares[n] == q, piece, block)
        blocks.append(block)
        height += rows
        low = codes[0:1, lanes]
        high = turned(codes[:, lanes], size)[1:2]
        both = jnp.where(shares[n] == 0, low, jnp.where(shares[n] == 1, high, 0.0))
        code_rows = jnp.where(code == n, both, code_rows)
    if height < code_row:
        blocks.append(jnp.zeros((code_row - height, LANES), F32))
    return jnp.concatenate([*blocks, code_rows], axis=0)


def unpacked(recv_ref, first, count, features, capacity):
    chunks, code_row = chunks_of(capacity, features)
    lane = lax.broadcasted_iota(jnp.int32, (1, LANES), 1)
    out = []
    for n, (_, size, row, rows) in enumerate(chunks):
        parts = LANES // size
        share = lane // size
        for start in range(first, first + count, parts):

            def merged(q, lo, hi):
                block = None
                for s in range(parts):
                    piece = recv_ref[start + s, lo:hi].astype(F32)
                    here = share == (q + s) % parts
                    block = piece if block is None else jnp.where(here, piece, block)
                return turned(block, -q * size)

            values = jnp.concatenate(
                [merged(q, row, row + rows) for q in range(parts)], axis=0
            )
            low, high = (
                merged(q, code_row, code_row + CODE_ROWS)[n : n + 1] for q in range(2)
            )
            out.append((values, low, high))
    return [jnp.concatenate(part, axis=1) for part in zip(*out, strict=True)]


def dispatch_kernel(devices, capacity, me_ref, *refs):
    sources, out_ref, (raw_ref, dest_ref, slot_ref, wide_ref, held), (sems, out_sems) = (
        refs[:4],
        refs[4],
        refs[5:10],
        refs[10:],
    )
    copies = [
        pltpu.make_async_copy(source, ref, sems.at[n])
        for n, (source, ref) in enumerate(
            zip(sources, (raw_ref, dest_ref, slot_ref, wide_ref), strict=True)
        )
    ]
    for copy in copies:
        copy.start()
    copies[1].wait()
    features, rows = raw_ref.shape
    chunks = rows // LANES
    dest = dest_ref[...]
    hot = (lax.broadcasted_iota(jnp.int32, (devices, rows), 0) == dest).astype(F32)
    hot_bf = hot.astype(BF16)
    before = lax.broadcasted_iota(jnp.int32, (LANES, 2 * LANES), 0)
    column = lax.broadcasted_iota(jnp.int32, (LANES, 2 * LANES), 1)
    prefix = ((before < column) | (column >= LANES)).astype(F32).astype(BF16)
    base = jnp.zeros((devices, LANES), F32)
    ranks = []
    for chunk in range(chunks):
        lanes = slice(chunk * LANES, (chunk + 1) * LANES)
        counted = jnp.dot(hot_bf[:, lanes], prefix, preferred_element_type=F32)
        ranks.append(
            jnp.sum((counted[:, :LANES] + base) * hot[:, lanes], axis=0, keepdims=True)
        )
        base = base + counted[:, LANES:]
    rank = jnp.concatenate(ranks, axis=1)
    plan, code_row = chunks_of(capacity, features)
    lane = lax.broadcasted_iota(jnp.int32, (1, LANES), 1)
    line = lax.broadcasted_iota(jnp.int32, (LANES, 1), 0)
    shares, places = [], []
    for first, size, _, _ in plan:
        parts = LANES // size
        turn = me_ref[0] % parts
        shares.append((lane // size + parts - turn) % parts)
        slot_of = line - turn * size
        inside = (slot_of >= 0) & (slot_of < size)
        wanted = jnp.where(inside, slot_of + first, -1).astype(F32)
        places.append((wanted == rank).astype(F32).astype(BF16))
    place = jnp.concatenate(places, axis=0)
    for copy in (copies[0], copies[2], copies[3]):
        copy.wait()
    slot = slot_ref[...]
    code = lax.broadcasted_iota(jnp.int32, (2 * CODE_ROWS, rows), 0)
    codes = jnp.where(
        code == 0,
        slot % 256,
        jnp.where(code == 1, slot // 256 * 2 + wide_ref[...], 0),
    )
    ext = jnp.concatenate([raw_ref[...], codes.astype(F32).astype(BF16)], axis=0)
    height = features + CODE_ROWS
    middle = jnp.concatenate(
        [ext[features : features + CODE_ROWS].astype(F32), ext[:CODE_ROWS].astype(F32)], axis=0
    ).astype(BF16)
    rest = jnp.concatenate(
        [ext[CODE_ROWS:features].astype(F32), ext[features : features + CODE_ROWS].astype(F32)],
        axis=0,
    ).astype(BF16)
    upper = lax.broadcasted_iota(jnp.int32, (2 * CODE_ROWS, 1), 0) < CODE_ROWS
    writes = []
    for n, first in enumerate(range(0, devices, GROUP)):
        masked = jnp.concatenate(
            [
                piece
                for d in range(first, first + GROUP, 2)
                for piece in (
                    ext[:features] * hot_bf[d : d + 1],
                    middle * jnp.where(upper, hot_bf[d : d + 1], hot_bf[d + 1 : d + 2]),
                    rest * hot_bf[d + 1 : d + 2],
                )
            ],
            axis=0,
        )
        placed = lax.dot_general(masked, place, NT, preferred_element_type=F32)
        for d in range(GROUP):
            mine = placed[d * height : (d + 1) * height]
            held[first + d] = packed(
                mine[:features],
                mine[features : features + CODE_ROWS],
                plan,
                code_row,
                shares,
            ).astype(BF16)
        writes.append(
            pltpu.make_async_copy(
                held.at[pl.ds(first, GROUP)], out_ref.at[pl.ds(first, GROUP)], out_sems.at[n]
            )
        )
        writes[-1].start()
    for write in writes:
        write.wait()


def dispatch(me, raw, dest, slot, wide, devices, capacity):
    features, rows = raw.shape
    shape = (devices, chunks_of(capacity, features)[1] + CODE_ROWS, LANES)
    return pl.pallas_call(
        functools.partial(dispatch_kernel, devices, capacity),
        out_shape=jax.ShapeDtypeStruct(shape, BF16),
        in_specs=[pl.BlockSpec(memory_space=pltpu.SMEM)]
        + [pl.BlockSpec(memory_space=pltpu.HBM)] * 4,
        out_specs=pl.BlockSpec(memory_space=pltpu.HBM),
        scratch_shapes=[
            pltpu.VMEM(raw.shape, raw.dtype),
            *[pltpu.VMEM((1, rows), jnp.int32) for _ in range(3)],
            pltpu.VMEM(shape, BF16),
            pltpu.SemaphoreType.DMA((4,)),
            pltpu.SemaphoreType.DMA((devices // GROUP,)),
        ],
        compiler_params=whole_vmem(),
        name="dispatch",
    )(me, raw, dest, slot, wide)


def segment_kernel(
    capacity, upd, moved, me_ref, recv_ref, proj_narrow_ref, proj_wide_ref, *refs
):
    adj_refs, outs = refs[:moved], refs[moved : moved + 3]
    held_refs, sems = refs[moved + 3 : -1], refs[-1]
    copies = [
        pltpu.make_async_copy(adj_ref, held_ref, sems.at[k])
        for k, (adj_ref, held_ref) in enumerate(zip(adj_refs, held_refs, strict=True))
    ]
    for copy in copies:
        copy.start()

    @pl.when(me_ref[0] >= 0)
    def _():
        initial_rows(capacity, upd, recv_ref, proj_narrow_ref, proj_wide_ref, *outs)

    for copy in copies:
        copy.wait()


def initial_rows(
    capacity, upd, recv_ref, proj_narrow_ref, proj_wide_ref, user_ref, user_t_ref, item_ref
):
    devices = recv_ref.shape[0]
    narrow, features = proj_narrow_ref.shape[0], proj_wide_ref.shape[0]
    nodes = user_ref.shape[0] + item_ref.shape[0]
    total = jnp.zeros((nodes, features + narrow), F32)
    count = max(GROUP, *[LANES // chunk[1] for chunk in chunks_of(capacity, features)[0]])
    for first in range(0, devices, count):
        rows, low, high = unpacked(recv_ref, first, count, features, capacity)
        rows = rows.astype(BF16)
        high = high.astype(jnp.int32)
        node = low.astype(jnp.int32) + (high >> 1) * 256
        wide = (high & 1).astype(F32).astype(BF16)
        values = jnp.concatenate([rows * wide, rows[:narrow] * (1 - wide)], axis=0)
        hot = (
            lax.broadcasted_iota(jnp.int32, (nodes, node.shape[1]), 0) == node
        ).astype(F32).astype(BF16)
        total = total + lax.dot_general(hot, values, NT, preferred_element_type=F32)
    weights = jnp.concatenate([proj_wide_ref[...], proj_narrow_ref[...]], axis=0)
    initial = jnp.zeros((nodes, weights.shape[1]), F32)
    rest = total
    for _ in range(3):
        part = rest.astype(BF16)
        initial = initial + jnp.dot(part, weights, preferred_element_type=F32)
        rest = rest - part.astype(F32)
    users = initial[:upd]
    items = initial[upd:].astype(BF16)
    user_ref[...] = users.astype(BF16)
    user_t_ref[...] = users.T.astype(BF16)
    item_ref[...] = items


def segment(me, recv, proj_narrow, proj_wide, adjacency, upd, ipd, capacity):
    cols = len(adjacency)
    d = proj_wide.shape[1]
    return pl.pallas_call(
        functools.partial(segment_kernel, capacity, upd, cols),
        out_shape=(
            jax.ShapeDtypeStruct((upd, d), BF16),
            jax.ShapeDtypeStruct((d, upd), BF16),
            jax.ShapeDtypeStruct((ipd, d), BF16),
            *[jax.ShapeDtypeStruct(block.shape, BF16) for block in adjacency],
        ),
        in_specs=[pl.BlockSpec(memory_space=pltpu.SMEM)]
        + [vmem_spec()] * 3
        + [pl.BlockSpec(memory_space=pltpu.HBM)] * cols,
        out_specs=(vmem_spec(),) * (3 + cols),
        scratch_shapes=[pltpu.SemaphoreType.DMA((cols,))],
        compiler_params=params(),
        name="segment",
    )(
        me,
        recv,
        proj_narrow,
        proj_wide,
        *[pltpu.with_memory_space_constraint(block, pltpu.HBM) for block in adjacency],
    )


def dequantize_kernel(shape, me_ref, mask_ref, scale_ref, values_ref, *refs):
    out_refs, (held, sems) = refs[:-2], refs[-2:]
    sides, chips, cols = shape
    upd, n = out_refs[0].shape
    ipd = n // (sides * chips)
    row_here, col_here = me_ref[0] // cols, me_ref[0] % cols
    chip, side_here = row_here // sides, row_here % sides
    blocks = [peer_to(col_here, k, cols) for k in range(cols)]
    lines = [
        peer_to(chip, k, chips) * sides + (side_here + side) % sides
        for side in range(sides)
        for k in range(chips)
    ]
    copies = []
    for k, block in enumerate(blocks):
        start = pl.multiple_of(block * upd, upd)
        for at, line in enumerate(lines):
            first = pl.multiple_of(line * ipd, ipd)
            copies.append(
                pltpu.make_async_copy(
                    values_ref.at[pl.ds(start, upd), pl.ds(first, ipd)],
                    held.at[k, :, pl.ds(at * ipd, ipd)],
                    sems.at[k, at],
                )
            )
            copies[-1].start()
    for k, (block, out_ref) in enumerate(zip(blocks, out_refs, strict=True)):
        for at, line in enumerate(lines):
            copies[k * len(lines) + at].wait()
            for i in range(upd // TILE):
                row = block * (upd // TILE) + i
                here = slice(i * TILE, (i + 1) * TILE)
                for j in range(ipd // TILE):
                    column = line * (ipd // TILE) + j
                    lanes = slice(at * ipd + j * TILE, at * ipd + (j + 1) * TILE)
                    factor = mask_ref[row, column].astype(F32) * scale_ref[row, column]
                    out_ref[here, lanes] = (
                        held[k, here, lanes].astype(F32) * factor
                    ).astype(BF16)


def dequantize(me, values, mask, scale, shape):
    m, n = values.shape
    sides, chips, cols = shape
    smem = pl.BlockSpec(memory_space=pltpu.SMEM)
    return pl.pallas_call(
        functools.partial(dequantize_kernel, shape),
        out_shape=(jax.ShapeDtypeStruct((m // cols, n), BF16),) * cols,
        in_specs=[smem, smem, smem, pl.BlockSpec(memory_space=pltpu.HBM)],
        out_specs=(vmem_spec(),) * cols,
        scratch_shapes=[
            pltpu.VMEM((cols, m // cols, n), BF16),
            pltpu.SemaphoreType.DMA((cols, sides * chips)),
        ],
        compiler_params=no_room(),
        cost_estimate=pl.CostEstimate(flops=m * n, bytes_accessed=4 * m * n, transcendentals=0),
        name="dequantize",
    )(me, mask, scale, values)


def from_order(n):
    return [k if power_of_two(n) else (n - k) % n for k in range(n)]


def user_sum_kernel(cols, *refs):
    adj_refs, items_refs, out_refs = refs[:cols], refs[cols:-cols], refs[-cols:]
    items = jnp.concatenate([ref[...].reshape(-1, ref.shape[-1]) for ref in items_refs], axis=0)
    for adj_ref, out_ref in zip(adj_refs, out_refs, strict=True):
        out_ref[...] = jnp.dot(adj_ref[...], items, preferred_element_type=F32).astype(BF16)


def merge_kernel(*refs):
    for k, ref in enumerate(refs[:-1]):
        refs[-1][k] = ref[...]


def merge(blocks):
    return pl.pallas_call(
        merge_kernel,
        out_shape=jax.ShapeDtypeStruct((len(blocks), *blocks[0].shape), blocks[0].dtype),
        in_specs=[vmem_spec()] * len(blocks),
        out_specs=vmem_spec(),
        compiler_params=params(),
        name="merge",
    )(*blocks)


def user_sums(adjacency, items):
    cols = len(adjacency)
    upd, n = adjacency[0].shape
    d = items[0].shape[-1]
    return pl.pallas_call(
        functools.partial(user_sum_kernel, cols),
        out_shape=(jax.ShapeDtypeStruct((upd, d), BF16),) * cols,
        in_specs=[vmem_spec()] * (cols + len(items)),
        out_specs=(vmem_spec(),) * cols,
        compiler_params=params(),
        cost_estimate=pl.CostEstimate(
            flops=2 * cols * upd * n * d, bytes_accessed=2 * cols * upd * n, transcendentals=0
        ),
        name="user_sums",
    )(*adjacency, *items)


def item_sum_kernel(cols, *refs):
    adj_refs, users_refs, out_refs = refs[:cols], refs[cols : 2 * cols], refs[2 * cols :]
    order = from_order(cols)
    users = [ref[...] for ref in users_refs]
    at = 0
    for out_ref in reversed(out_refs):
        for r in range(out_ref.shape[0]):
            ipd = out_ref.shape[2]
            lanes = slice(at * ipd, (at + 1) * ipd)
            total = None
            for k in range(cols):
                part = jnp.dot(
                    users[k], adj_refs[order[k]][:, lanes], preferred_element_type=F32
                )
                total = part if total is None else total + part
            out_ref[r] = total.astype(out_ref.dtype)
            at += 1


def item_sums(adjacency, users_t, sides, chips):
    cols = len(adjacency)
    upd, n = adjacency[0].shape
    d = users_t[0].shape[0]
    block = (chips, d, n // (sides * chips))
    outs = [jax.ShapeDtypeStruct(block, BF16)] * (sides - 1)
    return pl.pallas_call(
        functools.partial(item_sum_kernel, cols),
        out_shape=[*outs, jax.ShapeDtypeStruct(block, F32)],
        in_specs=[vmem_spec()] * (2 * cols),
        out_specs=[vmem_spec()] * sides,
        compiler_params=params(),
        cost_estimate=pl.CostEstimate(
            flops=2 * cols * upd * n * d, bytes_accessed=2 * cols * upd * n, transcendentals=0
        ),
        name="item_sums",
    )(*adjacency, *users_t)


def item_add_kernel(chips, *refs):
    parts, outs = refs[:-chips], refs[-chips:]
    for k, out_ref in enumerate(outs):
        total = parts[0][k]
        for part in parts[1:]:
            total = total + part[k].astype(F32)
        out_ref[...] = total.astype(BF16)


def item_add(parts):
    chips, d, ipd = parts[0].shape
    return pl.pallas_call(
        functools.partial(item_add_kernel, chips),
        out_shape=(jax.ShapeDtypeStruct((d, ipd), BF16),) * chips,
        in_specs=[vmem_spec()] * len(parts),
        out_specs=(vmem_spec(),) * chips,
        compiler_params=params(),
        name="item_add",
    )(*parts)


def updated(side, own, weight_sum, weight_product):
    own = own.astype(F32)
    linear = jnp.dot((side + own).astype(BF16), weight_sum, preferred_element_type=F32)
    linear = linear + jnp.dot(
        (side * own).astype(BF16), weight_product, preferred_element_type=F32
    )
    return jnp.where(linear > 0, linear, 0.2 * linear)


def user_update_kernel(layer, own_ref, sum_ref, product_ref, *refs):
    parts, outs = refs[:-2], refs[-2:]
    side = parts[0][...].astype(F32)
    for part in parts[1:]:
        side = side + part[...].astype(F32)
    new = updated(side, own_ref[...], sum_ref[layer], product_ref[layer])
    outs[0][...] = new.astype(BF16)
    outs[1][...] = new.T.astype(BF16)


def user_update(layer, parts, own, weight_sum, weight_product):
    upd, d = own.shape
    return pl.pallas_call(
        functools.partial(user_update_kernel, layer),
        out_shape=(jax.ShapeDtypeStruct((upd, d), BF16), jax.ShapeDtypeStruct((d, upd), BF16)),
        in_specs=[vmem_spec()] * (3 + len(parts)),
        out_specs=(vmem_spec(),) * 2,
        compiler_params=params(),
        name="user_update",
    )(own, weight_sum, weight_product, *parts)


def item_update_kernel(layer, own_ref, sum_ref, product_ref, *refs):
    parts, new_ref = refs[:-1], refs[-1]
    side = parts[0][...].astype(F32)
    for part in parts[1:]:
        side = side + part[...].astype(F32)
    new = updated(side.T, own_ref[...], sum_ref[layer], product_ref[layer])
    new_ref[...] = new.astype(BF16)


def item_update(layer, parts, own, weight_sum, weight_product):
    return pl.pallas_call(
        functools.partial(item_update_kernel, layer),
        out_shape=jax.ShapeDtypeStruct(own.shape, BF16),
        in_specs=[vmem_spec()] * (3 + len(parts)),
        out_specs=vmem_spec(),
        compiler_params=params(),
        name="item_update",
    )(own, weight_sum, weight_product, *parts)


def exchange(blocks, axis, n, inner=1):
    received = [blocks[0]]
    for k in range(1, n):
        pairs = [
            (i * inner + j, peer_to(i, k, n) * inner + j) for i in range(n) for j in range(inner)
        ]
        received.append(lax.ppermute(blocks[k], axis, pairs))
    return received


def swap(block, axis, n):
    return lax.ppermute(block, axis, [(i, i ^ 1) for i in range(n)])


def ordered(received):
    order = from_order(len(received))
    return [received[order.index(k)] for k in range(len(received))]


def per_device(
    raw_rows,
    raw_wide,
    raw_dest,
    raw_slot,
    proj_narrow,
    proj_wide,
    adj_values,
    tile_mask,
    tile_scale,
    weight_sum,
    weight_product,
):
    rows = lax.axis_size("row")
    cols = lax.axis_size("col")
    devices = rows * cols
    count = raw_rows.shape[0]
    capacity = 3 * count // devices
    upd = adj_values.shape[0] // cols
    ipd = adj_values.shape[1] // rows
    layers = weight_sum.shape[0]
    sides = 2 if rows % 2 == 0 else 1
    chips = rows // sides
    me = lax.axis_index(("row", "col")).astype(jnp.int32).reshape(1)
    send = dispatch(
        me,
        raw_rows.T,
        raw_dest.reshape(1, count),
        raw_slot.reshape(1, count),
        raw_wide.reshape(1, count),
        devices,
        capacity,
    )
    recv = lax.all_to_all(send, ("row", "col"), split_axis=0, concat_axis=0, tiled=True)
    adjacency = dequantize(
        me, adj_values, tile_mask, tile_scale, (sides, chips, cols)
    )
    users, users_t, items, *moved = segment(
        me, recv, proj_narrow, proj_wide, adjacency[KEPT:], upd, ipd, capacity
    )
    adjacency = [*adjacency[:KEPT], *moved]
    for n in range(layers):
        all_users_t = exchange([users_t] * cols, "col", cols)
        all_items = ordered(exchange([items] * chips, "row", chips, sides))
        if sides > 1:
            merged = merge(all_items)
            all_items = [*all_items, swap(merged, "row", rows)]
        *away, kept = item_sums(adjacency, all_users_t, sides, chips)
        came = [swap(part, "row", rows) for part in away]
        user_parts = user_sums(adjacency, all_items)
        item_parts = item_add([kept, *came])
        item_parts = exchange(item_parts, "row", chips, sides)
        user_parts = exchange(user_parts, "col", cols)
        items = item_update(n, item_parts, items, weight_sum, weight_product)
        users, users_t = user_update(n, user_parts, users, weight_sum, weight_product)
    return (users, items[None])


def solution(mesh):
    placed = (
        P(("row", "col"), None),
        P(("row", "col")),
        P(("row", "col")),
        P(("row", "col")),
        P(),
        P(),
        P("row", "col"),
        P("row", "col"),
        P("row", "col"),
        P(),
        P(),
    )
    return jax.shard_map(
        per_device,
        mesh=mesh,
        in_specs=placed,
        out_specs=(P(("row", "col"), None), P("col", "row", None)),
        check_vma=False,
    )
```

```python
import functools

import jax
import jax.numpy as jnp
from jax import lax
from jax.experimental import pallas as pl
from jax.experimental.pallas import tpu as pltpu
from jax.sharding import PartitionSpec as P


TILE = 128
LANES = 128
CODE_ROWS = 8
GROUP = 4
KEPT = 1
F32 = jnp.float32
BF16 = jnp.bfloat16
NT = (((1,), (1,)), ((), ()))


def power_of_two(n):
    return n & (n - 1) == 0


def peer_to(i, k, n):
    return i ^ k if power_of_two(n) else (i + k) % n


def vmem_spec():
    return pl.BlockSpec(memory_space=pltpu.VMEM)


def params():
    return pltpu.CompilerParams(vmem_limit_bytes=24 * 2**20)


def whole_vmem():
    return pltpu.CompilerParams(vmem_limit_bytes=67_043_328)


def no_room():
    return pltpu.CompilerParams(vmem_limit_bytes=52 * 2**20)


def chunks_of(capacity, features):
    chunks, base, row = [], 0, 0
    size = LANES // 2
    while base < capacity:
        while size > max(8, capacity - base):
            size //= 2
        height = features * size // LANES
        chunks.append((base, size, row, height))
        base += size
        row += height
    return chunks, -(-row // CODE_ROWS) * CODE_ROWS


def turned(block, shift):
    shift = shift % LANES
    return block if shift == 0 else pltpu.roll(block, shift, 1)


def packed(placed, codes, chunks, code_row, shares):
    blocks, code_rows, height = [], jnp.zeros((CODE_ROWS, LANES), F32), 0
    code = lax.broadcasted_iota(jnp.int32, (CODE_ROWS, LANES), 0)
    for n, (_, size, _, rows) in enumerate(chunks):
        lanes = slice(n * LANES, (n + 1) * LANES)
        block = None
        for q in range(LANES // size):
            piece = turned(placed[q * rows : (q + 1) * rows, lanes], q * size)
            block = piece if block is None else jnp.where(shares[n] == q, piece, block)
        blocks.append(block)
        height += rows
        low = codes[0:1, lanes]
        high = turned(codes[:, lanes], size)[1:2]
        both = jnp.where(shares[n] == 0, low, jnp.where(shares[n] == 1, high, 0.0))
        code_rows = jnp.where(code == n, both, code_rows)
    if height < code_row:
        blocks.append(jnp.zeros((code_row - height, LANES), F32))
    return jnp.concatenate([*blocks, code_rows], axis=0)


def unpacked(recv_ref, first, count, features, capacity):
    chunks, code_row = chunks_of(capacity, features)
    lane = lax.broadcasted_iota(jnp.int32, (1, LANES), 1)
    out = []
    for n, (_, size, row, rows) in enumerate(chunks):
        parts = LANES // size
        share = lane // size
        for start in range(first, first + count, parts):

            def merged(q, lo, hi):
                block = None
                for s in range(parts):
                    piece = recv_ref[start + s, lo:hi].astype(F32)
                    here = share == (q + s) % parts
                    block = piece if block is None else jnp.where(here, piece, block)
                return turned(block, -q * size)

            values = jnp.concatenate(
                [merged(q, row, row + rows) for q in range(parts)], axis=0
            )
            low, high = (
                merged(q, code_row, code_row + CODE_ROWS)[n : n + 1] for q in range(2)
            )
            out.append((values, low, high))
    return [jnp.concatenate(part, axis=1) for part in zip(*out, strict=True)]


def dispatch_kernel(devices, capacity, me_ref, *refs):
    sources, out_ref, (raw_ref, dest_ref, slot_ref, wide_ref, held), (sems, out_sems) = (
        refs[:4],
        refs[4],
        refs[5:10],
        refs[10:],
    )
    copies = [
        pltpu.make_async_copy(source, ref, sems.at[n])
        for n, (source, ref) in enumerate(
            zip(sources, (raw_ref, dest_ref, slot_ref, wide_ref), strict=True)
        )
    ]
    for copy in copies:
        copy.start()
    copies[1].wait()
    features, rows = raw_ref.shape
    chunks = rows // LANES
    dest = dest_ref[...]
    hot = (lax.broadcasted_iota(jnp.int32, (devices, rows), 0) == dest).astype(F32)
    hot_bf = hot.astype(BF16)
    before = lax.broadcasted_iota(jnp.int32, (LANES, 2 * LANES), 0)
    column = lax.broadcasted_iota(jnp.int32, (LANES, 2 * LANES), 1)
    prefix = ((before < column) | (column >= LANES)).astype(F32).astype(BF16)
    base = jnp.zeros((devices, LANES), F32)
    ranks = []
    for chunk in range(chunks):
        lanes = slice(chunk * LANES, (chunk + 1) * LANES)
        counted = jnp.dot(hot_bf[:, lanes], prefix, preferred_element_type=F32)
        ranks.append(
            jnp.sum((counted[:, :LANES] + base) * hot[:, lanes], axis=0, keepdims=True)
        )
        base = base + counted[:, LANES:]
    rank = jnp.concatenate(ranks, axis=1)
    plan, code_row = chunks_of(capacity, features)
    lane = lax.broadcasted_iota(jnp.int32, (1, LANES), 1)
    line = lax.broadcasted_iota(jnp.int32, (LANES, 1), 0)
    shares, places = [], []
    for first, size, _, _ in plan:
        parts = LANES // size
        turn = me_ref[0] % parts
        shares.append((lane // size + parts - turn) % parts)
        slot_of = line - turn * size
        inside = (slot_of >= 0) & (slot_of < size)
        wanted = jnp.where(inside, slot_of + first, -1).astype(F32)
        places.append((wanted == rank).astype(F32).astype(BF16))
    place = jnp.concatenate(places, axis=0)
    for copy in (copies[0], copies[2], copies[3]):
        copy.wait()
    slot = slot_ref[...]
    code = lax.broadcasted_iota(jnp.int32, (2 * CODE_ROWS, rows), 0)
    codes = jnp.where(
        code == 0,
        slot % 256,
        jnp.where(code == 1, slot // 256 * 2 + wide_ref[...], 0),
    )
    ext = jnp.concatenate([raw_ref[...], codes.astype(F32).astype(BF16)], axis=0)
    height = features + CODE_ROWS
    middle = jnp.concatenate(
        [ext[features : features + CODE_ROWS].astype(F32), ext[:CODE_ROWS].astype(F32)], axis=0
    ).astype(BF16)
    rest = jnp.concatenate(
        [ext[CODE_ROWS:features].astype(F32), ext[features : features + CODE_ROWS].astype(F32)],
        axis=0,
    ).astype(BF16)
    upper = lax.broadcasted_iota(jnp.int32, (2 * CODE_ROWS, 1), 0) < CODE_ROWS
    writes = []
    for n, first in enumerate(range(0, devices, GROUP)):
        masked = jnp.concatenate(
            [
                piece
                for d in range(first, first + GROUP, 2)
                for piece in (
                    ext[:features] * hot_bf[d : d + 1],
                    middle * jnp.where(upper, hot_bf[d : d + 1], hot_bf[d + 1 : d + 2]),
                    rest * hot_bf[d + 1 : d + 2],
                )
            ],
            axis=0,
        )
        placed = lax.dot_general(masked, place, NT, preferred_element_type=F32)
        for d in range(GROUP):
            mine = placed[d * height : (d + 1) * height]
            held[first + d] = packed(
                mine[:features],
                mine[features : features + CODE_ROWS],
                plan,
                code_row,
                shares,
            ).astype(BF16)
        writes.append(
            pltpu.make_async_copy(
                held.at[pl.ds(first, GROUP)], out_ref.at[pl.ds(first, GROUP)], out_sems.at[n]
            )
        )
        writes[-1].start()
    for write in writes:
        write.wait()


def dispatch(me, raw, dest, slot, wide, devices, capacity):
    features, rows = raw.shape
    shape = (devices, chunks_of(capacity, features)[1] + CODE_ROWS, LANES)
    return pl.pallas_call(
        functools.partial(dispatch_kernel, devices, capacity),
        out_shape=jax.ShapeDtypeStruct(shape, BF16),
        in_specs=[pl.BlockSpec(memory_space=pltpu.SMEM)]
        + [pl.BlockSpec(memory_space=pltpu.HBM)] * 4,
        out_specs=pl.BlockSpec(memory_space=pltpu.HBM),
        scratch_shapes=[
            pltpu.VMEM(raw.shape, raw.dtype),
            *[pltpu.VMEM((1, rows), jnp.int32) for _ in range(3)],
            pltpu.VMEM(shape, BF16),
            pltpu.SemaphoreType.DMA((4,)),
            pltpu.SemaphoreType.DMA((devices // GROUP,)),
        ],
        compiler_params=whole_vmem(),
        name="dispatch",
    )(me, raw, dest, slot, wide)


def segment_kernel(
    capacity, upd, moved, me_ref, recv_ref, proj_narrow_ref, proj_wide_ref, *refs
):
    adj_refs, outs = refs[:moved], refs[moved : moved + 3]
    held_refs, sems = refs[moved + 3 : -1], refs[-1]
    copies = [
        pltpu.make_async_copy(adj_ref, held_ref, sems.at[k])
        for k, (adj_ref, held_ref) in enumerate(zip(adj_refs, held_refs, strict=True))
    ]
    for copy in copies:
        copy.start()

    @pl.when(me_ref[0] >= 0)
    def _():
        initial_rows(capacity, upd, recv_ref, proj_narrow_ref, proj_wide_ref, *outs)

    for copy in copies:
        copy.wait()


def initial_rows(
    capacity, upd, recv_ref, proj_narrow_ref, proj_wide_ref, user_ref, user_t_ref, item_ref
):
    devices = recv_ref.shape[0]
    narrow, features = proj_narrow_ref.shape[0], proj_wide_ref.shape[0]
    nodes = user_ref.shape[0] + item_ref.shape[0]
    total = jnp.zeros((nodes, features + narrow), F32)
    count = max(GROUP, *[LANES // chunk[1] for chunk in chunks_of(capacity, features)[0]])
    for first in range(0, devices, count):
        rows, low, high = unpacked(recv_ref, first, count, features, capacity)
        rows = rows.astype(BF16)
        high = high.astype(jnp.int32)
        node = low.astype(jnp.int32) + (high >> 1) * 256
        wide = (high & 1).astype(F32).astype(BF16)
        values = jnp.concatenate([rows * wide, rows[:narrow] * (1 - wide)], axis=0)
        hot = (
            lax.broadcasted_iota(jnp.int32, (nodes, node.shape[1]), 0) == node
        ).astype(F32).astype(BF16)
        total = total + lax.dot_general(hot, values, NT, preferred_element_type=F32)
    weights = jnp.concatenate([proj_wide_ref[...], proj_narrow_ref[...]], axis=0)
    initial = jnp.zeros((nodes, weights.shape[1]), F32)
    rest = total
    for _ in range(3):
        part = rest.astype(BF16)
        initial = initial + jnp.dot(part, weights, preferred_element_type=F32)
        rest = rest - part.astype(F32)
    users = initial[:upd]
    items = initial[upd:].astype(BF16)
    user_ref[...] = users.astype(BF16)
    user_t_ref[...] = users.T.astype(BF16)
    item_ref[...] = items


def segment(me, recv, proj_narrow, proj_wide, adjacency, upd, ipd, capacity):
    cols = len(adjacency)
    d = proj_wide.shape[1]
    return pl.pallas_call(
        functools.partial(segment_kernel, capacity, upd, cols),
        out_shape=(
            jax.ShapeDtypeStruct((upd, d), BF16),
            jax.ShapeDtypeStruct((d, upd), BF16),
            jax.ShapeDtypeStruct((ipd, d), BF16),
            *[jax.ShapeDtypeStruct(block.shape, BF16) for block in adjacency],
        ),
        in_specs=[pl.BlockSpec(memory_space=pltpu.SMEM)]
        + [vmem_spec()] * 3
        + [pl.BlockSpec(memory_space=pltpu.HBM)] * cols,
        out_specs=(vmem_spec(),) * (3 + cols),
        scratch_shapes=[pltpu.SemaphoreType.DMA((cols,))],
        compiler_params=params(),
        name="segment",
    )(
        me,
        recv,
        proj_narrow,
        proj_wide,
        *[pltpu.with_memory_space_constraint(block, pltpu.HBM) for block in adjacency],
    )


def dequantize_kernel(shape, me_ref, mask_ref, scale_ref, values_ref, *refs):
    out_refs, (held, sems) = refs[:-2], refs[-2:]
    sides, chips, cols = shape
    upd, n = out_refs[0].shape
    ipd = n // (sides * chips)
    row_here, col_here = me_ref[0] // cols, me_ref[0] % cols
    chip, side_here = row_here // sides, row_here % sides
    blocks = [peer_to(col_here, k, cols) for k in range(cols)]
    lines = [
        peer_to(chip, k, chips) * sides + (side_here + side) % sides
        for side in range(sides)
        for k in range(chips)
    ]
    copies = []
    for k, block in enumerate(blocks):
        start = pl.multiple_of(block * upd, upd)
        for at, line in enumerate(lines):
            first = pl.multiple_of(line * ipd, ipd)
            copies.append(
                pltpu.make_async_copy(
                    values_ref.at[pl.ds(start, upd), pl.ds(first, ipd)],
                    held.at[k, :, pl.ds(at * ipd, ipd)],
                    sems.at[k, at],
                )
            )
            copies[-1].start()
    for k, (block, out_ref) in enumerate(zip(blocks, out_refs, strict=True)):
        for at, line in enumerate(lines):
            copies[k * len(lines) + at].wait()
            for i in range(upd // TILE):
                row = block * (upd // TILE) + i
                here = slice(i * TILE, (i + 1) * TILE)
                for j in range(ipd // TILE):
                    column = line * (ipd // TILE) + j
                    lanes = slice(at * ipd + j * TILE, at * ipd + (j + 1) * TILE)
                    factor = mask_ref[row, column].astype(F32) * scale_ref[row, column]
                    out_ref[here, lanes] = (
                        held[k, here, lanes].astype(F32) * factor
                    ).astype(BF16)


def dequantize(me, values, mask, scale, shape):
    m, n = values.shape
    sides, chips, cols = shape
    smem = pl.BlockSpec(memory_space=pltpu.SMEM)
    return pl.pallas_call(
        functools.partial(dequantize_kernel, shape),
        out_shape=(jax.ShapeDtypeStruct((m // cols, n), BF16),) * cols,
        in_specs=[smem, smem, smem, pl.BlockSpec(memory_space=pltpu.HBM)],
        out_specs=(vmem_spec(),) * cols,
        scratch_shapes=[
            pltpu.VMEM((cols, m // cols, n), BF16),
            pltpu.SemaphoreType.DMA((cols, sides * chips)),
        ],
        compiler_params=no_room(),
        cost_estimate=pl.CostEstimate(flops=m * n, bytes_accessed=4 * m * n, transcendentals=0),
        name="dequantize",
    )(me, mask, scale, values)


def from_order(n):
    return [k if power_of_two(n) else (n - k) % n for k in range(n)]


def user_sum_kernel(cols, first, began, *refs):
    adj_refs, refs, out_refs = refs[:cols], refs[cols:-cols], refs[-cols:]
    begun, items_refs = (refs[:cols], refs[cols:]) if began else (None, refs)
    items = jnp.concatenate([ref[...].reshape(-1, ref.shape[-1]) for ref in items_refs], axis=0)
    lanes = slice(first, first + items.shape[0])
    for k, (adj_ref, out_ref) in enumerate(zip(adj_refs, out_refs, strict=True)):
        total = jnp.dot(adj_ref[:, lanes], items, preferred_element_type=F32)
        if began:
            total = total + begun[k][...]
        out_ref[...] = total.astype(out_ref.dtype)


def merge_kernel(*refs):
    for k, ref in enumerate(refs[:-1]):
        refs[-1][k] = ref[...]


def merge(blocks):
    return pl.pallas_call(
        merge_kernel,
        out_shape=jax.ShapeDtypeStruct((len(blocks), *blocks[0].shape), blocks[0].dtype),
        in_specs=[vmem_spec()] * len(blocks),
        out_specs=vmem_spec(),
        compiler_params=params(),
        name="merge",
    )(*blocks)


def user_sums(adjacency, items, first=0, begun=(), dtype=BF16):
    cols = len(adjacency)
    upd = adjacency[0].shape[0]
    n = sum(block.size for block in items) // items[0].shape[-1]
    d = items[0].shape[-1]
    return pl.pallas_call(
        functools.partial(user_sum_kernel, cols, first, len(begun) > 0),
        out_shape=(jax.ShapeDtypeStruct((upd, d), dtype),) * cols,
        in_specs=[vmem_spec()] * (cols + len(begun) + len(items)),
        out_specs=(vmem_spec(),) * cols,
        compiler_params=params(),
        cost_estimate=pl.CostEstimate(
            flops=2 * cols * upd * n * d, bytes_accessed=2 * cols * upd * n, transcendentals=0
        ),
        name="user_sums",
    )(*adjacency, *begun, *items)


def item_sum_kernel(cols, *refs):
    adj_refs, users_refs, out_refs = refs[:cols], refs[cols : 2 * cols], refs[2 * cols :]
    order = from_order(cols)
    users = [ref[...] for ref in users_refs]
    at = 0
    for out_ref in reversed(out_refs):
        for r in range(out_ref.shape[0]):
            ipd = out_ref.shape[2]
            lanes = slice(at * ipd, (at + 1) * ipd)
            total = None
            for k in range(cols):
                part = jnp.dot(
                    users[k], adj_refs[order[k]][:, lanes], preferred_element_type=F32
                )
                total = part if total is None else total + part
            out_ref[r] = total.astype(out_ref.dtype)
            at += 1


def item_sums(adjacency, users_t, sides, chips):
    cols = len(adjacency)
    upd, n = adjacency[0].shape
    d = users_t[0].shape[0]
    block = (chips, d, n // (sides * chips))
    outs = [jax.ShapeDtypeStruct(block, BF16)] * (sides - 1)
    return pl.pallas_call(
        functools.partial(item_sum_kernel, cols),
        out_shape=[*outs, jax.ShapeDtypeStruct(block, F32)],
        in_specs=[vmem_spec()] * (2 * cols),
        out_specs=[vmem_spec()] * sides,
        compiler_params=params(),
        cost_estimate=pl.CostEstimate(
            flops=2 * cols * upd * n * d, bytes_accessed=2 * cols * upd * n, transcendentals=0
        ),
        name="item_sums",
    )(*adjacency, *users_t)


def item_add_kernel(chips, *refs):
    parts, outs = refs[:-chips], refs[-chips:]
    for k, out_ref in enumerate(outs):
        total = parts[0][k]
        for part in parts[1:]:
            total = total + part[k].astype(F32)
        out_ref[...] = total.astype(BF16)


def item_add(parts):
    chips, d, ipd = parts[0].shape
    return pl.pallas_call(
        functools.partial(item_add_kernel, chips),
        out_shape=(jax.ShapeDtypeStruct((d, ipd), BF16),) * chips,
        in_specs=[vmem_spec()] * len(parts),
        out_specs=(vmem_spec(),) * chips,
        compiler_params=params(),
        name="item_add",
    )(*parts)


def updated(side, own, weight_sum, weight_product):
    own = own.astype(F32)
    linear = jnp.dot((side + own).astype(BF16), weight_sum, preferred_element_type=F32)
    linear = linear + jnp.dot(
        (side * own).astype(BF16), weight_product, preferred_element_type=F32
    )
    return jnp.where(linear > 0, linear, 0.2 * linear)


def user_update_kernel(layer, own_ref, sum_ref, product_ref, *refs):
    parts, outs = refs[:-2], refs[-2:]
    side = parts[0][...].astype(F32)
    for part in parts[1:]:
        side = side + part[...].astype(F32)
    new = updated(side, own_ref[...], sum_ref[layer], product_ref[layer])
    outs[0][...] = new.astype(BF16)
    outs[1][...] = new.T.astype(BF16)


def user_update(layer, parts, own, weight_sum, weight_product):
    upd, d = own.shape
    return pl.pallas_call(
        functools.partial(user_update_kernel, layer),
        out_shape=(jax.ShapeDtypeStruct((upd, d), BF16), jax.ShapeDtypeStruct((d, upd), BF16)),
        in_specs=[vmem_spec()] * (3 + len(parts)),
        out_specs=(vmem_spec(),) * 2,
        compiler_params=params(),
        name="user_update",
    )(own, weight_sum, weight_product, *parts)


def item_update_kernel(layer, own_ref, sum_ref, product_ref, *refs):
    parts, new_ref = refs[:-1], refs[-1]
    side = parts[0][...].astype(F32)
    for part in parts[1:]:
        side = side + part[...].astype(F32)
    new = updated(side.T, own_ref[...], sum_ref[layer], product_ref[layer])
    new_ref[...] = new.astype(BF16)


def item_update(layer, parts, own, weight_sum, weight_product):
    return pl.pallas_call(
        functools.partial(item_update_kernel, layer),
        out_shape=jax.ShapeDtypeStruct(own.shape, BF16),
        in_specs=[vmem_spec()] * (3 + len(parts)),
        out_specs=vmem_spec(),
        compiler_params=params(),
        name="item_update",
    )(own, weight_sum, weight_product, *parts)


def exchange(blocks, axis, n, inner=1):
    received = [blocks[0]]
    for k in range(1, n):
        pairs = [
            (i * inner + j, peer_to(i, k, n) * inner + j) for i in range(n) for j in range(inner)
        ]
        received.append(lax.ppermute(blocks[k], axis, pairs))
    return received


def swap(block, axis, n):
    return lax.ppermute(block, axis, [(i, i ^ 1) for i in range(n)])


def ordered(received):
    order = from_order(len(received))
    return [received[order.index(k)] for k in range(len(received))]


def per_device(
    raw_rows,
    raw_wide,
    raw_dest,
    raw_slot,
    proj_narrow,
    proj_wide,
    adj_values,
    tile_mask,
    tile_scale,
    weight_sum,
    weight_product,
):
    rows = lax.axis_size("row")
    cols = lax.axis_size("col")
    devices = rows * cols
    count = raw_rows.shape[0]
    capacity = 3 * count // devices
    upd = adj_values.shape[0] // cols
    ipd = adj_values.shape[1] // rows
    layers = weight_sum.shape[0]
    sides = 2 if rows % 2 == 0 else 1
    chips = rows // sides
    me = lax.axis_index(("row", "col")).astype(jnp.int32).reshape(1)
    send = dispatch(
        me,
        raw_rows.T,
        raw_dest.reshape(1, count),
        raw_slot.reshape(1, count),
        raw_wide.reshape(1, count),
        devices,
        capacity,
    )
    recv = lax.all_to_all(send, ("row", "col"), split_axis=0, concat_axis=0, tiled=True)
    adjacency = dequantize(
        me, adj_values, tile_mask, tile_scale, (sides, chips, cols)
    )
    users, users_t, items, *moved = segment(
        me, recv, proj_narrow, proj_wide, adjacency[KEPT:], upd, ipd, capacity
    )
    adjacency = [*adjacency[:KEPT], *moved]
    for n in range(layers):
        all_users_t = exchange([users_t] * cols, "col", cols)
        all_items = ordered(exchange([items] * chips, "row", chips, sides))
        if sides > 1:
            merged = merge(all_items)
            all_items = [*all_items, swap(merged, "row", rows)]
        *away, kept = item_sums(adjacency, all_users_t, sides, chips)
        came = [swap(part, "row", rows) for part in away]
        if n > 0 and sides > 1:
            begun = user_sums(adjacency, all_items[:chips], dtype=F32)
            user_parts = user_sums(
                adjacency, all_items[chips:], chips * ipd, begun
            )
        else:
            user_parts = user_sums(adjacency, all_items)
        item_parts = item_add([kept, *came])
        item_parts = exchange(item_parts, "row", chips, sides)
        user_parts = exchange(user_parts, "col", cols)
        items = item_update(n, item_parts, items, weight_sum, weight_product)
        users, users_t = user_update(n, user_parts, users, weight_sum, weight_product)
    return (users, items[None])


def solution(mesh):
    placed = (
        P(("row", "col"), None),
        P(("row", "col")),
        P(("row", "col")),
        P(("row", "col")),
        P(),
        P(),
        P("row", "col"),
        P("row", "col"),
        P("row", "col"),
        P(),
        P(),
    )
    return jax.shard_map(
        per_device,
        mesh=mesh,
        in_specs=placed,
        out_specs=(P(("row", "col"), None), P("col", "row", None)),
        check_vma=False,
    )
```
